32 devices in a mesh: groups: 2 (over x), particle: 8 (over z, y), classes: 2 (over core).
Axes of the slice: x: 2, y: 2, z: 4, core: 2. Of those that a mesh axis runs over, the one named last changes fastest.
Arguments:
- boxes: bfloat16 [2048, 12288], P(('groups', 'particle', 'classes')), parts along dimension 0
- counts: int32 [32], P(('groups', 'particle', 'classes')), parts along dimension 0, may hold values from 1 to 64, as said below
- destinations: int32 [2048], P(('groups', 'particle', 'classes')), parts along dimension 0, may hold values from 0 to 7, as said below
- prior_rot: int32 [2048], P(('groups', 'particle', 'classes')), parts along dimension 0, may hold values from 0 to 23
- references: bfloat16 [128, 12288], P(('groups', 'classes')), parts along dimension 0
- cycle_weights: float32 [16, 64], P(('groups', 'particle')), parts along dimension 0, may hold values from 0.01 to 0.05
- prior_strength: float32 [128], P(('groups', 'classes')), parts along dimension 0, may hold values from 0.5 to 3
Outputs:
- new_references: float32 [128, 64, 192], P(('groups', 'classes'), 'particle'), parts along dimension 0
- log_evidence: float32 [2048], P(('groups', 'particle', 'classes')), parts along dimension 0
The draws below stay inside these ranges and needn't reach their ends.
There are 2 independent parts, one for each index of `groups`. The reference program is written for one: setup_inputs(seed, part) draws one part's arguments, and reference() takes and returns one part's arrays. A program takes and returns all parts, laid end to end along the dimension named above; each array names one. Nothing has to cross between parts.
Inputs may be any that keep to these rules, and one draw needn't show every extreme that they name: On each index of classes, the counts of the 8 owners with that index sum to 128, and one of them is exactly 64. `destinations`: only an owner's first counts slots are picked; its other slots hold arbitrary indices. Each device receives exactly 16 picked boxes, all from owners with its own index of classes, and at most 8 from any one owner; some owner sends exactly 8 to one device.
All inputs are finite; a program needn't handle non-finite values.
Results may differ from the reference program's by a relative error of at most 0.004.
Values may be sent and summed in bfloat16 or wider, within the bound.
A program may use at most 192 MiB of HBM per device.

```python
import math
import jax
import jax.numpy as jnp
from jax import lax

CYCLES = 64
ANGLES = 192
CLASSES = 64
ROTATIONS = 24
REC = 16
OWN = 64
BOXES = 1024
LIVE = 256
N_PARTICLE = 8
N_CLASSES = 2


def pick_plan(key):
    plan_key = jax.random.fold_in(key, 301)
    key_full, key_share, key_rank, key_perm, key_junk = jax.random.split(plan_key, 5)
    lane_ids = jnp.arange(N_PARTICLE, dtype=jnp.int32)
    full_owner = jax.random.randint(key_full, (N_CLASSES,), 0, N_PARTICLE)
    is_full = lane_ids[None, :] == full_owner[:, None]
    shares = jnp.where(is_full, 0, jax.random.randint(key_share, (N_CLASSES, N_PARTICLE), 1, 3))
    spare = (N_PARTICLE - 4) * REC - (N_PARTICLE - 1)
    portion = spare * shares // jnp.sum(shares, axis=1, keepdims=True)
    leftover = spare - jnp.sum(portion, axis=1, keepdims=True)
    rank_keys = jax.random.randint(key_rank, (N_CLASSES, N_PARTICLE), 0, 1 << 20) * N_PARTICLE + lane_ids[None, :]
    rank_keys = jnp.where(is_full, jnp.int32(1 << 30), rank_keys)
    ranks = jnp.argsort(jnp.argsort(rank_keys, axis=1), axis=1)
    owner_counts = jnp.where(is_full, 4 * REC, 1 + portion + (ranks < leftover).astype(jnp.int32))
    positions = (lane_ids[None, :] - full_owner[:, None]) % N_PARTICLE
    earlier = positions[:, None, :] < positions[:, :, None]
    starts = jnp.sum(jnp.where(earlier, owner_counts[:, None, :], 0), axis=2)
    perms = jax.vmap(lambda sub_key: jax.random.permutation(sub_key, N_PARTICLE))(jax.random.split(key_perm, N_CLASSES))
    slot_ids = jnp.arange(OWN, dtype=jnp.int32)
    blocks = (starts[:, :, None] + slot_ids[None, None, :]) // 2 % N_PARTICLE
    routed = jnp.take_along_axis(jnp.broadcast_to(perms[:, None, :], (N_CLASSES, N_PARTICLE, N_PARTICLE)), blocks, axis=2)
    junk = jax.random.randint(key_junk, (N_CLASSES, N_PARTICLE, OWN), 0, N_PARTICLE)
    chosen = jnp.where(slot_ids[None, None, :] < owner_counts[:, :, None], routed, junk)
    dest_out = jnp.transpose(chosen, (1, 0, 2)).reshape(BOXES).astype(jnp.int32)
    count_out = jnp.transpose(owner_counts).reshape(N_PARTICLE * N_CLASSES).astype(jnp.int32)
    return (dest_out, count_out)


def base_refs(key):
    ref_key = jax.random.fold_in(key, 17)
    ref_values = jax.random.normal(ref_key, (CLASSES, CYCLES * ANGLES), jnp.float32)
    return ref_values


def draw_counts(key, part):
    return pick_plan(key)[1]


def draw_destinations(key, part):
    return pick_plan(key)[0]


def draw_references(key, part):
    return base_refs(key).astype(jnp.bfloat16)


def draw_boxes(key, part):
    box_key = jax.random.fold_in(key, 23)
    base_noise = jax.random.normal(box_key, (BOXES, CYCLES * ANGLES), jnp.float32)
    return base_noise.astype(jnp.bfloat16)


def set_ends(values, stream_key, low, high):
    dims = values.shape
    spot = [jax.random.randint(jax.random.fold_in(stream_key, axis), (), 0, dims[axis]) for axis in range(len(dims))]
    values = values.at[tuple(spot)].set(low)
    longest = dims.index(max(dims))
    spot[longest] = (spot[longest] + 1) % dims[longest]
    return values.at[tuple(spot)].set(high)


def steps_of(key, extent, shards, least, largest):
    level = 1.0
    for dim, shards_of in shards:
        steps = jax.random.uniform(jax.random.fold_in(jax.random.fold_in(key, 6), dim), (shards_of,), jnp.float32, least / len(shards), largest / len(shards))
        level = level * jnp.repeat(jnp.exp(steps), extent[dim] // shards_of).reshape((-1,) + (1,) * (len(extent) - 1 - dim))
    return level


def setup_inputs(seed: int = 0, part: int = 0) -> dict:
    keys = jax.random.split(jax.random.key(seed), 8)
    part_splits = jax.random.split(jax.random.fold_in(keys[7], part), 8)
    return {
        "boxes": draw_boxes(jax.random.fold_in(jax.random.fold_in(keys[7], part), 71), part),
        "counts": draw_counts(jax.random.fold_in(jax.random.fold_in(keys[7], part), 71), part),
        "destinations": draw_destinations(jax.random.fold_in(jax.random.fold_in(keys[7], part), 71), part),
        "prior_rot": set_ends(jax.random.randint(part_splits[3], (BOXES,), 0, ROTATIONS), jax.random.fold_in(part_splits[3], 1), 0, ROTATIONS - 1).astype(jnp.int32),
        "references": draw_references(jax.random.fold_in(jax.random.fold_in(keys[7], part), 71), part),
        "cycle_weights": jnp.clip(jnp.exp(math.log(0.05) - 1.609438 * jax.random.uniform(part_splits[5], (N_PARTICLE, CYCLES), jnp.float32) ** steps_of(part_splits[5], (N_PARTICLE, CYCLES), ((0, 8),), -0.2, 0.2)), 0.01, 0.05),
        "prior_strength": jnp.clip(jnp.exp(math.log(3.0) - 1.7917595 * jax.random.uniform(part_splits[6], (CLASSES,), jnp.float32) ** steps_of(part_splits[6], (CLASSES,), ((0, 2),), -0.2, 0.2)), 0.5, 3.0),
    }


HIGHEST = lax.Precision.HIGHEST
TWO_PI = 2.0 * math.pi


def rotated_stack(ref_cube, turn_shift):
    return jnp.concatenate([jnp.roll(ref_cube, turn_id * turn_shift, axis=2) for turn_id in range(ROTATIONS)], axis=0)


def score_rows(box_rows, row_wts, prior_turn, ref_stack, energy, strength):
    cycle_dots = jnp.einsum("nga,qga->gnq", box_rows.astype(jnp.float32), ref_stack.astype(jnp.float32), precision=HIGHEST)
    weighted = jnp.einsum("gnq,ng->nq", cycle_dots, row_wts, precision=HIGHEST)
    row_count = box_rows.shape[0]
    class_count = energy.shape[0]
    weighted = weighted.reshape(row_count, ROTATIONS, class_count)
    offset = -0.5 * jnp.dot(row_wts, energy.T, precision=HIGHEST)
    turn_ids = jnp.arange(ROTATIONS, dtype=jnp.float32)
    angle_gap = TWO_PI * (turn_ids[None, :] - prior_turn[:, None].astype(jnp.float32)) / ROTATIONS
    return weighted + offset[:, None, :] + jnp.cos(angle_gap)[:, :, None] * strength[None, None, :]


def reference(boxes, counts, destinations, prior_rot, references, cycle_weights, prior_strength):
    turn_shift = ANGLES // ROTATIONS
    slot_ids = jnp.arange(BOXES, dtype=jnp.int32)
    is_live = (slot_ids % OWN) < jnp.repeat(counts, OWN, total_repeat_length=BOXES)
    picked = jnp.nonzero(is_live, size=LIVE)[0].astype(jnp.int32)
    box_rows = boxes[picked].reshape(LIVE, CYCLES, ANGLES)
    row_wts = cycle_weights[destinations[picked]]
    prior_turn = prior_rot[picked].astype(jnp.float32)
    ref_cube = references.reshape(CLASSES, CYCLES, ANGLES)
    ref_stack = rotated_stack(ref_cube, turn_shift)
    ref_wide = ref_cube.astype(jnp.float32)
    energy = jnp.sum(ref_wide * ref_wide, axis=2)
    block_rows = math.gcd(LIVE, 64)

    def one_block(block_id):
        first_row = block_id * block_rows
        return score_rows(lax.dynamic_slice_in_dim(box_rows, first_row, block_rows, 0),
                          lax.dynamic_slice_in_dim(row_wts, first_row, block_rows, 0),
                          lax.dynamic_slice_in_dim(prior_turn, first_row, block_rows, 0),
                          ref_stack, energy, prior_strength)

    scores = lax.map(one_block, jnp.arange(LIVE // block_rows, dtype=jnp.int32)).reshape(LIVE, ROTATIONS, CLASSES)
    row_top = jnp.max(scores, axis=(1, 2))
    exp_terms = jnp.exp(scores - row_top[:, None, None])
    norm_sum = jnp.sum(exp_terms, axis=(1, 2))
    weights = (exp_terms / norm_sum[:, None, None]).astype(jnp.bfloat16)
    evidence_live = (row_top + jnp.log(norm_sum)) / (ANGLES * jnp.sum(row_wts, axis=1))
    evidence = jnp.zeros((BOXES,), jnp.float32).at[picked].set(evidence_live)
    class_sum = jnp.zeros((CLASSES, CYCLES, ANGLES), jnp.float32)
    for turn_id in range(ROTATIONS):
        spread = jnp.einsum("nk,nga->kga", weights[:, turn_id, :].astype(jnp.float32), box_rows.astype(jnp.float32), precision=HIGHEST)
        class_sum = class_sum + jnp.roll(spread, -turn_id * turn_shift, axis=2)
    class_mass = jnp.sum(weights.astype(jnp.float32), axis=(0, 1))
    new_references = (class_sum + ref_wide) / (class_mass + 1.0)[:, None, None]
    return new_references, evidence
```

```python
import functools
import math

import jax
import jax.numpy as jnp
from jax import lax
from jax.experimental import pallas as pl
from jax.experimental.pallas import tpu as pltpu
from jax.sharding import PartitionSpec as P

CYCLES = 64
ANGLES = 192
ROTATIONS = 24
FINE = 4
COARSE = ROTATIONS // FINE
SHIFT = ANGLES // ROTATIONS
STEP_CYCLES = 4
STEP = STEP_CYCLES * ANGLES
STEPS = CYCLES // STEP_CYCLES
TWO_PI = 2.0 * math.pi


def roll_rows(block, shift):
    shift = shift % ANGLES
    if shift == 0:
        return block
    pieces = []
    for c in range(STEP_CYCLES):
        base = c * ANGLES
        pieces.append(block[base + ANGLES - shift : base + ANGLES])
        pieces.append(block[base : base + ANGLES - shift])
    return jnp.concatenate(pieces, axis=0)


def fan_out(rows, sign):
    plain = jnp.concatenate([rows, rows], axis=0).T
    low = lax.broadcasted_iota(jnp.int32, plain.shape, 1) < rows.shape[0]
    tiles = [
        jnp.where(low, roll_rows(plain, sign * SHIFT * f), roll_rows(plain, sign * SHIFT * (f + 1)))
        for f in range(0, FINE, 2)
    ]
    return jnp.concatenate([t.astype(jnp.bfloat16) for t in tiles], axis=1), plain


def score_kernel(boxes_ref, refs_ref, wts_ref, aux_ref, str_ref, post, mass, ev_ref, acc, off):
    step = pl.program_id(0)
    owned = boxes_ref.shape[0]
    half = str_ref.shape[1]

    @pl.when(step == 0)
    def _():
        acc[...] = jnp.zeros_like(acc)
        off[...] = jnp.zeros_like(off)

    @pl.when(step >= 0)
    def _():
        wts = wts_ref[0]
        lane = lax.broadcasted_iota(jnp.int32, (owned, STEP), 1)
        spread = jnp.broadcast_to(wts[:, 0:1], (owned, STEP))
        for c in range(1, STEP_CYCLES):
            spread = jnp.where(lane >= c * ANGLES, wts[:, c : c + 1], spread)
        scaled = boxes_ref[...].astype(jnp.float32) * spread
        high = scaled.astype(jnp.bfloat16)
        rest = (scaled - high.astype(jnp.float32)).astype(jnp.bfloat16)
        lhs = jnp.concatenate([high, rest], axis=0)
        fan, plain = fan_out(refs_ref[...].astype(jnp.float32), 1)
        total = off[...]
        for c in range(STEP_CYCLES):
            piece = plain[c * ANGLES : (c + 1) * ANGLES]
            total = total + wts[:, c : c + 1] * jnp.sum(piece * piece, axis=0, keepdims=True)
        off[...] = total
        for q in range(COARSE):
            acc[q] += jnp.dot(
                lhs, roll_rows(fan, SHIFT * FINE * q), preferred_element_type=jnp.float32
            )

    @pl.when(step == STEPS - 1)
    def _():
        aux = aux_ref[...]
        live = aux[:, ROTATIONS : ROTATIONS + 1]
        wsum = aux[:, ROTATIONS + 1 : ROTATIONS + 2]
        low = lax.broadcasted_iota(jnp.int32, (owned, half), 1) < owned
        base = -0.5 * off[...]
        strength = str_ref[...]
        top = None
        for q in range(COARSE):
            for t in range(FINE // 2):
                r = q * FINE + 2 * t
                cols = slice(t * half, (t + 1) * half)
                turn = jnp.where(low, aux[:, r : r + 1], aux[:, r + 1 : r + 2])
                score = acc[q, :owned, cols] + acc[q, owned:, cols] + base + turn * strength
                acc[q, :owned, cols] = score
                top = score if top is None else jnp.maximum(top, score)
        top = jnp.max(top, axis=1, keepdims=True)
        norm = jnp.zeros((owned, half), jnp.float32)
        for q in range(COARSE):
            for t in range(FINE // 2):
                cols = slice(t * half, (t + 1) * half)
                term = jnp.exp(acc[q, :owned, cols] - top)
                acc[q, :owned, cols] = term
                norm = norm + term
        norm = jnp.sum(norm, axis=1, keepdims=True)
        ev_ref[...] = jnp.where(live > 0.0, (top + jnp.log(norm)) / (ANGLES * wsum), 0.0)
        seen = jnp.zeros((owned, half), jnp.float32)

        def weight(q, t):
            cols = slice(t * half, (t + 1) * half)
            value = jnp.where(live > 0.0, acc[q, :owned, cols] / norm, 0.0)
            return value.astype(jnp.bfloat16).astype(jnp.float32)

        for q in range(0, COARSE, 2):
            for t in range(FINE // 2):
                first, second = weight(q, t), weight(q + 1, t)
                seen = seen + first + second
                even = jnp.where(low, first, pltpu.roll(second, half // 2, 1))
                odd = jnp.where(low, pltpu.roll(first, half // 2, 1), second)
                cols = slice(q // 2 * half, (q // 2 + 1) * half)
                post[2 * t * owned : (2 * t + 1) * owned, cols] = even.astype(jnp.bfloat16)
                post[(2 * t + 1) * owned : (2 * t + 2) * owned, cols] = odd.astype(jnp.bfloat16)
        seen = jnp.sum(seen, axis=0, keepdims=True)
        mass[...] = seen + pltpu.roll(seen, half // 2, 1)


def turned_sums(boxes, post):
    half = 2 * boxes.shape[0]
    fan, _unused = fan_out(boxes.astype(jnp.float32), -1)
    sums = jnp.dot(fan, post, preferred_element_type=jnp.float32)
    both = sums[:, :half]
    for p in range(1, COARSE // 2):
        both = both + roll_rows(sums[:, p * half : (p + 1) * half], -2 * p * SHIFT * FINE)
    whole = both + pltpu.roll(roll_rows(both, -SHIFT * FINE), half // 2, 1)
    return whole.T


def plain_sums_kernel(width, boxes_ref, post_ref, mass_ref, out_ref):
    turned = turned_sums(boxes_ref[...], post_ref[...])
    classes = out_ref.shape[2]
    mass = jnp.broadcast_to(mass_ref[...], (128, 128)).T
    for h in range(2):
        rows = turned[h * classes : (h + 1) * classes]
        tail = mass[h * classes : (h + 1) * classes, : out_ref.shape[3] - width]
        for j in range(STEP // width):
            out_ref[j, h, :, :width] = rows[:, j * width : (j + 1) * width]
            out_ref[j, h, :, width:] = tail


def plain_sums(boxes, post, mass, classes, peers):
    width = CYCLES // peers * ANGLES
    padded = (width + 1 + 127) // 128 * 128
    return pl.pallas_call(
        functools.partial(plain_sums_kernel, width),
        grid=(STEPS,),
        in_specs=[
            pl.BlockSpec((boxes.shape[0], STEP), lambda i: (0, i)),
            pl.BlockSpec(post.shape, lambda i: (0, 0)),
            pl.BlockSpec(mass.shape, lambda i: (0, 0)),
        ],
        out_specs=pl.BlockSpec((STEP // width, 2, classes, padded), lambda i: (i, 0, 0, 0)),
        out_shape=jax.ShapeDtypeStruct((peers, 2, classes, padded), jnp.float32),
    )(boxes, post, mass)


def scores(boxes, refs, wts, aux, strength):
    owned, classes, half = boxes.shape[0], refs.shape[0], strength.shape[1]
    whole = lambda shape: pl.BlockSpec(shape, lambda i: (0, 0))
    post = (FINE * owned, COARSE * classes)
    return pl.pallas_call(
        score_kernel,
        grid=(STEPS,),
        in_specs=[
            pl.BlockSpec((owned, STEP), lambda i: (0, i)),
            pl.BlockSpec((classes, STEP), lambda i: (0, i)),
            pl.BlockSpec((1, owned, STEP_CYCLES), lambda i: (i, 0, 0)),
            whole(aux.shape),
            whole((1, half)),
        ],
        out_specs=[whole(post), whole((1, half)), whole((owned, 1))],
        out_shape=[
            jax.ShapeDtypeStruct(post, jnp.bfloat16),
            jax.ShapeDtypeStruct((1, half), jnp.float32),
            jax.ShapeDtypeStruct((owned, 1), jnp.float32),
        ],
        scratch_shapes=[
            pltpu.VMEM((COARSE, 2 * owned, FINE * classes), jnp.float32),
            pltpu.VMEM((owned, half), jnp.float32),
        ],
        compiler_params=pltpu.CompilerParams(
            dimension_semantics=("arbitrary",), vmem_limit_bytes=40 * 1024 * 1024
        ),
    )(boxes, refs, wts, aux, strength)


MESH = pl.DeviceIdType.MESH
CHUNKS = 4


def greet(devices):
    barrier = pltpu.get_barrier_semaphore()
    for device in devices:
        pl.semaphore_signal(barrier, inc=1, device_id=device, device_id_type=MESH)
    pl.semaphore_wait(barrier, len(devices))


def gather_kernel(peers, refs_ref, row_ref, all_refs, all_rows, local, send, recv):
    mine, core = lax.axis_index("particle"), lax.axis_index("classes")
    partner = {"classes": 1 - core}
    others = [{"particle": lax.rem(mine + d, peers)} for d in range(1, peers)]
    greet([partner] + others)
    copies = [
        pltpu.make_async_remote_copy(
            src_ref=refs_ref, dst_ref=all_refs.at[core], send_sem=send.at[0], recv_sem=recv.at[0],
            device_id=partner, device_id_type=MESH,
        ),
        pltpu.make_async_remote_copy(
            src_ref=row_ref, dst_ref=all_rows.at[peers], send_sem=send.at[1], recv_sem=recv.at[1],
            device_id=partner, device_id_type=MESH,
        ),
    ]
    for d, other in enumerate(others):
        copies.append(
            pltpu.make_async_remote_copy(
                src_ref=row_ref, dst_ref=all_rows.at[mine], send_sem=send.at[2 + d],
                recv_sem=recv.at[2 + d], device_id=other, device_id_type=MESH,
            )
        )
    for copy in copies:
        copy.start()
    own = [
        pltpu.make_async_copy(refs_ref, all_refs.at[core], local.at[0]),
        pltpu.make_async_copy(row_ref, all_rows.at[mine], local.at[1]),
    ]
    for copy in own:
        copy.start()
    for copy in own + copies:
        copy.wait()


def gathered(refs, row, peers):
    return pl.pallas_call(
        functools.partial(gather_kernel, peers),
        in_specs=[pl.BlockSpec(memory_space=pltpu.VMEM)] * 2,
        out_specs=[pl.BlockSpec(memory_space=pltpu.VMEM)] * 2,
        out_shape=[
            jax.ShapeDtypeStruct((2,) + refs.shape, refs.dtype),
            jax.ShapeDtypeStruct((peers + 1,) + row.shape, row.dtype),
        ],
        scratch_shapes=[
            pltpu.SemaphoreType.DMA((2,)),
            pltpu.SemaphoreType.DMA((peers + 1,)),
            pltpu.SemaphoreType.DMA((peers + 1,)),
        ],
        compiler_params=pltpu.CompilerParams(collective_id=0, has_side_effects=True),
    )(refs, row)


def scatter_kernel(depth, parts, out, pair_in, side_out, side_in, line_out, line_in,
                   pair_send, pair_recv, side_send, side_recv, line_send, line_recv):
    mine, core = lax.axis_index("particle"), lax.axis_index("classes")
    level, side = mine // 2, lax.rem(mine, 2)
    partner = {"classes": 1 - core}
    across = {"particle": level * 2 + 1 - side}
    levels = [lax.rem(level + d, depth) for d in range(1, depth)]
    line = [{"particle": other * 2 + side} for other in levels]
    greet([partner, across] + line)
    rows = out.shape[0] // CHUNKS
    pair, cross, lines = [], [], []
    for j in range(CHUNKS):
        copy = pltpu.make_async_remote_copy(
            src_ref=parts.at[:, :, 1 - core, j * rows : (j + 1) * rows], dst_ref=pair_in.at[j],
            send_sem=pair_send.at[j], recv_sem=pair_recv.at[j], device_id=partner,
            device_id_type=MESH,
        )
        copy.start()
        pair.append(copy)
    for j in range(CHUNKS):
        span = slice(j * rows, (j + 1) * rows)
        pair[j].wait_recv()
        side_out[j] = parts[:, 1 - side, core, span] + pair_in[j, :, 1 - side]
        copy = pltpu.make_async_remote_copy(
            src_ref=side_out.at[j], dst_ref=side_in.at[j], send_sem=side_send.at[j],
            recv_sem=side_recv.at[j], device_id=across, device_id_type=MESH,
        )
        copy.start()
        cross.append(copy)
        line_out[j] = parts[:, side, core, span] + pair_in[j, :, side]
    for j in range(CHUNKS):
        cross[j].wait_recv()
        line_out[j] = line_out[j] + side_in[j]
        for d in range(depth - 1):
            copy = pltpu.make_async_remote_copy(
                src_ref=line_out.at[j, levels[d]], dst_ref=line_in.at[j, d],
                send_sem=line_send.at[j, d], recv_sem=line_recv.at[j, d], device_id=line[d],
                device_id_type=MESH,
            )
            copy.start()
            lines.append(copy)
    for j in range(CHUNKS):
        total = line_out[j, level]
        for d in range(depth - 1):
            lines[j * (depth - 1) + d].wait_recv()
            total = total + line_in[j, d]
        out[j * rows : (j + 1) * rows] = total
    for copy in pair + cross + lines:
        copy.wait_send()


def scattered(parts):
    peers, _, classes, width = parts.shape
    depth = peers // 2
    rows = classes // CHUNKS
    sems = pltpu.SemaphoreType.DMA((CHUNKS,))
    line_sems = pltpu.SemaphoreType.DMA((CHUNKS, max(depth - 1, 1)))
    return pl.pallas_call(
        functools.partial(scatter_kernel, depth),
        in_specs=[pl.BlockSpec(memory_space=pltpu.VMEM)],
        out_specs=pl.BlockSpec(memory_space=pltpu.VMEM),
        out_shape=jax.ShapeDtypeStruct((classes, width), jnp.float32),
        scratch_shapes=[
            pltpu.VMEM((CHUNKS, depth, 2, rows, width), jnp.float32),
            pltpu.VMEM((CHUNKS, depth, rows, width), jnp.float32),
            pltpu.VMEM((CHUNKS, depth, rows, width), jnp.float32),
            pltpu.VMEM((CHUNKS, depth, rows, width), jnp.float32),
            pltpu.VMEM((CHUNKS, max(depth - 1, 1), rows, width), jnp.float32),
            sems, sems, sems, sems, line_sems, line_sems,
        ],
        compiler_params=pltpu.CompilerParams(
            collective_id=1, has_side_effects=True, vmem_limit_bytes=48 * 1024 * 1024
        ),
    )(parts.reshape(depth, 2, 2, classes, width))


def sums_kernel(peers, boxes, post, mass, refs, out, pair_out, pair_in, keep, side_out, side_in,
                line_in, mass_in, column, pair_send, pair_recv, side_send, side_recv, line_send,
                line_recv, mass_send, mass_recv):
    mine, core = lax.axis_index("particle"), lax.axis_index("classes")
    depth, width, classes = peers // 2, out.shape[1], out.shape[0]
    level, side = mine // 2, lax.rem(mine, 2)
    place = mine * 2 + core
    partner = {"classes": 1 - core}
    across = {"particle": level * 2 + 1 - side}
    everyone = []
    for e in range(1, 2 * peers):
        there = lax.rem(place + e, 2 * peers)
        everyone.append({"particle": there // 2, "classes": lax.rem(there, 2)})
    greet(everyone)
    started, masses = [], []

    def send(src, dst, sends, recvs, device):
        copy = pltpu.make_async_remote_copy(
            src_ref=src, dst_ref=dst, send_sem=sends, recv_sem=recvs, device_id=device,
            device_id_type=MESH,
        )
        copy.start()
        started.append(copy)
        return copy

    for e, device in enumerate(everyone):
        masses.append(
            send(mass, mass_in.at[e], mass_send.at[e], mass_recv.at[e], device)
        )
    turns = list(range(1, depth)) + [0]
    blocks = [(i, d, True) for i, d in enumerate(turns)] + [(i, d, False) for i, d in enumerate(turns)]
    pair, cross, lines = [], [], []

    def advance(n):
        i, d, away = blocks[n]
        pair[n].wait_recv()
        if away:
            side_out[i] = keep[n] + pair_in[n]
            cross.append(
                send(side_out.at[i], side_in.at[i], side_send.at[i], side_recv.at[i], across)
            )
            return
        cross[i].wait_recv()
        keep[n] = keep[n] + pair_in[n] + side_in[i]
        if d > 0:
            there = {"particle": lax.rem(level + d, depth) * 2 + side}
            lines.append(
                send(keep.at[n], line_in.at[i], line_send.at[i], line_recv.at[i], there)
            )

    for n, (i, d, away) in enumerate(blocks):
        shard = lax.rem(level + d, depth) * 2 + (1 - side if away else side)

        @pl.loop(0, width // STEP)
        def _(part):
            source = pl.multiple_of(shard * width + part * STEP, 128)
            target = pl.multiple_of(part * STEP, 128)
            turned = turned_sums(boxes[:, pl.ds(source, STEP)], post[...])
            low, high = turned[:classes], turned[classes : 2 * classes]
            keep[n, :, pl.ds(target, STEP)] = jnp.where(core == 0, low, high)
            pair_out[n, :, pl.ds(target, STEP)] = jnp.where(core == 0, high, low)

        pair.append(send(pair_out.at[n], pair_in.at[n], pair_send.at[n], pair_recv.at[n], partner))
        if n > 0:
            advance(n - 1)
    advance(len(blocks) - 1)
    weight = mass[...]
    for e, copy in enumerate(masses):
        copy.wait_recv()
        weight = weight + mass_in[e]
    column[...] = jnp.broadcast_to(weight, column.shape).T
    scale = column[pl.ds(pl.multiple_of(core * classes, 8), classes), :]
    total = keep[len(blocks) - 1]
    for i in range(depth - 1):
        lines[i].wait_recv()
        total = total + line_in[i]
    base = refs[:, pl.ds(pl.multiple_of(mine * width, 128), width)].astype(jnp.float32)
    out[...] = (total + base) / (scale[:, 0:1] + 1.0)
    for copy in started:
        copy.wait_send()


def fused_sums(boxes, post, mass, refs, peers):
    classes, width, depth = refs.shape[0], CYCLES // peers * ANGLES, peers // 2
    room = lambda count: pltpu.VMEM((count, classes, width), jnp.float32)
    sems = lambda count: pltpu.SemaphoreType.DMA((count,))
    others = 2 * peers - 1
    return pl.pallas_call(
        functools.partial(sums_kernel, peers),
        in_specs=[pl.BlockSpec(memory_space=pltpu.VMEM)] * 4,
        out_specs=pl.BlockSpec(memory_space=pltpu.VMEM),
        out_shape=jax.ShapeDtypeStruct((classes, width), jnp.float32),
        scratch_shapes=[
            room(peers), room(peers), room(peers), room(depth), room(depth), room(depth - 1),
            pltpu.VMEM((others,) + mass.shape, jnp.float32),
            pltpu.VMEM((mass.shape[1], mass.shape[1]), jnp.float32),
            sems(peers), sems(peers), sems(depth), sems(depth), sems(depth - 1), sems(depth - 1),
            sems(others), sems(others),
        ],
        compiler_params=pltpu.CompilerParams(
            collective_id=2, has_side_effects=True, vmem_limit_bytes=48 * 1024 * 1024
        ),
    )(boxes, post, mass, refs)


PARTS = 4
QUARTERS = 4
TILES = 6
APART = ANGLES // QUARTERS
SLOTS = 128
LEVELS = 32767.0


def turned(block, shift):
    shift = shift % ANGLES
    if shift == 0:
        return block
    return jnp.concatenate([block[ANGLES - shift :], block[: ANGLES - shift]], axis=0)


def flip(block):
    return pltpu.roll(block, 64, 1)


def low_lanes(rows, width=64, period=128):
    lane = lax.broadcasted_iota(jnp.int32, (rows, 128), 1)
    return lax.rem(lane, period) < width


def encode(block, codes, scales, h):
    largest = jnp.maximum(jnp.max(jnp.abs(block), axis=0, keepdims=True), 1e-30)
    scaled = jnp.round(block * (LEVELS / largest))
    codes[h] = scaled.astype(jnp.int32).astype(jnp.int16)
    scales[h : h + 1, :] = largest * (1.0 / LEVELS)


def decode(codes, scales, h):
    return codes[h].astype(jnp.int32).astype(jnp.float32) * scales[h : h + 1, :]


def refs_fan(refs, fans, energies, p):
    cols = slice(p * STEP, (p + 1) * STEP)
    rows = refs[:, cols].astype(jnp.float32)
    plain = jnp.concatenate([rows, rows], axis=0).T
    low = low_lanes(ANGLES)
    for c in range(PARTS):
        base = p * STEP + c * ANGLES
        piece = plain[c * ANGLES : (c + 1) * ANGLES]
        energies[p * PARTS + c : p * PARTS + c + 1, :] = jnp.sum(piece * piece, axis=0, keepdims=True)
        both = jnp.where(low, piece, turned(piece, APART))
        fans[0, base : base + ANGLES, :] = both.astype(jnp.bfloat16)
        fans[1, base : base + ANGLES, :] = turned(both, SHIFT).astype(jnp.bfloat16)


def boxes_fan(boxes, fans, p):
    cols = slice(p * STEP, (p + 1) * STEP)
    plain = boxes[:, cols].astype(jnp.float32).T
    fans[0, cols, :] = plain.astype(jnp.bfloat16)
    for c in range(PARTS):
        base = p * STEP + c * ANGLES
        piece = plain[c * ANGLES : (c + 1) * ANGLES]
        fans[1, base : base + ANGLES, :] = turned(piece, -SHIFT).astype(jnp.bfloat16)


def scaled_boxes(boxes, weights, energies, lhs, p, base):
    low = low_lanes(SLOTS)
    wide = [
        jnp.broadcast_to(weights[:, 2 * PARTS * p + c : 2 * PARTS * p + c + 1], (SLOTS, 128))
        for c in range(PARTS)
    ]
    for c in range(PARTS):
        base = base + wide[c] * energies[p * PARTS + c : p * PARTS + c + 1, :]
    spread = [
        wide[0], jnp.where(low, wide[0], wide[1]), wide[1],
        wide[2], jnp.where(low, wide[2], wide[3]), wide[3],
    ]
    for t, factor in enumerate(spread):
        cols = slice(p * STEP + t * 128, p * STEP + (t + 1) * 128)
        scaled = boxes[:, cols].astype(jnp.float32) * factor
        high = scaled.astype(jnp.bfloat16)
        lhs[:SLOTS, cols] = high
        lhs[SLOTS:, cols] = (scaled - high.astype(jnp.float32)).astype(jnp.bfloat16)
    return base


def score_tile(lhs, fans, f, peers):
    total = None
    for p in range(peers):
        pieces = []
        for c in range(PARTS):
            base = p * STEP + c * ANGLES
            piece = fans[f % 2, base : base + ANGLES, :]
            shift = SHIFT * (f - f % 2)
            pieces.append(
                jnp.concatenate([turned(piece, shift), turned(piece, shift + 2 * APART)], axis=1)
            )
        part = jnp.dot(
            lhs[:, p * STEP : (p + 1) * STEP], jnp.concatenate(pieces, axis=0),
            preferred_element_type=jnp.float32,
        )
        total = part if total is None else total + part
    return total[:SLOTS] + total[SLOTS:]


def class_sums(fans, post, shard):
    rows = []
    for c in range(PARTS):
        base = pl.multiple_of(shard * STEP + c * ANGLES, 64)
        even = fans[0, pl.ds(base, ANGLES), :]
        odd = fans[1, pl.ds(base, ANGLES), :]
        rows.append(
            jnp.concatenate(
                [turned(x, -2 * SHIFT * s) for s in range(TILES // 2) for x in (even, odd)], axis=1
            )
        )
    sums = jnp.dot(jnp.concatenate(rows, axis=0), post[...], preferred_element_type=jnp.float32)
    low, first = low_lanes(ANGLES), low_lanes(ANGLES, 32, 64)
    both = []
    for c in range(PARTS):
        piece = sums[c * ANGLES : (c + 1) * ANGLES]
        b = piece[:, :128] + turned(piece[:, 128:], -2 * APART)
        both.append((b, turned(b, -APART)))

    def pair(i, j):
        return jnp.where(low, both[i][0], both[j][1]) + flip(jnp.where(low, both[j][0], both[i][1]))

    a, b = pair(0, 2), pair(1, 3)
    return jnp.where(first, a, pltpu.roll(b, 32, 1)), jnp.where(first, pltpu.roll(a, 96, 1), b)


def whole_kernel(
    peers, boxes, counts, places, turns, refs, weights, strength, out, evidence,
    xs, rs, own, cards, duo, ref_fans, box_fans, energies, base_refs, lhs, mine_s, theirs_s, terms,
    post, masses, y_out, y_out_s, y_in, y_in_s, keep, z_out, z_out_s, z_in, z_in_s, pair_out, pair_in,
    box_local, ref_local, own_local, box_send, box_recv, ref_send, ref_recv, card_send, card_recv,
    duo_send, duo_recv, score_send, score_recv, mass_send, mass_recv, y_send, y_recv, ys_send, ys_recv,
    z_send, z_recv, zs_send, zs_recv, pair_send, pair_recv,
):
    mine, core = lax.axis_index("particle"), lax.axis_index("classes")
    depth, owned, classes = peers // 2, boxes.shape[0], refs.shape[0]
    level, side = mine // 2, lax.rem(mine, 2)
    partner = {"classes": 1 - core}
    across = {"particle": level * 2 + 1 - side}
    others = [{"particle": lax.rem(mine + d, peers)} for d in range(1, peers)]
    order = [
        lax.rem(level + 2, depth), depth - 1 - level, level + 1 - 2 * lax.rem(level, 2),
    ]
    diagonal = [{"particle": there * 2 + side, "classes": 1 - core} for there in order]
    straight = [{"particle": there * 2 + side} for there in order]
    barrier = pltpu.get_barrier_semaphore()
    friends = [partner] + others + diagonal
    for device in friends:
        pl.semaphore_signal(barrier, inc=1, device_id=device, device_id_type=MESH)
    box_rows = pl.ds(pl.multiple_of(core * owned, owned), owned)
    ref_rows = pl.ds(pl.multiple_of(core * classes, classes), classes)
    local = []
    for p in range(peers):
        source = pl.ds(pl.multiple_of((2 * p + core) * STEP, 128), STEP)
        target = pl.ds(p * STEP, STEP)
        local.append(
            pltpu.make_async_copy(refs.at[:, source], rs.at[ref_rows, target], ref_local.at[p])
        )
        local.append(
            pltpu.make_async_copy(boxes.at[:, source], xs.at[box_rows, target], box_local.at[p])
        )
    width = 2 * STEP
    own_copy = pltpu.make_async_copy(
        refs.at[:, pl.ds(pl.multiple_of(mine * width, 128), width)], own, own_local.at[0]
    )
    own_copy.start()
    for copy in local:
        copy.start()
    card = jnp.zeros((8, 128), jnp.float32)
    cards[mine] = card
    slot = lax.broadcasted_iota(jnp.int32, (1, owned), 1)
    cards[mine, 0:1, :CYCLES] = weights[...]
    cards[mine, 1:2, :owned] = places[...].astype(jnp.float32)
    cards[mine, 2:3, :owned] = turns[...].astype(jnp.float32)
    cards[mine, 3:4, :owned] = jnp.where(
        slot < jnp.broadcast_to(counts[...], (1, owned)), 1.0, 0.0
    )
    cards[mine, 4:5, :classes] = strength[...]
    duo[core] = cards[mine]

    started = []

    def send(src, dst, sends, recvs, device):
        copy = pltpu.make_async_remote_copy(
            src_ref=src, dst_ref=dst, send_sem=sends, recv_sem=recvs, device_id=device,
            device_id_type=MESH,
        )
        copy.start()
        started.append(copy)
        return copy

    pl.semaphore_wait(barrier, len(friends))
    card_copies = [
        send(cards.at[mine], cards.at[mine], card_send.at[d], card_recv.at[d], device)
        for d, device in enumerate(others)
    ]
    duo_copy = send(duo.at[core], duo.at[core], duo_send.at[0], duo_recv.at[0], partner)
    ref_copies, box_copies = [], []
    for p in range(peers):
        source = pl.ds(pl.multiple_of((2 * p + 1 - core) * STEP, 128), STEP)
        target = pl.ds(p * STEP, STEP)
        ref_copies.append(
            send(refs.at[:, source], rs.at[ref_rows, target], ref_send.at[p], ref_recv.at[p], partner)
        )
    for p in range(peers):
        source = pl.ds(pl.multiple_of((2 * p + 1 - core) * STEP, 128), STEP)
        target = pl.ds(p * STEP, STEP)
        box_copies.append(
            send(boxes.at[:, source], xs.at[box_rows, target], box_send.at[p], box_recv.at[p], partner)
        )
    own_copy.wait()
    for h in range(2):
        for c in range(PARTS):
            base = (h * PARTS + c) * ANGLES
            base_refs[h, c * classes : (c + 1) * classes, :] = own[:, base : base + ANGLES].astype(
                jnp.float32
            )
    for copy in local:
        copy.wait()
    for p in range(peers):
        ref_copies[p].wait_recv()
        refs_fan(rs, ref_fans, energies, p)

    duo_copy.wait_recv()
    facts = duo[0] + flip(duo[1])
    facts = jnp.concatenate([facts] * (SLOTS // 8), axis=0).T
    place, turn, live = facts[:, 1:2], facts[:, 2:3], facts[:, 3:4]
    force = duo[0, 4:5, :] + pltpu.roll(duo[1, 4:5, :], classes, 1)
    force = force + flip(force)
    lane = lax.broadcasted_iota(jnp.int32, (SLOTS, 128), 1).astype(jnp.float32)
    swing = jnp.cos(TWO_PI * (lane - turn) / ROTATIONS)
    for copy in card_copies:
        copy.wait_recv()
    spread = jnp.zeros((SLOTS, 128), jnp.float32)
    for g in range(peers):
        spread = jnp.where(place == float(g), cards[g, 0:1, :], spread)
    wsum = jnp.sum(spread, axis=1, keepdims=True)
    spread = jnp.where(core == 0, spread, pltpu.roll(spread, 128 - PARTS, 1))
    base = jnp.zeros((SLOTS, 128), jnp.float32)
    for p in range(peers):
        box_copies[p].wait_recv()
        base = scaled_boxes(xs, spread, energies, lhs, p, base)
    base = -0.5 * base

    low = low_lanes(SLOTS)
    score_copies, tops, norms = [], [], []

    def finish(f):
        score_copies[f].wait_recv()
        values = []
        for t in range(2):
            cols = slice(t * 128, (t + 1) * 128)
            r = f + 2 * t * TILES
            prior = jnp.where(low, swing[:, r : r + 1], swing[:, r + TILES : r + TILES + 1]) * force
            values.append(mine_s[f, :, cols] + theirs_s[f, :, cols] + prior)
        top = jnp.max(jnp.maximum(values[0], values[1]), axis=1, keepdims=True)
        values = [jnp.exp(v - top) for v in values]
        for t in range(2):
            terms[f, :, t * 128 : (t + 1) * 128] = values[t]
        tops.append(top)
        norms.append(jnp.sum(values[0] + values[1], axis=1, keepdims=True))

    for f in range(TILES):
        tile = score_tile(lhs, ref_fans, f, peers)
        mine_s[f] = tile + jnp.concatenate([base, base], axis=1)
        score_copies.append(
            send(mine_s.at[f], theirs_s.at[f], score_send.at[f], score_recv.at[f], partner)
        )
        if f > 0:
            finish(f - 1)
    for p in range(peers):
        boxes_fan(xs, box_fans, p)
    finish(TILES - 1)
    top = functools.reduce(jnp.maximum, tops)
    factors = [jnp.exp(t - top) for t in tops]
    norm = sum(n * s for n, s in zip(norms, factors))
    mass = jnp.zeros((8, 256), jnp.float32)
    for f in range(TILES):
        factor = jnp.where(live > 0.0, factors[f] / norm, 0.0)
        value = (terms[f] * factor).astype(jnp.bfloat16)
        post[f * SLOTS : (f + 1) * SLOTS, :] = value
        value = value.astype(jnp.float32)
        for i in range(SLOTS // 8):
            mass = mass + value[i * 8 : (i + 1) * 8]
    mass = mass[:, :128] + mass[:, 128:]
    mass = mass + flip(mass)
    masses[mine] = jnp.broadcast_to(jnp.sum(mass, axis=0, keepdims=True), (8, 128))
    mass_copies = [
        send(masses.at[mine], masses.at[mine], mass_send.at[d], mass_recv.at[d], device)
        for d, device in enumerate(others)
    ]
    proof = jnp.where(live > 0.0, (top + jnp.log(norm)) / (ANGLES * wsum), 0.0)
    proof = jnp.broadcast_to(proof, (SLOTS, 128)).T[0:1]
    evidence[...] = jnp.where(core == 0, proof, flip(proof))[:, :owned]

    y_copies, z_copies = [], []
    levels = order + [level]

    def advance(i):
        for copy in y_copies[i]:
            copy.wait_recv()
        for h in range(2):
            total = keep[i, h] + decode(y_in.at[i], y_in_s.at[i], h)
            if i < depth - 1:
                encode(total, z_out.at[i], z_out_s.at[i], h)
            else:
                keep[i, h] = total
        if i == depth - 1:
            pair_out[...] = jnp.where(core == 0, keep[i, 1], keep[i, 0])
            return send(pair_out, pair_in, pair_send.at[0], pair_recv.at[0], partner)
        for n, device in enumerate([straight[i], diagonal[i]]):
            half = core if n == 0 else 1 - core
            z_copies.append(
                send(z_out.at[i, half], z_in.at[i, core], z_send.at[i, n], z_recv.at[i, n], device)
            )
            z_copies.append(
                send(z_out_s.at[i], z_in_s.at[i, core], zs_send.at[i, n], zs_recv.at[i, n], device)
            )
        return None

    for i, there in enumerate(levels):
        for h, value in enumerate(class_sums(box_fans, post, there * 2 + 1 - side)):
            encode(value, y_out.at[i], y_out_s.at[i], h)
        y_copies.append(
            [
                send(y_out.at[i], y_in.at[i], y_send.at[i], y_recv.at[i], across),
                send(y_out_s.at[i], y_in_s.at[i], ys_send.at[i], ys_recv.at[i], across),
            ]
        )
        for h, value in enumerate(class_sums(box_fans, post, there * 2 + side)):
            keep[i, h] = value
        if i > 0:
            advance(i - 1)
    pair_copy = advance(depth - 1)

    for copy in mass_copies:
        copy.wait_recv()
    weight = masses[0]
    for g in range(1, peers):
        weight = weight + masses[g]
    first = low_lanes(8, 32, 64)
    weight = jnp.where(
        core == 0,
        jnp.where(first, weight, pltpu.roll(weight, 32, 1)),
        jnp.where(first, pltpu.roll(weight, 96, 1), weight),
    )
    scale = jnp.concatenate([weight] * 16, axis=0).T[:, 0:1] + 1.0
    for copy in z_copies:
        copy.wait_recv()
    pair_copy.wait_recv()
    held = jnp.where(core == 0, keep[depth - 1, 0], keep[depth - 1, 1])
    for h in range(2):
        total = jnp.where(core == h, held, pair_in[...])
        for i in range(depth - 1):
            factor = jnp.where(core == 0, z_in_s[i, h, 0:1, :], z_in_s[i, h, 1:2, :])
            total = total + z_in[i, h].astype(jnp.int32).astype(jnp.float32) * factor
        result = (total.T + base_refs[h]) / scale
        for c in range(PARTS):
            out[:, h * PARTS + c, :] = result[c * classes : (c + 1) * classes]
    for copy in started:
        copy.wait_send()


def whole(boxes, counts, places, turns, refs, weights, strength, peers):
    classes, depth = refs.shape[0], peers // 2
    half = CYCLES * ANGLES // 2
    f32, bf16, i16 = jnp.float32, jnp.bfloat16, jnp.int16
    room = lambda dtype, *shape: pltpu.VMEM(shape, dtype)
    sems = lambda *shape: pltpu.SemaphoreType.DMA(shape)
    vmem = pl.BlockSpec(memory_space=pltpu.VMEM)
    hbm = pl.BlockSpec(memory_space=pl.ANY)
    return pl.pallas_call(
        functools.partial(whole_kernel, peers),
        in_specs=[hbm, vmem, vmem, vmem, hbm, vmem, vmem],
        out_specs=[vmem, vmem],
        out_shape=[
            jax.ShapeDtypeStruct((classes, CYCLES // peers, ANGLES), f32),
            jax.ShapeDtypeStruct((1, boxes.shape[0]), f32),
        ],
        scratch_shapes=[
            room(bf16, SLOTS, half), room(bf16, 2 * classes, half), room(bf16, classes, 2 * STEP),
            room(f32, peers, 8, 128), room(f32, 2, 8, 128),
            room(bf16, 2, half, 128), room(bf16, 2, half, 128), room(f32, CYCLES // 2, 128),
            room(f32, 2, 128, ANGLES), room(bf16, 2 * SLOTS, half),
            room(f32, TILES, SLOTS, 256), room(f32, TILES, SLOTS, 256), room(f32, TILES, SLOTS, 256),
            room(bf16, TILES * SLOTS, 256), room(f32, peers, 8, 128),
            room(i16, depth, 2, ANGLES, 128), room(f32, depth, 8, 128),
            room(i16, depth, 2, ANGLES, 128), room(f32, depth, 8, 128),
            room(f32, depth, 2, ANGLES, 128),
            room(i16, depth - 1, 2, ANGLES, 128), room(f32, depth - 1, 8, 128),
            room(i16, depth - 1, 2, ANGLES, 128), room(f32, depth - 1, 2, 8, 128),
            room(f32, ANGLES, 128), room(f32, ANGLES, 128),
            sems(peers), sems(peers), sems(1), sems(peers), sems(peers), sems(peers), sems(peers),
            sems(peers - 1), sems(peers - 1), sems(1), sems(1), sems(TILES), sems(TILES),
            sems(peers - 1), sems(peers - 1), sems(depth), sems(depth), sems(depth), sems(depth),
            sems(depth - 1, 2), sems(depth - 1, 2), sems(depth - 1, 2), sems(depth - 1, 2),
            sems(1), sems(1),
        ],
        compiler_params=pltpu.CompilerParams(
            collective_id=3, has_side_effects=True, vmem_limit_bytes=48 * 1024 * 1024
        ),
    )(boxes, counts, places, turns, refs, weights, strength)


def on_device(boxes, counts, destinations, prior_rot, references, cycle_weights, prior_strength):
    peers = lax.axis_size("particle")
    cycle_index = lax.axis_index("particle")
    cycles_dev = CYCLES // peers
    width = cycles_dev * ANGLES
    if width == 2 * STEP:
        new_references, evidence = whole(
            boxes, counts[None, :], destinations[None, :], prior_rot[None, :], references,
            cycle_weights, prior_strength[None, :], peers,
        )
        return new_references, evidence[0]
    owned = boxes.shape[0]
    classes_dev = references.shape[0]
    lane_index = lax.axis_index("classes")
    row = jnp.concatenate([cycle_weights[0], prior_strength])
    row = jnp.pad(row, (0, 128 - row.shape[0]))[None, :]
    refs, rows = gathered(references, row, peers)
    refs = refs.reshape(2 * classes_dev, -1)
    group_wts = rows[:peers, 0, :CYCLES]
    other = rows[peers, 0, CYCLES : CYCLES + classes_dev]
    strength = jnp.where(
        lane_index == 0,
        jnp.concatenate([prior_strength, other]),
        jnp.concatenate([other, prior_strength]),
    ).reshape(1, -1)
    mine = destinations[:, None] == jnp.arange(peers, dtype=jnp.int32)[None, :]
    wts = jnp.sum(jnp.where(mine[:, :, None], group_wts[None], 0.0), axis=1)
    live = (jnp.arange(owned, dtype=jnp.int32) < counts[0]).astype(jnp.float32)
    turn_ids = jnp.arange(ROTATIONS, dtype=jnp.float32)
    gap = TWO_PI * (turn_ids[None, :] - prior_rot[:, None].astype(jnp.float32)) / ROTATIONS
    aux = jnp.concatenate([jnp.cos(gap), live[:, None], jnp.sum(wts, axis=1)[:, None]], axis=1)
    wts = jnp.transpose(wts.reshape(owned, STEPS, STEP_CYCLES), (1, 0, 2))
    post, mass, evidence = scores(
        boxes, refs, wts, aux, jnp.concatenate([strength, strength], axis=1)
    )
    if width % STEP == 0:
        new_references = fused_sums(boxes, post, mass, references, peers)
    else:
        sums = scattered(plain_sums(boxes, post, mass, classes_dev, peers))
        own_refs = lax.dynamic_slice_in_dim(references, cycle_index * width, width, 1)
        new_references = (sums[:, :width] + own_refs.astype(jnp.float32)) / (
            sums[:, width : width + 1] + 1.0
        )
    return new_references.reshape(classes_dev, cycles_dev, ANGLES), evidence[:, 0]


def solution(mesh):
    in_specs = (
        P(("groups", "particle", "classes"), None),
        P(("groups", "particle", "classes")),
        P(("groups", "particle", "classes")),
        P(("groups", "particle", "classes")),
        P(("groups", "classes"), None),
        P(("groups", "particle"), None),
        P(("groups", "classes")),
    )
    out_specs = (P(("groups", "classes"), "particle", None), P(("groups", "particle", "classes")))
    return jax.shard_map(
        on_device, mesh=mesh, in_specs=in_specs, out_specs=out_specs, check_vma=False
    )
```

```python
import functools
import math

import jax
import jax.numpy as jnp
from jax import lax
from jax.experimental import pallas as pl
from jax.experimental.pallas import tpu as pltpu
from jax.sharding import PartitionSpec as P

CYCLES = 64
ANGLES = 192
ROTATIONS = 24
FINE = 4
COARSE = ROTATIONS // FINE
SHIFT = ANGLES // ROTATIONS
STEP_CYCLES = 4
STEP = STEP_CYCLES * ANGLES
STEPS = CYCLES // STEP_CYCLES
TWO_PI = 2.0 * math.pi


def roll_rows(block, shift):
    shift = shift % ANGLES
    if shift == 0:
        return block
    pieces = []
    for c in range(STEP_CYCLES):
        base = c * ANGLES
        pieces.append(block[base + ANGLES - shift : base + ANGLES])
        pieces.append(block[base : base + ANGLES - shift])
    return jnp.concatenate(pieces, axis=0)


def fan_out(rows, sign):
    plain = jnp.concatenate([rows, rows], axis=0).T
    low = lax.broadcasted_iota(jnp.int32, plain.shape, 1) < rows.shape[0]
    tiles = [
        jnp.where(low, roll_rows(plain, sign * SHIFT * f), roll_rows(plain, sign * SHIFT * (f + 1)))
        for f in range(0, FINE, 2)
    ]
    return jnp.concatenate([t.astype(jnp.bfloat16) for t in tiles], axis=1), plain


def score_kernel(boxes_ref, refs_ref, wts_ref, aux_ref, str_ref, post, mass, ev_ref, acc, off):
    step = pl.program_id(0)
    owned = boxes_ref.shape[0]
    half = str_ref.shape[1]

    @pl.when(step == 0)
    def _():
        acc[...] = jnp.zeros_like(acc)
        off[...] = jnp.zeros_like(off)

    @pl.when(step >= 0)
    def _():
        wts = wts_ref[0]
        lane = lax.broadcasted_iota(jnp.int32, (owned, STEP), 1)
        spread = jnp.broadcast_to(wts[:, 0:1], (owned, STEP))
        for c in range(1, STEP_CYCLES):
            spread = jnp.where(lane >= c * ANGLES, wts[:, c : c + 1], spread)
        scaled = boxes_ref[...].astype(jnp.float32) * spread
        high = scaled.astype(jnp.bfloat16)
        rest = (scaled - high.astype(jnp.float32)).astype(jnp.bfloat16)
        lhs = jnp.concatenate([high, rest], axis=0)
        fan, plain = fan_out(refs_ref[...].astype(jnp.float32), 1)
        total = off[...]
        for c in range(STEP_CYCLES):
            piece = plain[c * ANGLES : (c + 1) * ANGLES]
            total = total + wts[:, c : c + 1] * jnp.sum(piece * piece, axis=0, keepdims=True)
        off[...] = total
        for q in range(COARSE):
            acc[q] += jnp.dot(
                lhs, roll_rows(fan, SHIFT * FINE * q), preferred_element_type=jnp.float32
            )

    @pl.when(step == STEPS - 1)
    def _():
        aux = aux_ref[...]
        live = aux[:, ROTATIONS : ROTATIONS + 1]
        wsum = aux[:, ROTATIONS + 1 : ROTATIONS + 2]
        low = lax.broadcasted_iota(jnp.int32, (owned, half), 1) < owned
        base = -0.5 * off[...]
        strength = str_ref[...]
        top = None
        for q in range(COARSE):
            for t in range(FINE // 2):
                r = q * FINE + 2 * t
                cols = slice(t * half, (t + 1) * half)
                turn = jnp.where(low, aux[:, r : r + 1], aux[:, r + 1 : r + 2])
                score = acc[q, :owned, cols] + acc[q, owned:, cols] + base + turn * strength
                acc[q, :owned, cols] = score
                top = score if top is None else jnp.maximum(top, score)
        top = jnp.max(top, axis=1, keepdims=True)
        norm = jnp.zeros((owned, half), jnp.float32)
        for q in range(COARSE):
            for t in range(FINE // 2):
                cols = slice(t * half, (t + 1) * half)
                term = jnp.exp(acc[q, :owned, cols] - top)
                acc[q, :owned, cols] = term
                norm = norm + term
        norm = jnp.sum(norm, axis=1, keepdims=True)
        ev_ref[...] = jnp.where(live > 0.0, (top + jnp.log(norm)) / (ANGLES * wsum), 0.0)
        seen = jnp.zeros((owned, half), jnp.float32)

        def weight(q, t):
            cols = slice(t * half, (t + 1) * half)
            value = jnp.where(live > 0.0, acc[q, :owned, cols] / norm, 0.0)
            return value.astype(jnp.bfloat16).astype(jnp.float32)

        for q in range(0, COARSE, 2):
            for t in range(FINE // 2):
                first, second = weight(q, t), weight(q + 1, t)
                seen = seen + first + second
                even = jnp.where(low, first, pltpu.roll(second, half // 2, 1))
                odd = jnp.where(low, pltpu.roll(first, half // 2, 1), second)
                cols = slice(q // 2 * half, (q // 2 + 1) * half)
                post[2 * t * owned : (2 * t + 1) * owned, cols] = even.astype(jnp.bfloat16)
                post[(2 * t + 1) * owned : (2 * t + 2) * owned, cols] = odd.astype(jnp.bfloat16)
        seen = jnp.sum(seen, axis=0, keepdims=True)
        mass[...] = seen + pltpu.roll(seen, half // 2, 1)


def turned_sums(boxes, post):
    half = 2 * boxes.shape[0]
    fan, _unused = fan_out(boxes.astype(jnp.float32), -1)
    sums = jnp.dot(fan, post, preferred_element_type=jnp.float32)
    both = sums[:, :half]
    for p in range(1, COARSE // 2):
        both = both + roll_rows(sums[:, p * half : (p + 1) * half], -2 * p * SHIFT * FINE)
    whole = both + pltpu.roll(roll_rows(both, -SHIFT * FINE), half // 2, 1)
    return whole.T


def plain_sums_kernel(width, boxes_ref, post_ref, mass_ref, out_ref):
    turned = turned_sums(boxes_ref[...], post_ref[...])
    classes = out_ref.shape[2]
    mass = jnp.broadcast_to(mass_ref[...], (128, 128)).T
    for h in range(2):
        rows = turned[h * classes : (h + 1) * classes]
        tail = mass[h * classes : (h + 1) * classes, : out_ref.shape[3] - width]
        for j in range(STEP // width):
            out_ref[j, h, :, :width] = rows[:, j * width : (j + 1) * width]
            out_ref[j, h, :, width:] = tail


def plain_sums(boxes, post, mass, classes, peers):
    width = CYCLES // peers * ANGLES
    padded = (width + 1 + 127) // 128 * 128
    return pl.pallas_call(
        functools.partial(plain_sums_kernel, width),
        grid=(STEPS,),
        in_specs=[
            pl.BlockSpec((boxes.shape[0], STEP), lambda i: (0, i)),
            pl.BlockSpec(post.shape, lambda i: (0, 0)),
            pl.BlockSpec(mass.shape, lambda i: (0, 0)),
        ],
        out_specs=pl.BlockSpec((STEP // width, 2, classes, padded), lambda i: (i, 0, 0, 0)),
        out_shape=jax.ShapeDtypeStruct((peers, 2, classes, padded), jnp.float32),
    )(boxes, post, mass)


def scores(boxes, refs, wts, aux, strength):
    owned, classes, half = boxes.shape[0], refs.shape[0], strength.shape[1]
    whole = lambda shape: pl.BlockSpec(shape, lambda i: (0, 0))
    post = (FINE * owned, COARSE * classes)
    return pl.pallas_call(
        score_kernel,
        grid=(STEPS,),
        in_specs=[
            pl.BlockSpec((owned, STEP), lambda i: (0, i)),
            pl.BlockSpec((classes, STEP), lambda i: (0, i)),
            pl.BlockSpec((1, owned, STEP_CYCLES), lambda i: (i, 0, 0)),
            whole(aux.shape),
            whole((1, half)),
        ],
        out_specs=[whole(post), whole((1, half)), whole((owned, 1))],
        out_shape=[
            jax.ShapeDtypeStruct(post, jnp.bfloat16),
            jax.ShapeDtypeStruct((1, half), jnp.float32),
            jax.ShapeDtypeStruct((owned, 1), jnp.float32),
        ],
        scratch_shapes=[
            pltpu.VMEM((COARSE, 2 * owned, FINE * classes), jnp.float32),
            pltpu.VMEM((owned, half), jnp.float32),
        ],
        compiler_params=pltpu.CompilerParams(
            dimension_semantics=("arbitrary",), vmem_limit_bytes=40 * 1024 * 1024
        ),
    )(boxes, refs, wts, aux, strength)


MESH = pl.DeviceIdType.MESH
CHUNKS = 4


def greet(devices):
    barrier = pltpu.get_barrier_semaphore()
    for device in devices:
        pl.semaphore_signal(barrier, inc=1, device_id=device, device_id_type=MESH)
    pl.semaphore_wait(barrier, len(devices))


def gather_kernel(peers, refs_ref, row_ref, all_refs, all_rows, local, send, recv):
    mine, core = lax.axis_index("particle"), lax.axis_index("classes")
    partner = {"classes": 1 - core}
    others = [{"particle": lax.rem(mine + d, peers)} for d in range(1, peers)]
    greet([partner] + others)
    copies = [
        pltpu.make_async_remote_copy(
            src_ref=refs_ref, dst_ref=all_refs.at[core], send_sem=send.at[0], recv_sem=recv.at[0],
            device_id=partner, device_id_type=MESH,
        ),
        pltpu.make_async_remote_copy(
            src_ref=row_ref, dst_ref=all_rows.at[peers], send_sem=send.at[1], recv_sem=recv.at[1],
            device_id=partner, device_id_type=MESH,
        ),
    ]
    for d, other in enumerate(others):
        copies.append(
            pltpu.make_async_remote_copy(
                src_ref=row_ref, dst_ref=all_rows.at[mine], send_sem=send.at[2 + d],
                recv_sem=recv.at[2 + d], device_id=other, device_id_type=MESH,
            )
        )
    for copy in copies:
        copy.start()
    own = [
        pltpu.make_async_copy(refs_ref, all_refs.at[core], local.at[0]),
        pltpu.make_async_copy(row_ref, all_rows.at[mine], local.at[1]),
    ]
    for copy in own:
        copy.start()
    for copy in own + copies:
        copy.wait()


def gathered(refs, row, peers):
    return pl.pallas_call(
        functools.partial(gather_kernel, peers),
        in_specs=[pl.BlockSpec(memory_space=pltpu.VMEM)] * 2,
        out_specs=[pl.BlockSpec(memory_space=pltpu.VMEM)] * 2,
        out_shape=[
            jax.ShapeDtypeStruct((2,) + refs.shape, refs.dtype),
            jax.ShapeDtypeStruct((peers + 1,) + row.shape, row.dtype),
        ],
        scratch_shapes=[
            pltpu.SemaphoreType.DMA((2,)),
            pltpu.SemaphoreType.DMA((peers + 1,)),
            pltpu.SemaphoreType.DMA((peers + 1,)),
        ],
        compiler_params=pltpu.CompilerParams(collective_id=0, has_side_effects=True),
    )(refs, row)


def scatter_kernel(depth, parts, out, pair_in, side_out, side_in, line_out, line_in,
                   pair_send, pair_recv, side_send, side_recv, line_send, line_recv):
    mine, core = lax.axis_index("particle"), lax.axis_index("classes")
    level, side = mine // 2, lax.rem(mine, 2)
    partner = {"classes": 1 - core}
    across = {"particle": level * 2 + 1 - side}
    levels = [lax.rem(level + d, depth) for d in range(1, depth)]
    line = [{"particle": other * 2 + side} for other in levels]
    greet([partner, across] + line)
    rows = out.shape[0] // CHUNKS
    pair, cross, lines = [], [], []
    for j in range(CHUNKS):
        copy = pltpu.make_async_remote_copy(
            src_ref=parts.at[:, :, 1 - core, j * rows : (j + 1) * rows], dst_ref=pair_in.at[j],
            send_sem=pair_send.at[j], recv_sem=pair_recv.at[j], device_id=partner,
            device_id_type=MESH,
        )
        copy.start()
        pair.append(copy)
    for j in range(CHUNKS):
        span = slice(j * rows, (j + 1) * rows)
        pair[j].wait_recv()
        side_out[j] = parts[:, 1 - side, core, span] + pair_in[j, :, 1 - side]
        copy = pltpu.make_async_remote_copy(
            src_ref=side_out.at[j], dst_ref=side_in.at[j], send_sem=side_send.at[j],
            recv_sem=side_recv.at[j], device_id=across, device_id_type=MESH,
        )
        copy.start()
        cross.append(copy)
        line_out[j] = parts[:, side, core, span] + pair_in[j, :, side]
    for j in range(CHUNKS):
        cross[j].wait_recv()
        line_out[j] = line_out[j] + side_in[j]
        for d in range(depth - 1):
            copy = pltpu.make_async_remote_copy(
                src_ref=line_out.at[j, levels[d]], dst_ref=line_in.at[j, d],
                send_sem=line_send.at[j, d], recv_sem=line_recv.at[j, d], device_id=line[d],
                device_id_type=MESH,
            )
            copy.start()
            lines.append(copy)
    for j in range(CHUNKS):
        total = line_out[j, level]
        for d in range(depth - 1):
            lines[j * (depth - 1) + d].wait_recv()
            total = total + line_in[j, d]
        out[j * rows : (j + 1) * rows] = total
    for copy in pair + cross + lines:
        copy.wait_send()


def scattered(parts):
    peers, _, classes, width = parts.shape
    depth = peers // 2
    rows = classes // CHUNKS
    sems = pltpu.SemaphoreType.DMA((CHUNKS,))
    line_sems = pltpu.SemaphoreType.DMA((CHUNKS, max(depth - 1, 1)))
    return pl.pallas_call(
        functools.partial(scatter_kernel, depth),
        in_specs=[pl.BlockSpec(memory_space=pltpu.VMEM)],
        out_specs=pl.BlockSpec(memory_space=pltpu.VMEM),
        out_shape=jax.ShapeDtypeStruct((classes, width), jnp.float32),
        scratch_shapes=[
            pltpu.VMEM((CHUNKS, depth, 2, rows, width), jnp.float32),
            pltpu.VMEM((CHUNKS, depth, rows, width), jnp.float32),
            pltpu.VMEM((CHUNKS, depth, rows, width), jnp.float32),
            pltpu.VMEM((CHUNKS, depth, rows, width), jnp.float32),
            pltpu.VMEM((CHUNKS, max(depth - 1, 1), rows, width), jnp.float32),
            sems, sems, sems, sems, line_sems, line_sems,
        ],
        compiler_params=pltpu.CompilerParams(
            collective_id=1, has_side_effects=True, vmem_limit_bytes=48 * 1024 * 1024
        ),
    )(parts.reshape(depth, 2, 2, classes, width))


def sums_kernel(peers, boxes, post, mass, refs, out, pair_out, pair_in, keep, side_out, side_in,
                line_in, mass_in, column, pair_send, pair_recv, side_send, side_recv, line_send,
                line_recv, mass_send, mass_recv):
    mine, core = lax.axis_index("particle"), lax.axis_index("classes")
    depth, width, classes = peers // 2, out.shape[1], out.shape[0]
    level, side = mine // 2, lax.rem(mine, 2)
    place = mine * 2 + core
    partner = {"classes": 1 - core}
    across = {"particle": level * 2 + 1 - side}
    everyone = []
    for e in range(1, 2 * peers):
        there = lax.rem(place + e, 2 * peers)
        everyone.append({"particle": there // 2, "classes": lax.rem(there, 2)})
    greet(everyone)
    started, masses = [], []

    def send(src, dst, sends, recvs, device):
        copy = pltpu.make_async_remote_copy(
            src_ref=src, dst_ref=dst, send_sem=sends, recv_sem=recvs, device_id=device,
            device_id_type=MESH,
        )
        copy.start()
        started.append(copy)
        return copy

    for e, device in enumerate(everyone):
        masses.append(
            send(mass, mass_in.at[e], mass_send.at[e], mass_recv.at[e], device)
        )
    turns = list(range(1, depth)) + [0]
    blocks = [(i, d, True) for i, d in enumerate(turns)] + [(i, d, False) for i, d in enumerate(turns)]
    pair, cross, lines = [], [], []

    def advance(n):
        i, d, away = blocks[n]
        pair[n].wait_recv()
        if away:
            side_out[i] = keep[n] + pair_in[n]
            cross.append(
                send(side_out.at[i], side_in.at[i], side_send.at[i], side_recv.at[i], across)
            )
            return
        cross[i].wait_recv()
        keep[n] = keep[n] + pair_in[n] + side_in[i]
        if d > 0:
            there = {"particle": lax.rem(level + d, depth) * 2 + side}
            lines.append(
                send(keep.at[n], line_in.at[i], line_send.at[i], line_recv.at[i], there)
            )

    for n, (i, d, away) in enumerate(blocks):
        shard = lax.rem(level + d, depth) * 2 + (1 - side if away else side)

        @pl.loop(0, width // STEP)
        def _(part):
            source = pl.multiple_of(shard * width + part * STEP, 128)
            target = pl.multiple_of(part * STEP, 128)
            turned = turned_sums(boxes[:, pl.ds(source, STEP)], post[...])
            low, high = turned[:classes], turned[classes : 2 * classes]
            keep[n, :, pl.ds(target, STEP)] = jnp.where(core == 0, low, high)
            pair_out[n, :, pl.ds(target, STEP)] = jnp.where(core == 0, high, low)

        pair.append(send(pair_out.at[n], pair_in.at[n], pair_send.at[n], pair_recv.at[n], partner))
        if n > 0:
            advance(n - 1)
    advance(len(blocks) - 1)
    weight = mass[...]
    for e, copy in enumerate(masses):
        copy.wait_recv()
        weight = weight + mass_in[e]
    column[...] = jnp.broadcast_to(weight, column.shape).T
    scale = column[pl.ds(pl.multiple_of(core * classes, 8), classes), :]
    total = keep[len(blocks) - 1]
    for i in range(depth - 1):
        lines[i].wait_recv()
        total = total + line_in[i]
    base = refs[:, pl.ds(pl.multiple_of(mine * width, 128), width)].astype(jnp.float32)
    out[...] = (total + base) / (scale[:, 0:1] + 1.0)
    for copy in started:
        copy.wait_send()


def fused_sums(boxes, post, mass, refs, peers):
    classes, width, depth = refs.shape[0], CYCLES // peers * ANGLES, peers // 2
    room = lambda count: pltpu.VMEM((count, classes, width), jnp.float32)
    sems = lambda count: pltpu.SemaphoreType.DMA((count,))
    others = 2 * peers - 1
    return pl.pallas_call(
        functools.partial(sums_kernel, peers),
        in_specs=[pl.BlockSpec(memory_space=pltpu.VMEM)] * 4,
        out_specs=pl.BlockSpec(memory_space=pltpu.VMEM),
        out_shape=jax.ShapeDtypeStruct((classes, width), jnp.float32),
        scratch_shapes=[
            room(peers), room(peers), room(peers), room(depth), room(depth), room(depth - 1),
            pltpu.VMEM((others,) + mass.shape, jnp.float32),
            pltpu.VMEM((mass.shape[1], mass.shape[1]), jnp.float32),
            sems(peers), sems(peers), sems(depth), sems(depth), sems(depth - 1), sems(depth - 1),
            sems(others), sems(others),
        ],
        compiler_params=pltpu.CompilerParams(
            collective_id=2, has_side_effects=True, vmem_limit_bytes=48 * 1024 * 1024
        ),
    )(boxes, post, mass, refs)


PARTS = 4
QUARTERS = 4
TILES = 6
APART = ANGLES // QUARTERS
SLOTS = 128
LEVELS = 32767.0


def turned(block, shift):
    shift = shift % ANGLES
    if shift == 0:
        return block
    return jnp.concatenate([block[ANGLES - shift :], block[: ANGLES - shift]], axis=0)


def flip(block):
    return pltpu.roll(block, 64, 1)


def low_lanes(rows, width=64, period=128):
    lane = lax.broadcasted_iota(jnp.int32, (rows, 128), 1)
    return lax.rem(lane, period) < width


def encode(block, codes, scales, h):
    largest = jnp.maximum(jnp.max(jnp.abs(block), axis=0, keepdims=True), 1e-30)
    scaled = jnp.round(block * (LEVELS / largest))
    codes[h] = scaled.astype(jnp.int32).astype(jnp.int16)
    scales[h : h + 1, :] = largest * (1.0 / LEVELS)


def decode(codes, scales, h):
    return codes[h].astype(jnp.int32).astype(jnp.float32) * scales[h : h + 1, :]


def refs_fan(refs, fans, energies, p):
    cols = slice(p * STEP, (p + 1) * STEP)
    rows = refs[:, cols].astype(jnp.float32)
    plain = jnp.concatenate([rows, rows], axis=0).T
    low = low_lanes(ANGLES)
    for c in range(PARTS):
        base = p * STEP + c * ANGLES
        piece = plain[c * ANGLES : (c + 1) * ANGLES]
        energies[p * PARTS + c : p * PARTS + c + 1, :] = jnp.sum(piece * piece, axis=0, keepdims=True)
        both = jnp.where(low, piece, turned(piece, APART))
        fans[0, base : base + ANGLES, :] = both.astype(jnp.bfloat16)
        fans[1, base : base + ANGLES, :] = turned(both, SHIFT).astype(jnp.bfloat16)


def boxes_fan(boxes, fans, p):
    cols = slice(p * STEP, (p + 1) * STEP)
    plain = boxes[:, cols].astype(jnp.float32).T
    fans[0, cols, :] = plain.astype(jnp.bfloat16)
    for c in range(PARTS):
        base = p * STEP + c * ANGLES
        piece = plain[c * ANGLES : (c + 1) * ANGLES]
        fans[1, base : base + ANGLES, :] = turned(piece, -SHIFT).astype(jnp.bfloat16)


def scaled_boxes(boxes, weights, energies, lhs, offsets, p, first):
    rows = boxes.shape[0] // 2
    span, rest = pl.ds(first, rows), pl.ds(first + SLOTS, rows)
    low = low_lanes(rows)
    wide = [
        jnp.broadcast_to(
            weights[span, 2 * PARTS * p + c : 2 * PARTS * p + c + 1], (rows, 128)
        )
        for c in range(PARTS)
    ]
    total = sum(
        wide[c] * energies[p * PARTS + c : p * PARTS + c + 1, :] for c in range(PARTS)
    )
    offsets[span, :] = total if p == 0 else offsets[span, :] + total
    spread = [
        wide[0], jnp.where(low, wide[0], wide[1]), wide[1],
        wide[2], jnp.where(low, wide[2], wide[3]), wide[3],
    ]
    for t, factor in enumerate(spread):
        cols = slice(p * STEP + t * 128, p * STEP + (t + 1) * 128)
        scaled = boxes[span, cols].astype(jnp.float32) * factor
        high = scaled.astype(jnp.bfloat16)
        lhs[span, cols] = high
        lhs[rest, cols] = (scaled - high.astype(jnp.float32)).astype(jnp.bfloat16)


def score_tiles(lhs, fans, g, peers):
    total = None
    for p in range(peers):
        pieces = []
        for c in range(PARTS):
            base = p * STEP + c * ANGLES
            shift = 2 * SHIFT * g
            pieces.append(
                jnp.concatenate(
                    [
                        turned(fans[parity, base : base + ANGLES, :], shift + extra)
                        for parity in range(2) for extra in (0, 2 * APART)
                    ],
                    axis=1,
                )
            )
        part = jnp.dot(
            lhs[:, p * STEP : (p + 1) * STEP], jnp.concatenate(pieces, axis=0),
            preferred_element_type=jnp.float32,
        )
        total = part if total is None else total + part
    total = total[:SLOTS] + total[SLOTS:]
    return total[:, :256], total[:, 256:]


def class_sums(fans, post, shard):
    rows = []
    for c in range(PARTS):
        base = pl.multiple_of(shard * STEP + c * ANGLES, 64)
        even = fans[0, pl.ds(base, ANGLES), :]
        odd = fans[1, pl.ds(base, ANGLES), :]
        rows.append(
            jnp.concatenate(
                [turned(x, -2 * SHIFT * s) for s in range(TILES // 2) for x in (even, odd)], axis=1
            )
        )
    sums = jnp.dot(jnp.concatenate(rows, axis=0), post[...], preferred_element_type=jnp.float32)
    low, first = low_lanes(ANGLES), low_lanes(ANGLES, 32, 64)
    both = []
    for c in range(PARTS):
        piece = sums[c * ANGLES : (c + 1) * ANGLES]
        b = piece[:, :128] + turned(piece[:, 128:], -2 * APART)
        both.append((b, turned(b, -APART)))

    def pair(i, j):
        return jnp.where(low, both[i][0], both[j][1]) + flip(jnp.where(low, both[j][0], both[i][1]))

    a, b = pair(0, 2), pair(1, 3)
    return jnp.where(first, a, pltpu.roll(b, 32, 1)), jnp.where(first, pltpu.roll(a, 96, 1), b)


def whole_kernel(
    peers, boxes, counts, places_in, turns_in, refs, weights_in, strength_in, out, evidence,
    alive, places, turns, weights, strength, xs, rs, own, cards, duo, ref_fans, box_fans, energies, base_refs, box_weights, offsets, lhs, mine_s, theirs_s, terms,
    post, masses, y_out, y_out_s, y_in, y_in_s, keep, near_out, near_out_s, near_in, near_in_s, z_out, z_out_s, z_in, z_in_s, pair_out, pair_in,
    small_local, box_local, ref_local, own_local, box_send, box_recv, ref_send, ref_recv, card_send, card_recv,
    duo_send, duo_recv, score_send, score_recv, mass_send, mass_recv, y_send, y_recv, ys_send, ys_recv,
    near_send, near_recv, z_send, z_recv, zs_send, zs_recv, pair_send, pair_recv,
):
    mine, core = lax.axis_index("particle"), lax.axis_index("classes")
    depth, owned, classes = peers // 2, boxes.shape[0], refs.shape[0]
    level, side = mine // 2, lax.rem(mine, 2)
    partner = {"classes": 1 - core}
    across = {"particle": level * 2 + 1 - side}
    others = [{"particle": lax.rem(mine + d, peers)} for d in range(1, peers)]
    near, far = level + 1 - 2 * lax.rem(level, 2), lax.rem(level + 2, depth)
    levels = [lax.rem(near + 2, depth), far, near, level]
    diagonal = [{"particle": there * 2 + side, "classes": 1 - core} for there in (far, near)]
    straight = [{"particle": there * 2 + side} for there in (far, near)]
    barrier = pltpu.get_barrier_semaphore()
    friends = [partner] + others + diagonal
    for device in friends:
        pl.semaphore_signal(barrier, inc=1, device_id=device, device_id_type=MESH)
    box_rows = pl.ds(pl.multiple_of(core * owned, owned), owned)
    ref_rows = pl.ds(pl.multiple_of(core * classes, classes), classes)
    local = []
    for p in range(peers):
        source = pl.ds(pl.multiple_of((2 * p + core) * STEP, 128), STEP)
        target = pl.ds(p * STEP, STEP)
        local.append(
            pltpu.make_async_copy(refs.at[:, source], rs.at[ref_rows, target], ref_local.at[p])
        )
        local.append(
            pltpu.make_async_copy(boxes.at[:, source], xs.at[box_rows, target], box_local.at[p])
        )
    width = 2 * STEP
    own_copy = pltpu.make_async_copy(
        refs.at[:, pl.ds(pl.multiple_of(mine * width, 128), width)], own, own_local.at[0]
    )
    small = [
        pltpu.make_async_copy(source, target, small_local.at[n])
        for n, (source, target) in enumerate(
            [
                (counts, alive), (places_in, places), (turns_in, turns), (weights_in, weights), (strength_in, strength),
            ]
        )
    ]
    for copy in small + local + [own_copy]:
        copy.start()
    for copy in small:
        copy.wait()
    card = jnp.zeros((8, 128), jnp.float32)
    cards[mine] = card
    slot = lax.broadcasted_iota(jnp.int32, (1, owned), 1)
    cards[mine, 0:1, :CYCLES] = weights[...]
    cards[mine, 1:2, :owned] = places[...].astype(jnp.float32)
    cards[mine, 2:3, :owned] = turns[...].astype(jnp.float32)
    cards[mine, 3:4, :owned] = jnp.where(slot < alive[...], 1.0, 0.0)
    cards[mine, 4:5, :classes] = strength[...]
    duo[core] = cards[mine]

    started = []

    def send(src, dst, sends, recvs, device):
        copy = pltpu.make_async_remote_copy(
            src_ref=src, dst_ref=dst, send_sem=sends, recv_sem=recvs, device_id=device,
            device_id_type=MESH,
        )
        copy.start()
        started.append(copy)
        return copy

    pl.semaphore_wait(barrier, len(friends))
    card_copies = [
        send(cards.at[mine], cards.at[mine], card_send.at[d], card_recv.at[d], device)
        for d, device in enumerate(others)
    ]
    duo_copy = send(duo.at[core], duo.at[core], duo_send.at[0], duo_recv.at[0], partner)
    ref_copies, box_copies = [], []
    for p in range(peers):
        source = pl.ds(pl.multiple_of((2 * p + 1 - core) * STEP, 128), STEP)
        target = pl.ds(p * STEP, STEP)
        ref_copies.append(
            send(refs.at[:, source], rs.at[ref_rows, target], ref_send.at[p], ref_recv.at[p], partner)
        )
    for p in range(peers):
        source = pl.ds(pl.multiple_of((2 * p + 1 - core) * STEP, 128), STEP)
        target = pl.ds(p * STEP, STEP)
        box_copies.append(
            send(boxes.at[:, source], xs.at[box_rows, target], box_send.at[p], box_recv.at[p], partner)
        )
    own_copy.wait()
    for h in range(2):
        for c in range(PARTS):
            base = (h * PARTS + c) * ANGLES
            base_refs[h, c * classes : (c + 1) * classes, :] = own[:, base : base + ANGLES].astype(
                jnp.float32
            )
    for copy in local:
        copy.wait()
    for p in range(peers):
        ref_copies[p].wait_recv()
        refs_fan(rs, ref_fans, energies, p)

    duo_copy.wait_recv()
    facts = duo[0] + flip(duo[1])
    facts = jnp.concatenate([facts] * (SLOTS // 8), axis=0).T
    place, turn, live = facts[:, 1:2], facts[:, 2:3], facts[:, 3:4]
    force = duo[0, 4:5, :] + pltpu.roll(duo[1, 4:5, :], classes, 1)
    force = force + flip(force)
    lane = lax.broadcasted_iota(jnp.int32, (SLOTS, 128), 1).astype(jnp.float32)
    swing = jnp.cos(TWO_PI * (lane - turn) / ROTATIONS)
    for copy in card_copies:
        copy.wait_recv()
    spread = jnp.zeros((SLOTS, 128), jnp.float32)
    for g in range(peers):
        spread = jnp.where(place == float(g), cards[g, 0:1, :], spread)
    wsum = jnp.sum(spread, axis=1, keepdims=True)
    spread = jnp.where(core == 0, spread, pltpu.roll(spread, 128 - PARTS, 1))
    box_weights[...] = spread
    for p in range(peers):
        scaled_boxes(
            xs, box_weights, energies, lhs, offsets, p, pl.multiple_of(core * owned, owned)
        )
    for p in range(peers):
        box_copies[p].wait_recv()
        scaled_boxes(
            xs, box_weights, energies, lhs, offsets, p, pl.multiple_of((1 - core) * owned, owned)
        )
    base = -0.5 * offsets[...]

    low = low_lanes(SLOTS)
    score_copies, tops, norms = [], [], []

    def finish(f):
        score_copies[f].wait_recv()
        values = []
        for t in range(2):
            cols = slice(t * 128, (t + 1) * 128)
            r = f + 2 * t * TILES
            prior = jnp.where(low, swing[:, r : r + 1], swing[:, r + TILES : r + TILES + 1]) * force
            values.append(mine_s[f, :, cols] + theirs_s[f, :, cols] + prior)
        top = jnp.max(jnp.maximum(values[0], values[1]), axis=1, keepdims=True)
        values = [jnp.exp(v - top) for v in values]
        for t in range(2):
            terms[f, :, t * 128 : (t + 1) * 128] = values[t]
        tops.append(top)
        norms.append(jnp.sum(values[0] + values[1], axis=1, keepdims=True))

    for g in range(TILES // 2):
        for f, tile in enumerate(score_tiles(lhs, ref_fans, g, peers), 2 * g):
            mine_s[f] = tile + jnp.concatenate([base, base], axis=1)
        for f in (2 * g, 2 * g + 1):
            score_copies.append(
                send(mine_s.at[f], theirs_s.at[f], score_send.at[f], score_recv.at[f], partner)
            )
        if g > 0:
            finish(2 * g - 2)
            finish(2 * g - 1)
    for p in range(peers):
        boxes_fan(xs, box_fans, p)
    finish(TILES - 2)
    finish(TILES - 1)
    top = functools.reduce(jnp.maximum, tops)
    factors = [jnp.exp(t - top) for t in tops]
    norm = sum(n * s for n, s in zip(norms, factors))
    mass = jnp.zeros((8, 256), jnp.float32)
    for f in range(TILES):
        factor = jnp.where(live > 0.0, factors[f] / norm, 0.0)
        value = (terms[f] * factor).astype(jnp.bfloat16)
        post[f * SLOTS : (f + 1) * SLOTS, :] = value
        value = value.astype(jnp.float32)
        for i in range(SLOTS // 8):
            mass = mass + value[i * 8 : (i + 1) * 8]
    mass = mass[:, :128] + mass[:, 128:]
    mass = mass + flip(mass)
    masses[mine] = jnp.broadcast_to(jnp.sum(mass, axis=0, keepdims=True), (8, 128))
    mass_copies = [
        send(masses.at[mine], masses.at[mine], mass_send.at[d], mass_recv.at[d], device)
        for d, device in enumerate(others)
    ]
    proof = jnp.where(live > 0.0, (top + jnp.log(norm)) / (ANGLES * wsum), 0.0)
    proof = jnp.broadcast_to(proof, (SLOTS, 128)).T[0:1]
    evidence[...] = jnp.where(core == 0, proof, flip(proof))[:, :owned]

    y_copies, z_copies, near_copies = [], [], []

    def away(i, blocks):
        for h, value in enumerate(blocks):
            encode(value, y_out.at[i], y_out_s.at[i], h)
        y_copies.append(
            [
                send(y_out.at[i], y_in.at[i], y_send.at[i], y_recv.at[i], across),
                send(y_out_s.at[i], y_in_s.at[i], ys_send.at[i], ys_recv.at[i], across),
            ]
        )

    def home(i, blocks):
        for h, value in enumerate(blocks):
            keep[i, h] = value

    def advance(i):
        for copy in y_copies[i] + (near_copies if i == 1 else []):
            copy.wait_recv()
        for h in range(2):
            total = keep[i, h] + decode(y_in.at[i], y_in_s.at[i], h)
            if i == 0:
                encode(total, near_out, near_out_s, h)
            elif i == 1:
                encode(total + decode(near_in, near_in_s, h), z_out.at[0], z_out_s.at[0], h)
            elif i == 2:
                encode(total, z_out.at[1], z_out_s.at[1], h)
            else:
                keep[i, h] = total
        if i == 0:
            near_copies.append(
                send(near_out, near_in, near_send.at[0], near_recv.at[0], straight[1])
            )
            near_copies.append(
                send(near_out_s, near_in_s, near_send.at[1], near_recv.at[1], straight[1])
            )
            return None
        if i == depth - 1:
            pair_out[...] = jnp.where(core == 0, keep[i, 1], keep[i, 0])
            return send(pair_out, pair_in, pair_send.at[0], pair_recv.at[0], partner)
        j = i - 1
        for n, device in enumerate([straight[j], diagonal[j]]):
            half = core if n == 0 else 1 - core
            z_copies.append(
                send(z_out.at[j, half], z_in.at[j, core], z_send.at[j, n], z_recv.at[j, n], device)
            )
            z_copies.append(
                send(z_out_s.at[j], z_in_s.at[j, core], zs_send.at[j, n], zs_recv.at[j, n], device)
            )
        return None

    shards = lambda i: (levels[i] * 2 + 1 - side, levels[i] * 2 + side)
    away(0, class_sums(box_fans, post, shards(0)[0]))
    for i in range(1, depth):
        held = class_sums(box_fans, post, shards(i - 1)[1])
        away(i, class_sums(box_fans, post, shards(i)[0]))
        home(i - 1, held)
        if i == 2:
            advance(0)
    home(depth - 1, class_sums(box_fans, post, shards(depth - 1)[1]))
    for i in range(1, depth - 1):
        advance(i)
    pair_copy = advance(depth - 1)

    for copy in mass_copies:
        copy.wait_recv()
    weight = masses[0]
    for g in range(1, peers):
        weight = weight + masses[g]
    first = low_lanes(8, 32, 64)
    weight = jnp.where(
        core == 0,
        jnp.where(first, weight, pltpu.roll(weight, 32, 1)),
        jnp.where(first, pltpu.roll(weight, 96, 1), weight),
    )
    scale = jnp.concatenate([weight] * 16, axis=0).T[:, 0:1] + 1.0
    for copy in z_copies:
        copy.wait_recv()
    pair_copy.wait_recv()
    held = jnp.where(core == 0, keep[depth - 1, 0], keep[depth - 1, 1])
    for h in range(2):
        total = jnp.where(core == h, held, pair_in[...])
        for i in range(2):
            factor = jnp.where(core == 0, z_in_s[i, h, 0:1, :], z_in_s[i, h, 1:2, :])
            total = total + z_in[i, h].astype(jnp.int32).astype(jnp.float32) * factor
        result = (total.T + base_refs[h]) / scale
        for c in range(PARTS):
            out[:, h * PARTS + c, :] = result[c * classes : (c + 1) * classes]
    for copy in started:
        copy.wait_send()


def whole(boxes, counts, places, turns, refs, weights, strength, peers):
    given = (boxes, counts, places, turns, refs, weights, strength)
    classes, depth = refs.shape[0], peers // 2
    half = CYCLES * ANGLES // 2
    f32, bf16, i16 = jnp.float32, jnp.bfloat16, jnp.int16
    room = lambda dtype, *shape: pltpu.VMEM(shape, dtype)
    sems = lambda *shape: pltpu.SemaphoreType.DMA(shape)
    vmem = pl.BlockSpec(memory_space=pltpu.VMEM)
    hbm = pl.BlockSpec(memory_space=pltpu.HBM)
    return pl.pallas_call(
        functools.partial(whole_kernel, peers),
        in_specs=[hbm] * 7,
        out_specs=[vmem, vmem],
        out_shape=[
            jax.ShapeDtypeStruct((classes, CYCLES // peers, ANGLES), f32),
            jax.ShapeDtypeStruct((1, boxes.shape[0]), f32),
        ],
        scratch_shapes=[
            pltpu.VMEM(counts.shape, counts.dtype), pltpu.VMEM(places.shape, places.dtype),
            pltpu.VMEM(turns.shape, turns.dtype), pltpu.VMEM(weights.shape, f32),
            pltpu.VMEM(strength.shape, f32), room(bf16, SLOTS, half), room(bf16, 2 * classes, half), room(bf16, classes, 2 * STEP),
            room(f32, peers, 8, 128), room(f32, 2, 8, 128),
            room(bf16, 2, half, 128), room(bf16, 2, half, 128), room(f32, CYCLES // 2, 128),
            room(f32, 2, 128, ANGLES), room(f32, SLOTS, 128), room(f32, SLOTS, 128), room(bf16, 2 * SLOTS, half),
            room(f32, TILES, SLOTS, 256), room(f32, TILES, SLOTS, 256), room(f32, TILES, SLOTS, 256),
            room(bf16, TILES * SLOTS, 256), room(f32, peers, 8, 128),
            room(i16, depth, 2, ANGLES, 128), room(f32, depth, 8, 128),
            room(i16, depth, 2, ANGLES, 128), room(f32, depth, 8, 128),
            room(f32, depth, 2, ANGLES, 128),
            room(i16, 2, ANGLES, 128), room(f32, 8, 128), room(i16, 2, ANGLES, 128), room(f32, 8, 128),
            room(i16, 2, 2, ANGLES, 128), room(f32, 2, 8, 128),
            room(i16, 2, 2, ANGLES, 128), room(f32, 2, 2, 8, 128),
            room(f32, ANGLES, 128), room(f32, ANGLES, 128),
            sems(5), sems(peers), sems(peers), sems(1), sems(peers), sems(peers), sems(peers), sems(peers),
            sems(peers - 1), sems(peers - 1), sems(1), sems(1), sems(TILES), sems(TILES),
            sems(peers - 1), sems(peers - 1), sems(depth), sems(depth), sems(depth), sems(depth),
            sems(2), sems(2), sems(2, 2), sems(2, 2), sems(2, 2), sems(2, 2),
            sems(1), sems(1),
        ],
        compiler_params=pltpu.CompilerParams(
            collective_id=3, has_side_effects=True, vmem_limit_bytes=48 * 1024 * 1024
        ),
    )(*[pltpu.with_memory_space_constraint(x, pltpu.HBM) for x in given])


def on_device(boxes, counts, destinations, prior_rot, references, cycle_weights, prior_strength):
    peers = lax.axis_size("particle")
    cycle_index = lax.axis_index("particle")
    cycles_dev = CYCLES // peers
    width = cycles_dev * ANGLES
    if width == 2 * STEP:
        new_references, evidence = whole(
            boxes, jnp.broadcast_to(counts[None, :], (1, boxes.shape[0])), destinations[None, :], prior_rot[None, :], references,
            cycle_weights, prior_strength[None, :], peers,
        )
        return new_references, evidence[0]
    owned = boxes.shape[0]
    classes_dev = references.shape[0]
    lane_index = lax.axis_index("classes")
    row = jnp.concatenate([cycle_weights[0], prior_strength])
    row = jnp.pad(row, (0, 128 - row.shape[0]))[None, :]
    refs, rows = gathered(references, row, peers)
    refs = refs.reshape(2 * classes_dev, -1)
    group_wts = rows[:peers, 0, :CYCLES]
    other = rows[peers, 0, CYCLES : CYCLES + classes_dev]
    strength = jnp.where(
        lane_index == 0,
        jnp.concatenate([prior_strength, other]),
        jnp.concatenate([other, prior_strength]),
    ).reshape(1, -1)
    mine = destinations[:, None] == jnp.arange(peers, dtype=jnp.int32)[None, :]
    wts = jnp.sum(jnp.where(mine[:, :, None], group_wts[None], 0.0), axis=1)
    live = (jnp.arange(owned, dtype=jnp.int32) < counts[0]).astype(jnp.float32)
    turn_ids = jnp.arange(ROTATIONS, dtype=jnp.float32)
    gap = TWO_PI * (turn_ids[None, :] - prior_rot[:, None].astype(jnp.float32)) / ROTATIONS
    aux = jnp.concatenate([jnp.cos(gap), live[:, None], jnp.sum(wts, axis=1)[:, None]], axis=1)
    wts = jnp.transpose(wts.reshape(owned, STEPS, STEP_CYCLES), (1, 0, 2))
    post, mass, evidence = scores(
        boxes, refs, wts, aux, jnp.concatenate([strength, strength], axis=1)
    )
    if width % STEP == 0:
        new_references = fused_sums(boxes, post, mass, references, peers)
    else:
        sums = scattered(plain_sums(boxes, post, mass, classes_dev, peers))
        own_refs = lax.dynamic_slice_in_dim(references, cycle_index * width, width, 1)
        new_references = (sums[:, :width] + own_refs.astype(jnp.float32)) / (
            sums[:, width : width + 1] + 1.0
        )
    return new_references.reshape(classes_dev, cycles_dev, ANGLES), evidence[:, 0]


def solution(mesh):
    in_specs = (
        P(("groups", "particle", "classes"), None),
        P(("groups", "particle", "classes")),
        P(("groups", "particle", "classes")),
        P(("groups", "particle", "classes")),
        P(("groups", "classes"), None),
        P(("groups", "particle"), None),
        P(("groups", "classes")),
    )
    out_specs = (P(("groups", "classes"), "particle", None), P(("groups", "particle", "classes")))
    return jax.shard_map(
        on_device, mesh=mesh, in_specs=in_specs, out_specs=out_specs, check_vma=False
    )
```

```python
import functools
import math

import jax
import jax.numpy as jnp
from jax import lax
from jax.experimental import pallas as pl
from jax.experimental.pallas import tpu as pltpu
from jax.sharding import PartitionSpec as P

CYCLES = 64
ANGLES = 192
ROTATIONS = 24
FINE = 4
COARSE = ROTATIONS // FINE
SHIFT = ANGLES // ROTATIONS
STEP_CYCLES = 4
STEP = STEP_CYCLES * ANGLES
STEPS = CYCLES // STEP_CYCLES
TWO_PI = 2.0 * math.pi


def roll_rows(block, shift):
    shift = shift % ANGLES
    if shift == 0:
        return block
    pieces = []
    for c in range(STEP_CYCLES):
        base = c * ANGLES
        pieces.append(block[base + ANGLES - shift : base + ANGLES])
        pieces.append(block[base : base + ANGLES - shift])
    return jnp.concatenate(pieces, axis=0)


def fan_out(rows, sign):
    plain = jnp.concatenate([rows, rows], axis=0).T
    low = lax.broadcasted_iota(jnp.int32, plain.shape, 1) < rows.shape[0]
    tiles = [
        jnp.where(low, roll_rows(plain, sign * SHIFT * f), roll_rows(plain, sign * SHIFT * (f + 1)))
        for f in range(0, FINE, 2)
    ]
    return jnp.concatenate([t.astype(jnp.bfloat16) for t in tiles], axis=1), plain


def score_kernel(boxes_ref, refs_ref, wts_ref, aux_ref, str_ref, post, mass, ev_ref, acc, off):
    step = pl.program_id(0)
    owned = boxes_ref.shape[0]
    half = str_ref.shape[1]

    @pl.when(step == 0)
    def _():
        acc[...] = jnp.zeros_like(acc)
        off[...] = jnp.zeros_like(off)

    @pl.when(step >= 0)
    def _():
        wts = wts_ref[0]
        lane = lax.broadcasted_iota(jnp.int32, (owned, STEP), 1)
        spread = jnp.broadcast_to(wts[:, 0:1], (owned, STEP))
        for c in range(1, STEP_CYCLES):
            spread = jnp.where(lane >= c * ANGLES, wts[:, c : c + 1], spread)
        scaled = boxes_ref[...].astype(jnp.float32) * spread
        high = scaled.astype(jnp.bfloat16)
        rest = (scaled - high.astype(jnp.float32)).astype(jnp.bfloat16)
        lhs = jnp.concatenate([high, rest], axis=0)
        fan, plain = fan_out(refs_ref[...].astype(jnp.float32), 1)
        total = off[...]
        for c in range(STEP_CYCLES):
            piece = plain[c * ANGLES : (c + 1) * ANGLES]
            total = total + wts[:, c : c + 1] * jnp.sum(piece * piece, axis=0, keepdims=True)
        off[...] = total
        for q in range(COARSE):
            acc[q] += jnp.dot(
                lhs, roll_rows(fan, SHIFT * FINE * q), preferred_element_type=jnp.float32
            )

    @pl.when(step == STEPS - 1)
    def _():
        aux = aux_ref[...]
        live = aux[:, ROTATIONS : ROTATIONS + 1]
        wsum = aux[:, ROTATIONS + 1 : ROTATIONS + 2]
        low = lax.broadcasted_iota(jnp.int32, (owned, half), 1) < owned
        base = -0.5 * off[...]
        strength = str_ref[...]
        top = None
        for q in range(COARSE):
            for t in range(FINE // 2):
                r = q * FINE + 2 * t
                cols = slice(t * half, (t + 1) * half)
                turn = jnp.where(low, aux[:, r : r + 1], aux[:, r + 1 : r + 2])
                score = acc[q, :owned, cols] + acc[q, owned:, cols] + base + turn * strength
                acc[q, :owned, cols] = score
                top = score if top is None else jnp.maximum(top, score)
        top = jnp.max(top, axis=1, keepdims=True)
        norm = jnp.zeros((owned, half), jnp.float32)
        for q in range(COARSE):
            for t in range(FINE // 2):
                cols = slice(t * half, (t + 1) * half)
                term = jnp.exp(acc[q, :owned, cols] - top)
                acc[q, :owned, cols] = term
                norm = norm + term
        norm = jnp.sum(norm, axis=1, keepdims=True)
        ev_ref[...] = jnp.where(live > 0.0, (top + jnp.log(norm)) / (ANGLES * wsum), 0.0)
        seen = jnp.zeros((owned, half), jnp.float32)

        def weight(q, t):
            cols = slice(t * half, (t + 1) * half)
            value = jnp.where(live > 0.0, acc[q, :owned, cols] / norm, 0.0)
            return value.astype(jnp.bfloat16).astype(jnp.float32)

        for q in range(0, COARSE, 2):
            for t in range(FINE // 2):
                first, second = weight(q, t), weight(q + 1, t)
                seen = seen + first + second
                even = jnp.where(low, first, pltpu.roll(second, half // 2, 1))
                odd = jnp.where(low, pltpu.roll(first, half // 2, 1), second)
                cols = slice(q // 2 * half, (q // 2 + 1) * half)
                post[2 * t * owned : (2 * t + 1) * owned, cols] = even.astype(jnp.bfloat16)
                post[(2 * t + 1) * owned : (2 * t + 2) * owned, cols] = odd.astype(jnp.bfloat16)
        seen = jnp.sum(seen, axis=0, keepdims=True)
        mass[...] = seen + pltpu.roll(seen, half // 2, 1)


def turned_sums(boxes, post):
    half = 2 * boxes.shape[0]
    fan, _unused = fan_out(boxes.astype(jnp.float32), -1)
    sums = jnp.dot(fan, post, preferred_element_type=jnp.float32)
    both = sums[:, :half]
    for p in range(1, COARSE // 2):
        both = both + roll_rows(sums[:, p * half : (p + 1) * half], -2 * p * SHIFT * FINE)
    whole = both + pltpu.roll(roll_rows(both, -SHIFT * FINE), half // 2, 1)
    return whole.T


def plain_sums_kernel(width, boxes_ref, post_ref, mass_ref, out_ref):
    turned = turned_sums(boxes_ref[...], post_ref[...])
    classes = out_ref.shape[2]
    mass = jnp.broadcast_to(mass_ref[...], (128, 128)).T
    for h in range(2):
        rows = turned[h * classes : (h + 1) * classes]
        tail = mass[h * classes : (h + 1) * classes, : out_ref.shape[3] - width]
        for j in range(STEP // width):
            out_ref[j, h, :, :width] = rows[:, j * width : (j + 1) * width]
            out_ref[j, h, :, width:] = tail


def plain_sums(boxes, post, mass, classes, peers):
    width = CYCLES // peers * ANGLES
    padded = (width + 1 + 127) // 128 * 128
    return pl.pallas_call(
        functools.partial(plain_sums_kernel, width),
        grid=(STEPS,),
        in_specs=[
            pl.BlockSpec((boxes.shape[0], STEP), lambda i: (0, i)),
            pl.BlockSpec(post.shape, lambda i: (0, 0)),
            pl.BlockSpec(mass.shape, lambda i: (0, 0)),
        ],
        out_specs=pl.BlockSpec((STEP // width, 2, classes, padded), lambda i: (i, 0, 0, 0)),
        out_shape=jax.ShapeDtypeStruct((peers, 2, classes, padded), jnp.float32),
    )(boxes, post, mass)


def scores(boxes, refs, wts, aux, strength):
    owned, classes, half = boxes.shape[0], refs.shape[0], strength.shape[1]
    whole = lambda shape: pl.BlockSpec(shape, lambda i: (0, 0))
    post = (FINE * owned, COARSE * classes)
    return pl.pallas_call(
        score_kernel,
        grid=(STEPS,),
        in_specs=[
            pl.BlockSpec((owned, STEP), lambda i: (0, i)),
            pl.BlockSpec((classes, STEP), lambda i: (0, i)),
            pl.BlockSpec((1, owned, STEP_CYCLES), lambda i: (i, 0, 0)),
            whole(aux.shape),
            whole((1, half)),
        ],
        out_specs=[whole(post), whole((1, half)), whole((owned, 1))],
        out_shape=[
            jax.ShapeDtypeStruct(post, jnp.bfloat16),
            jax.ShapeDtypeStruct((1, half), jnp.float32),
            jax.ShapeDtypeStruct((owned, 1), jnp.float32),
        ],
        scratch_shapes=[
            pltpu.VMEM((COARSE, 2 * owned, FINE * classes), jnp.float32),
            pltpu.VMEM((owned, half), jnp.float32),
        ],
        compiler_params=pltpu.CompilerParams(
            dimension_semantics=("arbitrary",), vmem_limit_bytes=40 * 1024 * 1024
        ),
    )(boxes, refs, wts, aux, strength)


MESH = pl.DeviceIdType.MESH
CHUNKS = 4


def greet(devices):
    barrier = pltpu.get_barrier_semaphore()
    for device in devices:
        pl.semaphore_signal(barrier, inc=1, device_id=device, device_id_type=MESH)
    pl.semaphore_wait(barrier, len(devices))


def gather_kernel(peers, refs_ref, row_ref, all_refs, all_rows, local, send, recv):
    mine, core = lax.axis_index("particle"), lax.axis_index("classes")
    partner = {"classes": 1 - core}
    others = [{"particle": lax.rem(mine + d, peers)} for d in range(1, peers)]
    greet([partner] + others)
    copies = [
        pltpu.make_async_remote_copy(
            src_ref=refs_ref, dst_ref=all_refs.at[core], send_sem=send.at[0], recv_sem=recv.at[0],
            device_id=partner, device_id_type=MESH,
        ),
        pltpu.make_async_remote_copy(
            src_ref=row_ref, dst_ref=all_rows.at[peers], send_sem=send.at[1], recv_sem=recv.at[1],
            device_id=partner, device_id_type=MESH,
        ),
    ]
    for d, other in enumerate(others):
        copies.append(
            pltpu.make_async_remote_copy(
                src_ref=row_ref, dst_ref=all_rows.at[mine], send_sem=send.at[2 + d],
                recv_sem=recv.at[2 + d], device_id=other, device_id_type=MESH,
            )
        )
    for copy in copies:
        copy.start()
    own = [
        pltpu.make_async_copy(refs_ref, all_refs.at[core], local.at[0]),
        pltpu.make_async_copy(row_ref, all_rows.at[mine], local.at[1]),
    ]
    for copy in own:
        copy.start()
    for copy in own + copies:
        copy.wait()


def gathered(refs, row, peers):
    return pl.pallas_call(
        functools.partial(gather_kernel, peers),
        in_specs=[pl.BlockSpec(memory_space=pltpu.VMEM)] * 2,
        out_specs=[pl.BlockSpec(memory_space=pltpu.VMEM)] * 2,
        out_shape=[
            jax.ShapeDtypeStruct((2,) + refs.shape, refs.dtype),
            jax.ShapeDtypeStruct((peers + 1,) + row.shape, row.dtype),
        ],
        scratch_shapes=[
            pltpu.SemaphoreType.DMA((2,)),
            pltpu.SemaphoreType.DMA((peers + 1,)),
            pltpu.SemaphoreType.DMA((peers + 1,)),
        ],
        compiler_params=pltpu.CompilerParams(collective_id=0, has_side_effects=True),
    )(refs, row)


def scatter_kernel(depth, parts, out, pair_in, side_out, side_in, line_out, line_in,
                   pair_send, pair_recv, side_send, side_recv, line_send, line_recv):
    mine, core = lax.axis_index("particle"), lax.axis_index("classes")
    level, side = mine // 2, lax.rem(mine, 2)
    partner = {"classes": 1 - core}
    across = {"particle": level * 2 + 1 - side}
    levels = [lax.rem(level + d, depth) for d in range(1, depth)]
    line = [{"particle": other * 2 + side} for other in levels]
    greet([partner, across] + line)
    rows = out.shape[0] // CHUNKS
    pair, cross, lines = [], [], []
    for j in range(CHUNKS):
        copy = pltpu.make_async_remote_copy(
            src_ref=parts.at[:, :, 1 - core, j * rows : (j + 1) * rows], dst_ref=pair_in.at[j],
            send_sem=pair_send.at[j], recv_sem=pair_recv.at[j], device_id=partner,
            device_id_type=MESH,
        )
        copy.start()
        pair.append(copy)
    for j in range(CHUNKS):
        span = slice(j * rows, (j + 1) * rows)
        pair[j].wait_recv()
        side_out[j] = parts[:, 1 - side, core, span] + pair_in[j, :, 1 - side]
        copy = pltpu.make_async_remote_copy(
            src_ref=side_out.at[j], dst_ref=side_in.at[j], send_sem=side_send.at[j],
            recv_sem=side_recv.at[j], device_id=across, device_id_type=MESH,
        )
        copy.start()
        cross.append(copy)
        line_out[j] = parts[:, side, core, span] + pair_in[j, :, side]
    for j in range(CHUNKS):
        cross[j].wait_recv()
        line_out[j] = line_out[j] + side_in[j]
        for d in range(depth - 1):
            copy = pltpu.make_async_remote_copy(
                src_ref=line_out.at[j, levels[d]], dst_ref=line_in.at[j, d],
                send_sem=line_send.at[j, d], recv_sem=line_recv.at[j, d], device_id=line[d],
                device_id_type=MESH,
            )
            copy.start()
            lines.append(copy)
    for j in range(CHUNKS):
        total = line_out[j, level]
        for d in range(depth - 1):
            lines[j * (depth - 1) + d].wait_recv()
            total = total + line_in[j, d]
        out[j * rows : (j + 1) * rows] = total
    for copy in pair + cross + lines:
        copy.wait_send()


def scattered(parts):
    peers, _, classes, width = parts.shape
    depth = peers // 2
    rows = classes // CHUNKS
    sems = pltpu.SemaphoreType.DMA((CHUNKS,))
    line_sems = pltpu.SemaphoreType.DMA((CHUNKS, max(depth - 1, 1)))
    return pl.pallas_call(
        functools.partial(scatter_kernel, depth),
        in_specs=[pl.BlockSpec(memory_space=pltpu.VMEM)],
        out_specs=pl.BlockSpec(memory_space=pltpu.VMEM),
        out_shape=jax.ShapeDtypeStruct((classes, width), jnp.float32),
        scratch_shapes=[
            pltpu.VMEM((CHUNKS, depth, 2, rows, width), jnp.float32),
            pltpu.VMEM((CHUNKS, depth, rows, width), jnp.float32),
            pltpu.VMEM((CHUNKS, depth, rows, width), jnp.float32),
            pltpu.VMEM((CHUNKS, depth, rows, width), jnp.float32),
            pltpu.VMEM((CHUNKS, max(depth - 1, 1), rows, width), jnp.float32),
            sems, sems, sems, sems, line_sems, line_sems,
        ],
        compiler_params=pltpu.CompilerParams(
            collective_id=1, has_side_effects=True, vmem_limit_bytes=48 * 1024 * 1024
        ),
    )(parts.reshape(depth, 2, 2, classes, width))


def sums_kernel(peers, boxes, post, mass, refs, out, pair_out, pair_in, keep, side_out, side_in,
                line_in, mass_in, column, pair_send, pair_recv, side_send, side_recv, line_send,
                line_recv, mass_send, mass_recv):
    mine, core = lax.axis_index("particle"), lax.axis_index("classes")
    depth, width, classes = peers // 2, out.shape[1], out.shape[0]
    level, side = mine // 2, lax.rem(mine, 2)
    place = mine * 2 + core
    partner = {"classes": 1 - core}
    across = {"particle": level * 2 + 1 - side}
    everyone = []
    for e in range(1, 2 * peers):
        there = lax.rem(place + e, 2 * peers)
        everyone.append({"particle": there // 2, "classes": lax.rem(there, 2)})
    greet(everyone)
    started, masses = [], []

    def send(src, dst, sends, recvs, device):
        copy = pltpu.make_async_remote_copy(
            src_ref=src, dst_ref=dst, send_sem=sends, recv_sem=recvs, device_id=device,
            device_id_type=MESH,
        )
        copy.start()
        started.append(copy)
        return copy

    for e, device in enumerate(everyone):
        masses.append(
            send(mass, mass_in.at[e], mass_send.at[e], mass_recv.at[e], device)
        )
    turns = list(range(1, depth)) + [0]
    blocks = [(i, d, True) for i, d in enumerate(turns)] + [(i, d, False) for i, d in enumerate(turns)]
    pair, cross, lines = [], [], []

    def advance(n):
        i, d, away = blocks[n]
        pair[n].wait_recv()
        if away:
            side_out[i] = keep[n] + pair_in[n]
            cross.append(
                send(side_out.at[i], side_in.at[i], side_send.at[i], side_recv.at[i], across)
            )
            return
        cross[i].wait_recv()
        keep[n] = keep[n] + pair_in[n] + side_in[i]
        if d > 0:
            there = {"particle": lax.rem(level + d, depth) * 2 + side}
            lines.append(
                send(keep.at[n], line_in.at[i], line_send.at[i], line_recv.at[i], there)
            )

    for n, (i, d, away) in enumerate(blocks):
        shard = lax.rem(level + d, depth) * 2 + (1 - side if away else side)

        @pl.loop(0, width // STEP)
        def _(part):
            source = pl.multiple_of(shard * width + part * STEP, 128)
            target = pl.multiple_of(part * STEP, 128)
            turned = turned_sums(boxes[:, pl.ds(source, STEP)], post[...])
            low, high = turned[:classes], turned[classes : 2 * classes]
            keep[n, :, pl.ds(target, STEP)] = jnp.where(core == 0, low, high)
            pair_out[n, :, pl.ds(target, STEP)] = jnp.where(core == 0, high, low)

        pair.append(send(pair_out.at[n], pair_in.at[n], pair_send.at[n], pair_recv.at[n], partner))
        if n > 0:
            advance(n - 1)
    advance(len(blocks) - 1)
    weight = mass[...]
    for e, copy in enumerate(masses):
        copy.wait_recv()
        weight = weight + mass_in[e]
    column[...] = jnp.broadcast_to(weight, column.shape).T
    scale = column[pl.ds(pl.multiple_of(core * classes, 8), classes), :]
    total = keep[len(blocks) - 1]
    for i in range(depth - 1):
        lines[i].wait_recv()
        total = total + line_in[i]
    base = refs[:, pl.ds(pl.multiple_of(mine * width, 128), width)].astype(jnp.float32)
    out[...] = (total + base) / (scale[:, 0:1] + 1.0)
    for copy in started:
        copy.wait_send()


def fused_sums(boxes, post, mass, refs, peers):
    classes, width, depth = refs.shape[0], CYCLES // peers * ANGLES, peers // 2
    room = lambda count: pltpu.VMEM((count, classes, width), jnp.float32)
    sems = lambda count: pltpu.SemaphoreType.DMA((count,))
    others = 2 * peers - 1
    return pl.pallas_call(
        functools.partial(sums_kernel, peers),
        in_specs=[pl.BlockSpec(memory_space=pltpu.VMEM)] * 4,
        out_specs=pl.BlockSpec(memory_space=pltpu.VMEM),
        out_shape=jax.ShapeDtypeStruct((classes, width), jnp.float32),
        scratch_shapes=[
            room(peers), room(peers), room(peers), room(depth), room(depth), room(depth - 1),
            pltpu.VMEM((others,) + mass.shape, jnp.float32),
            pltpu.VMEM((mass.shape[1], mass.shape[1]), jnp.float32),
            sems(peers), sems(peers), sems(depth), sems(depth), sems(depth - 1), sems(depth - 1),
            sems(others), sems(others),
        ],
        compiler_params=pltpu.CompilerParams(
            collective_id=2, has_side_effects=True, vmem_limit_bytes=48 * 1024 * 1024
        ),
    )(boxes, post, mass, refs)


PARTS = 4
QUARTERS = 4
TILES = 6
APART = ANGLES // QUARTERS
SLOTS = 128
LEVELS = 32767.0


def turned(block, shift):
    shift = shift % ANGLES
    if shift == 0:
        return block
    return jnp.concatenate([block[ANGLES - shift :], block[: ANGLES - shift]], axis=0)


def flip(block):
    return pltpu.roll(block, 64, 1)


def low_lanes(rows, width=64, period=128):
    lane = lax.broadcasted_iota(jnp.int32, (rows, 128), 1)
    return lax.rem(lane, period) < width


def encode(block, codes, scales):
    largest = jnp.maximum(jnp.max(jnp.abs(block), axis=0, keepdims=True), 1e-30)
    codes[...] = jnp.round(block * (LEVELS / largest)).astype(jnp.int32).astype(jnp.int16)
    scales[0:1, :] = largest * (1.0 / LEVELS)


def refs_fan(refs, fans, energies, p):
    cols = slice(p * STEP, (p + 1) * STEP)
    rows = refs[:, cols].astype(jnp.float32)
    plain = jnp.concatenate([rows, rows], axis=0).T
    low = low_lanes(ANGLES)
    for c in range(PARTS):
        base = p * STEP + c * ANGLES
        piece = plain[c * ANGLES : (c + 1) * ANGLES]
        energies[p * PARTS + c : p * PARTS + c + 1, :] = jnp.sum(piece * piece, axis=0, keepdims=True)
        both = jnp.where(low, piece, turned(piece, APART))
        fans[0, base : base + ANGLES, :] = both.astype(jnp.bfloat16)
        fans[1, base : base + ANGLES, :] = turned(both, SHIFT).astype(jnp.bfloat16)


def boxes_fan(boxes, fans, p):
    cols = slice(p * STEP, (p + 1) * STEP)
    plain = boxes[:, cols].astype(jnp.float32).T
    fans[0, cols, :] = plain.astype(jnp.bfloat16)
    for c in range(PARTS):
        base = p * STEP + c * ANGLES
        piece = plain[c * ANGLES : (c + 1) * ANGLES]
        fans[1, base : base + ANGLES, :] = turned(piece, -SHIFT).astype(jnp.bfloat16)


def score_tiles(boxes, fans, wide, g, cycles):
    totals = [None, None]
    blank = jnp.zeros((256 - ANGLES, 256), jnp.bfloat16)
    for c in range(cycles):
        base, window = c * ANGLES, c // 2 * 2 * ANGLES + c % 2 * 128
        factor = wide[c]
        factor = jnp.concatenate([factor, factor], axis=1)
        for parity in range(2):
            piece = fans[parity, base : base + ANGLES, :]
            shift = 2 * SHIFT * g
            piece = jnp.concatenate(
                [turned(piece, shift), turned(piece, shift + 2 * APART)], axis=1
            )
            piece = jnp.concatenate([piece, blank] if c % 2 == 0 else [blank, piece], axis=0)
            part = factor * jnp.dot(
                boxes[:, window : window + 256], piece, preferred_element_type=jnp.float32
            )
            totals[parity] = part if totals[parity] is None else totals[parity] + part
    return totals


def class_sums(fans, post, shard):
    rows = []
    for c in range(PARTS):
        base = pl.multiple_of(shard * STEP + c * ANGLES, 64)
        even = fans[0, pl.ds(base, ANGLES), :]
        odd = fans[1, pl.ds(base, ANGLES), :]
        rows.append(
            jnp.concatenate(
                [turned(x, -2 * SHIFT * s) for s in range(TILES // 2) for x in (even, odd)], axis=1
            )
        )
    sums = jnp.dot(jnp.concatenate(rows, axis=0), post[...], preferred_element_type=jnp.float32)
    low, first = low_lanes(ANGLES), low_lanes(ANGLES, 32, 64)
    both = []
    for c in range(PARTS):
        piece = sums[c * ANGLES : (c + 1) * ANGLES]
        b = piece[:, :128] + turned(piece[:, 128:], -2 * APART)
        both.append((b, turned(b, -APART)))

    def pair(i, j):
        return jnp.where(low, both[i][0], both[j][1]) + flip(jnp.where(low, both[j][0], both[i][1]))

    a, b = pair(0, 2), pair(1, 3)
    return jnp.where(first, a, pltpu.roll(b, 32, 1)), jnp.where(first, pltpu.roll(a, 96, 1), b)


def whole_kernel(
    peers, boxes, counts, places_in, turns_in, refs, weights_in, strength_in, out, evidence,
    alive, places, turns, weights, strength, xs, rs, own, cards, duo, ref_fans, box_fans, energies, base_refs, wide, mine_s, theirs_s, terms,
    post, masses, y_out, y_out_s, y_in, y_in_s, keep, near_out, near_out_s, near_in, near_in_s, z_out, z_out_s, z_in, z_in_s, pair_out, pair_in, scale, totals,
    small_local, box_local, ref_local, own_local, box_send, box_recv, ref_send, ref_recv, card_send, card_recv,
    duo_send, duo_recv, score_send, score_recv, mass_send, mass_recv, y_send, y_recv, ys_send, ys_recv,
    near_send, near_recv, z_send, z_recv, zs_send, zs_recv, pair_send, pair_recv,
):
    mine, core = lax.axis_index("particle"), lax.axis_index("classes")
    depth, owned, classes = peers // 2, boxes.shape[0], refs.shape[0]
    level, side = mine // 2, lax.rem(mine, 2)
    partner = {"classes": 1 - core}
    across = {"particle": level * 2 + 1 - side}
    others = [{"particle": lax.rem(mine + d, peers)} for d in range(1, peers)]
    near, far = level + 1 - 2 * lax.rem(level, 2), lax.rem(level + 2, depth)
    levels = [lax.rem(near + 2, depth), far, near, level]
    diagonal = [{"particle": there * 2 + side, "classes": 1 - core} for there in (far, near)]
    straight = [{"particle": there * 2 + side} for there in (far, near)]
    barrier = pltpu.get_barrier_semaphore()
    friends = [partner] + others + diagonal
    for device in friends:
        pl.semaphore_signal(barrier, inc=1, device_id=device, device_id_type=MESH)
    box_rows = pl.ds(pl.multiple_of(core * owned, owned), owned)
    ref_rows = pl.ds(pl.multiple_of(core * classes, classes), classes)
    local = []
    for p in range(peers):
        source = pl.ds(pl.multiple_of((2 * p + core) * STEP, 128), STEP)
        target = pl.ds(p * STEP, STEP)
        local.append(
            pltpu.make_async_copy(refs.at[:, source], rs.at[ref_rows, target], ref_local.at[p])
        )
        local.append(
            pltpu.make_async_copy(boxes.at[:, source], xs.at[box_rows, target], box_local.at[p])
        )
    width = 2 * STEP
    own_copy = pltpu.make_async_copy(
        refs.at[:, pl.ds(pl.multiple_of(mine * width, 128), width)], own, own_local.at[0]
    )
    small = [
        pltpu.make_async_copy(source, target, small_local.at[n])
        for n, (source, target) in enumerate(
            [
                (counts, alive), (places_in, places), (turns_in, turns), (weights_in, weights), (strength_in, strength),
            ]
        )
    ]
    for copy in small + local + [own_copy]:
        copy.start()
    for copy in small:
        copy.wait()
    card = jnp.zeros((8, 128), jnp.float32)
    cards[mine] = card
    slot = lax.broadcasted_iota(jnp.int32, (1, owned), 1)
    cards[mine, 0:1, :CYCLES] = weights[...]
    cards[mine, 1:2, :owned] = places[...].astype(jnp.float32)
    cards[mine, 2:3, :owned] = turns[...].astype(jnp.float32)
    cards[mine, 3:4, :owned] = jnp.where(slot < alive[...], 1.0, 0.0)
    cards[mine, 4:5, :classes] = strength[...]
    duo[core] = cards[mine]

    started = []

    def send(src, dst, sends, recvs, device):
        copy = pltpu.make_async_remote_copy(
            src_ref=src, dst_ref=dst, send_sem=sends, recv_sem=recvs, device_id=device,
            device_id_type=MESH,
        )
        copy.start()
        started.append(copy)
        return copy

    pl.semaphore_wait(barrier, len(friends))
    card_copies = [
        send(cards.at[mine], cards.at[mine], card_send.at[d], card_recv.at[d], device)
        for d, device in enumerate(others)
    ]
    duo_copy = send(duo.at[core], duo.at[core], duo_send.at[0], duo_recv.at[0], partner)
    ref_copies, box_copies = [], []
    for p in range(peers):
        source = pl.ds(pl.multiple_of((2 * p + 1 - core) * STEP, 128), STEP)
        target = pl.ds(p * STEP, STEP)
        ref_copies.append(
            send(refs.at[:, source], rs.at[ref_rows, target], ref_send.at[p], ref_recv.at[p], partner)
        )
    for p in range(peers):
        source = pl.ds(pl.multiple_of((2 * p + 1 - core) * STEP, 128), STEP)
        target = pl.ds(p * STEP, STEP)
        box_copies.append(
            send(boxes.at[:, source], xs.at[box_rows, target], box_send.at[p], box_recv.at[p], partner)
        )
    own_copy.wait()
    for h in range(2):
        for c in range(PARTS):
            base = (h * PARTS + c) * ANGLES
            base_refs[h, c * classes : (c + 1) * classes, :] = own[:, base : base + ANGLES].astype(
                jnp.float32
            )
    for copy in local:
        copy.wait()
    for p in range(peers):
        ref_copies[p].wait_recv()
        refs_fan(rs, ref_fans, energies, p)

    duo_copy.wait_recv()
    facts = duo[0] + flip(duo[1])
    facts = jnp.concatenate([facts] * (SLOTS // 8), axis=0).T
    place, turn, live = facts[:, 1:2], facts[:, 2:3], facts[:, 3:4]
    force = duo[0, 4:5, :] + pltpu.roll(duo[1, 4:5, :], classes, 1)
    force = force + flip(force)
    lane = lax.broadcasted_iota(jnp.int32, (SLOTS, 128), 1).astype(jnp.float32)
    swing = jnp.cos(TWO_PI * (lane - turn) / ROTATIONS)
    for copy in card_copies:
        copy.wait_recv()
    spread = jnp.zeros((SLOTS, 128), jnp.float32)
    for g in range(peers):
        spread = jnp.where(place == float(g), cards[g, 0:1, :], spread)
    wsum = jnp.sum(spread, axis=1, keepdims=True)
    spread = jnp.where(core == 0, spread, pltpu.roll(spread, 128 - PARTS, 1))
    base = jnp.zeros((SLOTS, 128), jnp.float32)
    for c in range(CYCLES // 2):
        place = c // PARTS * 2 * PARTS + c % PARTS
        factor = jnp.broadcast_to(spread[:, place : place + 1], (SLOTS, 128))
        wide[c] = factor
        base = base + factor * energies[c : c + 1, :]
    base = -0.5 * base
    for copy in box_copies:
        copy.wait_recv()

    low = low_lanes(SLOTS)
    score_copies, tops, norms = [], [], []

    def finish(f):
        score_copies[f].wait_recv()
        values = []
        for t in range(2):
            cols = slice(t * 128, (t + 1) * 128)
            r = f + 2 * t * TILES
            prior = jnp.where(low, swing[:, r : r + 1], swing[:, r + TILES : r + TILES + 1]) * force
            values.append(mine_s[f, :, cols] + theirs_s[f, :, cols] + prior)
        top = jnp.max(jnp.maximum(values[0], values[1]), axis=1, keepdims=True)
        values = [jnp.exp(v - top) for v in values]
        for t in range(2):
            terms[f, :, t * 128 : (t + 1) * 128] = values[t]
        tops.append(top)
        norms.append(jnp.sum(values[0] + values[1], axis=1, keepdims=True))

    for g in range(TILES // 2):
        for f, tile in enumerate(score_tiles(xs, ref_fans, wide, g, CYCLES // 2), 2 * g):
            mine_s[f] = tile + jnp.concatenate([base, base], axis=1)
        for f in (2 * g, 2 * g + 1):
            score_copies.append(
                send(mine_s.at[f], theirs_s.at[f], score_send.at[f], score_recv.at[f], partner)
            )
        if g > 0:
            finish(2 * g - 2)
            finish(2 * g - 1)
    for p in range(peers):
        boxes_fan(xs, box_fans, p)
    finish(TILES - 2)
    finish(TILES - 1)
    top = functools.reduce(jnp.maximum, tops)
    factors = [jnp.exp(t - top) for t in tops]
    norm = sum(n * s for n, s in zip(norms, factors))
    mass = jnp.zeros((8, 256), jnp.float32)
    for f in range(TILES):
        factor = jnp.where(live > 0.0, factors[f] / norm, 0.0)
        value = (terms[f] * factor).astype(jnp.bfloat16)
        post[f * SLOTS : (f + 1) * SLOTS, :] = value
        value = value.astype(jnp.float32)
        for i in range(SLOTS // 8):
            mass = mass + value[i * 8 : (i + 1) * 8]
    mass = mass[:, :128] + mass[:, 128:]
    mass = mass + flip(mass)
    masses[mine] = jnp.broadcast_to(jnp.sum(mass, axis=0, keepdims=True), (8, 128))
    mass_copies = [
        send(masses.at[mine], masses.at[mine], mass_send.at[d], mass_recv.at[d], device)
        for d, device in enumerate(others)
    ]
    proof = jnp.where(live > 0.0, (top + jnp.log(norm)) / (ANGLES * wsum), 0.0)
    proof = jnp.broadcast_to(proof, (SLOTS, 128)).T[0:1]
    evidence[...] = jnp.where(core == 0, proof, flip(proof))[:, :owned]

    y_copies, z_copies, near_copies, waited = [], [[], []], [], set()

    def away(i, blocks):
        for h, value in enumerate(blocks):
            encode(value, y_out.at[i, h], y_out_s.at[i, h : h + 1])
        y_copies.append(
            [send(y_out_s.at[i], y_in_s.at[i], ys_send.at[i], ys_recv.at[i], across)]
            + [
                send(y_out.at[i, h], y_in.at[i, h], y_send.at[i, n], y_recv.at[i, n], across)
                for n, h in enumerate([1 - core, core])
            ]
        )

    def home(i, blocks):
        for h, value in enumerate(blocks):
            keep[i, h] = value

    halves = [1 - core, core]

    def arrived(copies):
        for copy in copies:
            if id(copy) not in waited:
                copy.wait_recv()
                waited.add(id(copy))

    def summed(i, n):
        half = halves[n]
        arrived(y_copies[i][: n + 2])
        row = jnp.where(half == 0, y_in_s[i, 0:1, :], y_in_s[i, 1:2, :])
        codes = y_in[i, half].astype(jnp.int32).astype(jnp.float32)
        return keep[i, half] + codes * row

    def to_near(n):
        half = halves[n]
        encode(summed(0, n), near_out.at[half], near_out_s.at[half])
        near_copies.append(
            [
                send(
                    near_out_s.at[half], near_in_s.at[half], near_send.at[n, 1],
                    near_recv.at[n, 1], straight[1],
                ),
                send(
                    near_out.at[half], near_in.at[half], near_send.at[n, 0], near_recv.at[n, 0],
                    straight[1],
                ),
            ]
        )

    def to_owner(j, n):
        half = halves[n]
        total = summed(j + 1, n)
        if j == 0:
            arrived(near_copies[n])
            codes = near_in[half].astype(jnp.int32).astype(jnp.float32)
            total = total + codes * near_in_s[half, 0:1, :]
        encode(total, z_out.at[j, half], z_out_s.at[j, half])
        device = diagonal[j] if n == 0 else straight[j]
        z_copies[j].append(
            send(
                z_out_s.at[j, half], z_in_s.at[j, core], zs_send.at[j, n], zs_recv.at[j, n], device
            )
        )
        z_copies[j].append(
            send(z_out.at[j, half], z_in.at[j, core], z_send.at[j, n], z_recv.at[j, n], device)
        )

    shards = lambda i: (levels[i] * 2 + 1 - side, levels[i] * 2 + side)
    away(0, class_sums(box_fans, post, shards(0)[0]))
    for i in range(1, depth):
        held = class_sums(box_fans, post, shards(i - 1)[1])
        away(i, class_sums(box_fans, post, shards(i)[0]))
        home(i - 1, held)
        if i < depth - 1:
            to_near(i - 1)
    home(depth - 1, class_sums(box_fans, post, shards(depth - 1)[1]))
    for j in range(2):
        for n in range(2):
            to_owner(j, n)

    for copy in mass_copies:
        copy.wait_recv()
    weight = masses[0]
    for g in range(1, peers):
        weight = weight + masses[g]
    first = low_lanes(8, 32, 64)
    weight = jnp.where(
        core == 0,
        jnp.where(first, weight, pltpu.roll(weight, 32, 1)),
        jnp.where(first, pltpu.roll(weight, 96, 1), weight),
    )
    scale[...] = jnp.concatenate([weight] * 16, axis=0).T + 1.0

    def crossed(j, h):
        arrived(z_copies[j])
        return z_in[j, h].astype(jnp.int32).astype(jnp.float32) * z_in_s[j, h, 0:1, :]

    def store(half, value):
        result = (value.T + base_refs[half]) / scale[:, 0:1]
        for c in range(PARTS):
            out[:, half * PARTS + c, :] = result[c * classes : (c + 1) * classes]

    pair_out[...] = summed(depth - 1, 0)
    pair_copy = send(pair_out, pair_in, pair_send.at[0], pair_recv.at[0], partner)
    held = summed(depth - 1, 1)
    for h in range(2):
        totals[h] = crossed(1, h)
    pair_copy.wait_recv()
    for h in range(2):
        totals[h] = totals[h] + jnp.where(core == h, held, pair_in[...])
    for h in range(2):
        store(h, totals[h] + crossed(0, h))
    for copy in started:
        copy.wait_send()


def whole(boxes, counts, places, turns, refs, weights, strength, peers):
    given = (boxes, counts, places, turns, refs, weights, strength)
    classes, depth = refs.shape[0], peers // 2
    half = CYCLES * ANGLES // 2
    f32, bf16, i16 = jnp.float32, jnp.bfloat16, jnp.int16
    room = lambda dtype, *shape: pltpu.VMEM(shape, dtype)
    sems = lambda *shape: pltpu.SemaphoreType.DMA(shape)
    vmem = pl.BlockSpec(memory_space=pltpu.VMEM)
    hbm = pl.BlockSpec(memory_space=pltpu.HBM)
    return pl.pallas_call(
        functools.partial(whole_kernel, peers),
        in_specs=[hbm] * 7,
        out_specs=[vmem, vmem],
        out_shape=[
            jax.ShapeDtypeStruct((classes, CYCLES // peers, ANGLES), f32),
            jax.ShapeDtypeStruct((1, boxes.shape[0]), f32),
        ],
        scratch_shapes=[
            pltpu.VMEM(counts.shape, counts.dtype), pltpu.VMEM(places.shape, places.dtype),
            pltpu.VMEM(turns.shape, turns.dtype), pltpu.VMEM(weights.shape, f32),
            pltpu.VMEM(strength.shape, f32), room(bf16, SLOTS, half), room(bf16, 2 * classes, half), room(bf16, classes, 2 * STEP),
            room(f32, peers, 8, 128), room(f32, 2, 8, 128),
            room(bf16, 2, half, 128), room(bf16, 2, half, 128), room(f32, CYCLES // 2, 128),
            room(f32, 2, 128, ANGLES), room(f32, CYCLES // 2, SLOTS, 128),
            room(f32, TILES, SLOTS, 256), room(f32, TILES, SLOTS, 256), room(f32, TILES, SLOTS, 256),
            room(bf16, TILES * SLOTS, 256), room(f32, peers, 8, 128),
            room(i16, depth, 2, ANGLES, 128), room(f32, depth, 8, 128),
            room(i16, depth, 2, ANGLES, 128), room(f32, depth, 8, 128),
            room(f32, depth, 2, ANGLES, 128),
            room(i16, 2, ANGLES, 128), room(f32, 2, 8, 128), room(i16, 2, ANGLES, 128), room(f32, 2, 8, 128),
            room(i16, 2, 2, ANGLES, 128), room(f32, 2, 2, 8, 128),
            room(i16, 2, 2, ANGLES, 128), room(f32, 2, 2, 8, 128),
            room(f32, ANGLES, 128), room(f32, ANGLES, 128), room(f32, 128, 128), room(f32, 2, ANGLES, 128),
            sems(5), sems(peers), sems(peers), sems(1), sems(peers), sems(peers), sems(peers), sems(peers),
            sems(peers - 1), sems(peers - 1), sems(1), sems(1), sems(TILES), sems(TILES),
            sems(peers - 1), sems(peers - 1), sems(depth, 2), sems(depth, 2), sems(depth), sems(depth),
            sems(2, 2), sems(2, 2), sems(2, 2), sems(2, 2), sems(2, 2), sems(2, 2),
            sems(1), sems(1),
        ],
        compiler_params=pltpu.CompilerParams(
            collective_id=3, has_side_effects=True, vmem_limit_bytes=48 * 1024 * 1024
        ),
    )(*[pltpu.with_memory_space_constraint(x, pltpu.HBM) for x in given])


def on_device(boxes, counts, destinations, prior_rot, references, cycle_weights, prior_strength):
    peers = lax.axis_size("particle")
    cycle_index = lax.axis_index("particle")
    cycles_dev = CYCLES // peers
    width = cycles_dev * ANGLES
    if width == 2 * STEP:
        new_references, evidence = whole(
            boxes, jnp.broadcast_to(counts[None, :], (1, boxes.shape[0])), destinations[None, :], prior_rot[None, :], references,
            cycle_weights, prior_strength[None, :], peers,
        )
        return new_references, evidence[0]
    owned = boxes.shape[0]
    classes_dev = references.shape[0]
    lane_index = lax.axis_index("classes")
    row = jnp.concatenate([cycle_weights[0], prior_strength])
    row = jnp.pad(row, (0, 128 - row.shape[0]))[None, :]
    refs, rows = gathered(references, row, peers)
    refs = refs.reshape(2 * classes_dev, -1)
    group_wts = rows[:peers, 0, :CYCLES]
    other = rows[peers, 0, CYCLES : CYCLES + classes_dev]
    strength = jnp.where(
        lane_index == 0,
        jnp.concatenate([prior_strength, other]),
        jnp.concatenate([other, prior_strength]),
    ).reshape(1, -1)
    mine = destinations[:, None] == jnp.arange(peers, dtype=jnp.int32)[None, :]
    wts = jnp.sum(jnp.where(mine[:, :, None], group_wts[None], 0.0), axis=1)
    live = (jnp.arange(owned, dtype=jnp.int32) < counts[0]).astype(jnp.float32)
    turn_ids = jnp.arange(ROTATIONS, dtype=jnp.float32)
    gap = TWO_PI * (turn_ids[None, :] - prior_rot[:, None].astype(jnp.float32)) / ROTATIONS
    aux = jnp.concatenate([jnp.cos(gap), live[:, None], jnp.sum(wts, axis=1)[:, None]], axis=1)
    wts = jnp.transpose(wts.reshape(owned, STEPS, STEP_CYCLES), (1, 0, 2))
    post, mass, evidence = scores(
        boxes, refs, wts, aux, jnp.concatenate([strength, strength], axis=1)
    )
    if width % STEP == 0:
        new_references = fused_sums(boxes, post, mass, references, peers)
    else:
        sums = scattered(plain_sums(boxes, post, mass, classes_dev, peers))
        own_refs = lax.dynamic_slice_in_dim(references, cycle_index * width, width, 1)
        new_references = (sums[:, :width] + own_refs.astype(jnp.float32)) / (
            sums[:, width : width + 1] + 1.0
        )
    return new_references.reshape(classes_dev, cycles_dev, ANGLES), evidence[:, 0]


def solution(mesh):
    in_specs = (
        P(("groups", "particle", "classes"), None),
        P(("groups", "particle", "classes")),
        P(("groups", "particle", "classes")),
        P(("groups", "particle", "classes")),
        P(("groups", "classes"), None),
        P(("groups", "particle"), None),
        P(("groups", "classes")),
    )
    out_specs = (P(("groups", "classes"), "particle", None), P(("groups", "particle", "classes")))
    return jax.shard_map(
        on_device, mesh=mesh, in_specs=in_specs, out_specs=out_specs, check_vma=False
    )
```

```python
import functools
import math

import jax
import jax.numpy as jnp
from jax import lax
from jax.experimental import pallas as pl
from jax.experimental.pallas import tpu as pltpu
from jax.sharding import PartitionSpec as P

CYCLES = 64
ANGLES = 192
ROTATIONS = 24
FINE = 4
COARSE = ROTATIONS // FINE
SHIFT = ANGLES // ROTATIONS
STEP_CYCLES = 4
STEP = STEP_CYCLES * ANGLES
STEPS = CYCLES // STEP_CYCLES
TWO_PI = 2.0 * math.pi


def roll_rows(block, shift):
    shift = shift % ANGLES
    if shift == 0:
        return block
    pieces = []
    for c in range(STEP_CYCLES):
        base = c * ANGLES
        pieces.append(block[base + ANGLES - shift : base + ANGLES])
        pieces.append(block[base : base + ANGLES - shift])
    return jnp.concatenate(pieces, axis=0)


def fan_out(rows, sign):
    plain = jnp.concatenate([rows, rows], axis=0).T
    low = lax.broadcasted_iota(jnp.int32, plain.shape, 1) < rows.shape[0]
    tiles = [
        jnp.where(low, roll_rows(plain, sign * SHIFT * f), roll_rows(plain, sign * SHIFT * (f + 1)))
        for f in range(0, FINE, 2)
    ]
    return jnp.concatenate([t.astype(jnp.bfloat16) for t in tiles], axis=1), plain


def score_kernel(boxes_ref, refs_ref, wts_ref, aux_ref, str_ref, post, mass, ev_ref, acc, off):
    step = pl.program_id(0)
    owned = boxes_ref.shape[0]
    half = str_ref.shape[1]

    @pl.when(step == 0)
    def _():
        acc[...] = jnp.zeros_like(acc)
        off[...] = jnp.zeros_like(off)

    @pl.when(step >= 0)
    def _():
        wts = wts_ref[0]
        lane = lax.broadcasted_iota(jnp.int32, (owned, STEP), 1)
        spread = jnp.broadcast_to(wts[:, 0:1], (owned, STEP))
        for c in range(1, STEP_CYCLES):
            spread = jnp.where(lane >= c * ANGLES, wts[:, c : c + 1], spread)
        scaled = boxes_ref[...].astype(jnp.float32) * spread
        high = scaled.astype(jnp.bfloat16)
        rest = (scaled - high.astype(jnp.float32)).astype(jnp.bfloat16)
        lhs = jnp.concatenate([high, rest], axis=0)
        fan, plain = fan_out(refs_ref[...].astype(jnp.float32), 1)
        total = off[...]
        for c in range(STEP_CYCLES):
            piece = plain[c * ANGLES : (c + 1) * ANGLES]
            total = total + wts[:, c : c + 1] * jnp.sum(piece * piece, axis=0, keepdims=True)
        off[...] = total
        for q in range(COARSE):
            acc[q] += jnp.dot(
                lhs, roll_rows(fan, SHIFT * FINE * q), preferred_element_type=jnp.float32
            )

    @pl.when(step == STEPS - 1)
    def _():
        aux = aux_ref[...]
        live = aux[:, ROTATIONS : ROTATIONS + 1]
        wsum = aux[:, ROTATIONS + 1 : ROTATIONS + 2]
        low = lax.broadcasted_iota(jnp.int32, (owned, half), 1) < owned
        base = -0.5 * off[...]
        strength = str_ref[...]
        top = None
        for q in range(COARSE):
            for t in range(FINE // 2):
                r = q * FINE + 2 * t
                cols = slice(t * half, (t + 1) * half)
                turn = jnp.where(low, aux[:, r : r + 1], aux[:, r + 1 : r + 2])
                score = acc[q, :owned, cols] + acc[q, owned:, cols] + base + turn * strength
                acc[q, :owned, cols] = score
                top = score if top is None else jnp.maximum(top, score)
        top = jnp.max(top, axis=1, keepdims=True)
        norm = jnp.zeros((owned, half), jnp.float32)
        for q in range(COARSE):
            for t in range(FINE // 2):
                cols = slice(t * half, (t + 1) * half)
                term = jnp.exp(acc[q, :owned, cols] - top)
                acc[q, :owned, cols] = term
                norm = norm + term
        norm = jnp.sum(norm, axis=1, keepdims=True)
        ev_ref[...] = jnp.where(live > 0.0, (top + jnp.log(norm)) / (ANGLES * wsum), 0.0)
        seen = jnp.zeros((owned, half), jnp.float32)

        def weight(q, t):
            cols = slice(t * half, (t + 1) * half)
            value = jnp.where(live > 0.0, acc[q, :owned, cols] / norm, 0.0)
            return value.astype(jnp.bfloat16).astype(jnp.float32)

        for q in range(0, COARSE, 2):
            for t in range(FINE // 2):
                first, second = weight(q, t), weight(q + 1, t)
                seen = seen + first + second
                even = jnp.where(low, first, pltpu.roll(second, half // 2, 1))
                odd = jnp.where(low, pltpu.roll(first, half // 2, 1), second)
                cols = slice(q // 2 * half, (q // 2 + 1) * half)
                post[2 * t * owned : (2 * t + 1) * owned, cols] = even.astype(jnp.bfloat16)
                post[(2 * t + 1) * owned : (2 * t + 2) * owned, cols] = odd.astype(jnp.bfloat16)
        seen = jnp.sum(seen, axis=0, keepdims=True)
        mass[...] = seen + pltpu.roll(seen, half // 2, 1)


def turned_sums(boxes, post):
    half = 2 * boxes.shape[0]
    fan, _unused = fan_out(boxes.astype(jnp.float32), -1)
    sums = jnp.dot(fan, post, preferred_element_type=jnp.float32)
    both = sums[:, :half]
    for p in range(1, COARSE // 2):
        both = both + roll_rows(sums[:, p * half : (p + 1) * half], -2 * p * SHIFT * FINE)
    whole = both + pltpu.roll(roll_rows(both, -SHIFT * FINE), half // 2, 1)
    return whole.T


def plain_sums_kernel(width, boxes_ref, post_ref, mass_ref, out_ref):
    turned = turned_sums(boxes_ref[...], post_ref[...])
    classes = out_ref.shape[2]
    mass = jnp.broadcast_to(mass_ref[...], (128, 128)).T
    for h in range(2):
        rows = turned[h * classes : (h + 1) * classes]
        tail = mass[h * classes : (h + 1) * classes, : out_ref.shape[3] - width]
        for j in range(STEP // width):
            out_ref[j, h, :, :width] = rows[:, j * width : (j + 1) * width]
            out_ref[j, h, :, width:] = tail


def plain_sums(boxes, post, mass, classes, peers):
    width = CYCLES // peers * ANGLES
    padded = (width + 1 + 127) // 128 * 128
    return pl.pallas_call(
        functools.partial(plain_sums_kernel, width),
        grid=(STEPS,),
        in_specs=[
            pl.BlockSpec((boxes.shape[0], STEP), lambda i: (0, i)),
            pl.BlockSpec(post.shape, lambda i: (0, 0)),
            pl.BlockSpec(mass.shape, lambda i: (0, 0)),
        ],
        out_specs=pl.BlockSpec((STEP // width, 2, classes, padded), lambda i: (i, 0, 0, 0)),
        out_shape=jax.ShapeDtypeStruct((peers, 2, classes, padded), jnp.float32),
    )(boxes, post, mass)


def scores(boxes, refs, wts, aux, strength):
    owned, classes, half = boxes.shape[0], refs.shape[0], strength.shape[1]
    whole = lambda shape: pl.BlockSpec(shape, lambda i: (0, 0))
    post = (FINE * owned, COARSE * classes)
    return pl.pallas_call(
        score_kernel,
        grid=(STEPS,),
        in_specs=[
            pl.BlockSpec((owned, STEP), lambda i: (0, i)),
            pl.BlockSpec((classes, STEP), lambda i: (0, i)),
            pl.BlockSpec((1, owned, STEP_CYCLES), lambda i: (i, 0, 0)),
            whole(aux.shape),
            whole((1, half)),
        ],
        out_specs=[whole(post), whole((1, half)), whole((owned, 1))],
        out_shape=[
            jax.ShapeDtypeStruct(post, jnp.bfloat16),
            jax.ShapeDtypeStruct((1, half), jnp.float32),
            jax.ShapeDtypeStruct((owned, 1), jnp.float32),
        ],
        scratch_shapes=[
            pltpu.VMEM((COARSE, 2 * owned, FINE * classes), jnp.float32),
            pltpu.VMEM((owned, half), jnp.float32),
        ],
        compiler_params=pltpu.CompilerParams(
            dimension_semantics=("arbitrary",), vmem_limit_bytes=40 * 1024 * 1024
        ),
    )(boxes, refs, wts, aux, strength)


MESH = pl.DeviceIdType.MESH
CHUNKS = 4


def greet(devices):
    barrier = pltpu.get_barrier_semaphore()
    for device in devices:
        pl.semaphore_signal(barrier, inc=1, device_id=device, device_id_type=MESH)
    pl.semaphore_wait(barrier, len(devices))


def gather_kernel(peers, refs_ref, row_ref, all_refs, all_rows, local, send, recv):
    mine, core = lax.axis_index("particle"), lax.axis_index("classes")
    partner = {"classes": 1 - core}
    others = [{"particle": lax.rem(mine + d, peers)} for d in range(1, peers)]
    greet([partner] + others)
    copies = [
        pltpu.make_async_remote_copy(
            src_ref=refs_ref, dst_ref=all_refs.at[core], send_sem=send.at[0], recv_sem=recv.at[0],
            device_id=partner, device_id_type=MESH,
        ),
        pltpu.make_async_remote_copy(
            src_ref=row_ref, dst_ref=all_rows.at[peers], send_sem=send.at[1], recv_sem=recv.at[1],
            device_id=partner, device_id_type=MESH,
        ),
    ]
    for d, other in enumerate(others):
        copies.append(
            pltpu.make_async_remote_copy(
                src_ref=row_ref, dst_ref=all_rows.at[mine], send_sem=send.at[2 + d],
                recv_sem=recv.at[2 + d], device_id=other, device_id_type=MESH,
            )
        )
    for copy in copies:
        copy.start()
    own = [
        pltpu.make_async_copy(refs_ref, all_refs.at[core], local.at[0]),
        pltpu.make_async_copy(row_ref, all_rows.at[mine], local.at[1]),
    ]
    for copy in own:
        copy.start()
    for copy in own + copies:
        copy.wait()


def gathered(refs, row, peers):
    return pl.pallas_call(
        functools.partial(gather_kernel, peers),
        in_specs=[pl.BlockSpec(memory_space=pltpu.VMEM)] * 2,
        out_specs=[pl.BlockSpec(memory_space=pltpu.VMEM)] * 2,
        out_shape=[
            jax.ShapeDtypeStruct((2,) + refs.shape, refs.dtype),
            jax.ShapeDtypeStruct((peers + 1,) + row.shape, row.dtype),
        ],
        scratch_shapes=[
            pltpu.SemaphoreType.DMA((2,)),
            pltpu.SemaphoreType.DMA((peers + 1,)),
            pltpu.SemaphoreType.DMA((peers + 1,)),
        ],
        compiler_params=pltpu.CompilerParams(collective_id=0, has_side_effects=True),
    )(refs, row)


def scatter_kernel(depth, parts, out, pair_in, side_out, side_in, line_out, line_in,
                   pair_send, pair_recv, side_send, side_recv, line_send, line_recv):
    mine, core = lax.axis_index("particle"), lax.axis_index("classes")
    level, side = mine // 2, lax.rem(mine, 2)
    partner = {"classes": 1 - core}
    across = {"particle": level * 2 + 1 - side}
    levels = [lax.rem(level + d, depth) for d in range(1, depth)]
    line = [{"particle": other * 2 + side} for other in levels]
    greet([partner, across] + line)
    rows = out.shape[0] // CHUNKS
    pair, cross, lines = [], [], []
    for j in range(CHUNKS):
        copy = pltpu.make_async_remote_copy(
            src_ref=parts.at[:, :, 1 - core, j * rows : (j + 1) * rows], dst_ref=pair_in.at[j],
            send_sem=pair_send.at[j], recv_sem=pair_recv.at[j], device_id=partner,
            device_id_type=MESH,
        )
        copy.start()
        pair.append(copy)
    for j in range(CHUNKS):
        span = slice(j * rows, (j + 1) * rows)
        pair[j].wait_recv()
        side_out[j] = parts[:, 1 - side, core, span] + pair_in[j, :, 1 - side]
        copy = pltpu.make_async_remote_copy(
            src_ref=side_out.at[j], dst_ref=side_in.at[j], send_sem=side_send.at[j],
            recv_sem=side_recv.at[j], device_id=across, device_id_type=MESH,
        )
        copy.start()
        cross.append(copy)
        line_out[j] = parts[:, side, core, span] + pair_in[j, :, side]
    for j in range(CHUNKS):
        cross[j].wait_recv()
        line_out[j] = line_out[j] + side_in[j]
        for d in range(depth - 1):
            copy = pltpu.make_async_remote_copy(
                src_ref=line_out.at[j, levels[d]], dst_ref=line_in.at[j, d],
                send_sem=line_send.at[j, d], recv_sem=line_recv.at[j, d], device_id=line[d],
                device_id_type=MESH,
            )
            copy.start()
            lines.append(copy)
    for j in range(CHUNKS):
        total = line_out[j, level]
        for d in range(depth - 1):
            lines[j * (depth - 1) + d].wait_recv()
            total = total + line_in[j, d]
        out[j * rows : (j + 1) * rows] = total
    for copy in pair + cross + lines:
        copy.wait_send()


def scattered(parts):
    peers, _, classes, width = parts.shape
    depth = peers // 2
    rows = classes // CHUNKS
    sems = pltpu.SemaphoreType.DMA((CHUNKS,))
    line_sems = pltpu.SemaphoreType.DMA((CHUNKS, max(depth - 1, 1)))
    return pl.pallas_call(
        functools.partial(scatter_kernel, depth),
        in_specs=[pl.BlockSpec(memory_space=pltpu.VMEM)],
        out_specs=pl.BlockSpec(memory_space=pltpu.VMEM),
        out_shape=jax.ShapeDtypeStruct((classes, width), jnp.float32),
        scratch_shapes=[
            pltpu.VMEM((CHUNKS, depth, 2, rows, width), jnp.float32),
            pltpu.VMEM((CHUNKS, depth, rows, width), jnp.float32),
            pltpu.VMEM((CHUNKS, depth, rows, width), jnp.float32),
            pltpu.VMEM((CHUNKS, depth, rows, width), jnp.float32),
            pltpu.VMEM((CHUNKS, max(depth - 1, 1), rows, width), jnp.float32),
            sems, sems, sems, sems, line_sems, line_sems,
        ],
        compiler_params=pltpu.CompilerParams(
            collective_id=1, has_side_effects=True, vmem_limit_bytes=48 * 1024 * 1024
        ),
    )(parts.reshape(depth, 2, 2, classes, width))


def sums_kernel(peers, boxes, post, mass, refs, out, pair_out, pair_in, keep, side_out, side_in,
                line_in, mass_in, column, pair_send, pair_recv, side_send, side_recv, line_send,
                line_recv, mass_send, mass_recv):
    mine, core = lax.axis_index("particle"), lax.axis_index("classes")
    depth, width, classes = peers // 2, out.shape[1], out.shape[0]
    level, side = mine // 2, lax.rem(mine, 2)
    place = mine * 2 + core
    partner = {"classes": 1 - core}
    across = {"particle": level * 2 + 1 - side}
    everyone = []
    for e in range(1, 2 * peers):
        there = lax.rem(place + e, 2 * peers)
        everyone.append({"particle": there // 2, "classes": lax.rem(there, 2)})
    greet(everyone)
    started, masses = [], []

    def send(src, dst, sends, recvs, device):
        copy = pltpu.make_async_remote_copy(
            src_ref=src, dst_ref=dst, send_sem=sends, recv_sem=recvs, device_id=device,
            device_id_type=MESH,
        )
        copy.start()
        started.append(copy)
        return copy

    for e, device in enumerate(everyone):
        masses.append(
            send(mass, mass_in.at[e], mass_send.at[e], mass_recv.at[e], device)
        )
    turns = list(range(1, depth)) + [0]
    blocks = [(i, d, True) for i, d in enumerate(turns)] + [(i, d, False) for i, d in enumerate(turns)]
    pair, cross, lines = [], [], []

    def advance(n):
        i, d, away = blocks[n]
        pair[n].wait_recv()
        if away:
            side_out[i] = keep[n] + pair_in[n]
            cross.append(
                send(side_out.at[i], side_in.at[i], side_send.at[i], side_recv.at[i], across)
            )
            return
        cross[i].wait_recv()
        keep[n] = keep[n] + pair_in[n] + side_in[i]
        if d > 0:
            there = {"particle": lax.rem(level + d, depth) * 2 + side}
            lines.append(
                send(keep.at[n], line_in.at[i], line_send.at[i], line_recv.at[i], there)
            )

    for n, (i, d, away) in enumerate(blocks):
        shard = lax.rem(level + d, depth) * 2 + (1 - side if away else side)

        @pl.loop(0, width // STEP)
        def _(part):
            source = pl.multiple_of(shard * width + part * STEP, 128)
            target = pl.multiple_of(part * STEP, 128)
            turned = turned_sums(boxes[:, pl.ds(source, STEP)], post[...])
            low, high = turned[:classes], turned[classes : 2 * classes]
            keep[n, :, pl.ds(target, STEP)] = jnp.where(core == 0, low, high)
            pair_out[n, :, pl.ds(target, STEP)] = jnp.where(core == 0, high, low)

        pair.append(send(pair_out.at[n], pair_in.at[n], pair_send.at[n], pair_recv.at[n], partner))
        if n > 0:
            advance(n - 1)
    advance(len(blocks) - 1)
    weight = mass[...]
    for e, copy in enumerate(masses):
        copy.wait_recv()
        weight = weight + mass_in[e]
    column[...] = jnp.broadcast_to(weight, column.shape).T
    scale = column[pl.ds(pl.multiple_of(core * classes, 8), classes), :]
    total = keep[len(blocks) - 1]
    for i in range(depth - 1):
        lines[i].wait_recv()
        total = total + line_in[i]
    base = refs[:, pl.ds(pl.multiple_of(mine * width, 128), width)].astype(jnp.float32)
    out[...] = (total + base) / (scale[:, 0:1] + 1.0)
    for copy in started:
        copy.wait_send()


def fused_sums(boxes, post, mass, refs, peers):
    classes, width, depth = refs.shape[0], CYCLES // peers * ANGLES, peers // 2
    room = lambda count: pltpu.VMEM((count, classes, width), jnp.float32)
    sems = lambda count: pltpu.SemaphoreType.DMA((count,))
    others = 2 * peers - 1
    return pl.pallas_call(
        functools.partial(sums_kernel, peers),
        in_specs=[pl.BlockSpec(memory_space=pltpu.VMEM)] * 4,
        out_specs=pl.BlockSpec(memory_space=pltpu.VMEM),
        out_shape=jax.ShapeDtypeStruct((classes, width), jnp.float32),
        scratch_shapes=[
            room(peers), room(peers), room(peers), room(depth), room(depth), room(depth - 1),
            pltpu.VMEM((others,) + mass.shape, jnp.float32),
            pltpu.VMEM((mass.shape[1], mass.shape[1]), jnp.float32),
            sems(peers), sems(peers), sems(depth), sems(depth), sems(depth - 1), sems(depth - 1),
            sems(others), sems(others),
        ],
        compiler_params=pltpu.CompilerParams(
            collective_id=2, has_side_effects=True, vmem_limit_bytes=48 * 1024 * 1024
        ),
    )(boxes, post, mass, refs)


PARTS = 4
QUARTERS = 4
TILES = 6
APART = ANGLES // QUARTERS
SLOTS = 128
LEVELS = 32767.0


def turned(block, shift):
    shift = shift % ANGLES
    if shift == 0:
        return block
    return jnp.concatenate([block[ANGLES - shift :], block[: ANGLES - shift]], axis=0)


def flip(block):
    return pltpu.roll(block, 64, 1)


def low_lanes(rows, width=64, period=128):
    lane = lax.broadcasted_iota(jnp.int32, (rows, 128), 1)
    return lax.rem(lane, period) < width


def encode(block, codes, scales):
    largest = jnp.maximum(jnp.max(jnp.abs(block), axis=0, keepdims=True), 1e-30)
    codes[...] = jnp.round(block * (LEVELS / largest)).astype(jnp.int32).astype(jnp.int16)
    scales[0:1, :] = largest * (1.0 / LEVELS)


def refs_fan(refs, fans, energies, p):
    cols = slice(p * STEP, (p + 1) * STEP)
    rows = refs[:, cols].astype(jnp.float32)
    plain = jnp.concatenate([rows, rows], axis=0).T
    low = low_lanes(ANGLES)
    for c in range(PARTS):
        base = p * STEP + c * ANGLES
        piece = plain[c * ANGLES : (c + 1) * ANGLES]
        energies[p * PARTS + c : p * PARTS + c + 1, :] = jnp.sum(piece * piece, axis=0, keepdims=True)
        both = jnp.where(low, piece, turned(piece, APART))
        fans[0, base : base + ANGLES, :] = both.astype(jnp.bfloat16)
        fans[1, base : base + ANGLES, :] = turned(both, SHIFT).astype(jnp.bfloat16)


def boxes_fan(boxes, fans, p):
    cols = slice(p * STEP, (p + 1) * STEP)
    plain = boxes[:, cols].astype(jnp.float32).T
    fans[0, cols, :] = plain.astype(jnp.bfloat16)
    for c in range(PARTS):
        base = p * STEP + c * ANGLES
        piece = plain[c * ANGLES : (c + 1) * ANGLES]
        fans[1, base : base + ANGLES, :] = turned(piece, -SHIFT).astype(jnp.bfloat16)


def score_tiles(boxes, fans, wide, g, cycles):
    totals = [None, None]
    blank = jnp.zeros((256 - ANGLES, 256), jnp.bfloat16)
    for c in range(cycles):
        base, window = c * ANGLES, c // 2 * 2 * ANGLES + c % 2 * 128
        factor = wide[c]
        factor = jnp.concatenate([factor, factor], axis=1)
        for parity in range(2):
            piece = fans[parity, base : base + ANGLES, :]
            shift = 2 * SHIFT * g
            piece = jnp.concatenate(
                [turned(piece, shift), turned(piece, shift + 2 * APART)], axis=1
            )
            piece = jnp.concatenate([piece, blank] if c % 2 == 0 else [blank, piece], axis=0)
            part = factor * jnp.dot(
                boxes[:, window : window + 256], piece, preferred_element_type=jnp.float32
            )
            totals[parity] = part if totals[parity] is None else totals[parity] + part
    return totals


def class_sums(fans, post, shard):
    rows = []
    for c in range(PARTS):
        base = pl.multiple_of(shard * STEP + c * ANGLES, 64)
        even = fans[0, pl.ds(base, ANGLES), :]
        odd = fans[1, pl.ds(base, ANGLES), :]
        rows.append(
            jnp.concatenate(
                [turned(x, -2 * SHIFT * s) for s in range(TILES // 2) for x in (even, odd)], axis=1
            )
        )
    sums = jnp.dot(jnp.concatenate(rows, axis=0), post[...], preferred_element_type=jnp.float32)
    low, first = low_lanes(ANGLES), low_lanes(ANGLES, 32, 64)
    both = []
    for c in range(PARTS):
        piece = sums[c * ANGLES : (c + 1) * ANGLES]
        b = piece[:, :128] + turned(piece[:, 128:], -2 * APART)
        both.append((b, turned(b, -APART)))

    def pair(i, j):
        return jnp.where(low, both[i][0], both[j][1]) + flip(jnp.where(low, both[j][0], both[i][1]))

    a, b = pair(0, 2), pair(1, 3)
    return jnp.where(first, a, pltpu.roll(b, 32, 1)), jnp.where(first, pltpu.roll(a, 96, 1), b)


def whole_kernel(
    peers, boxes, counts, places_in, turns_in, refs, weights_in, strength_in, out, evidence,
    alive, places, turns, weights, strength, xs, rs, own, cards, duo, ref_fans, box_fans, energies, base_refs, wide, mine_s, theirs_s, terms,
    post, masses, y_out, y_out_s, y_in, y_in_s, keep, near_out, near_out_s, near_in, near_in_s, z_out, z_out_s, z_in, z_in_s, pair_out, pair_in, scale, totals,
    small_local, box_local, ref_local, own_local, box_send, box_recv, ref_send, ref_recv, card_send, card_recv,
    duo_send, duo_recv, score_send, score_recv, mass_send, mass_recv, y_send, y_recv, ys_send, ys_recv,
    near_send, near_recv, z_send, z_recv, zs_send, zs_recv, pair_send, pair_recv,
):
    mine, core = lax.axis_index("particle"), lax.axis_index("classes")
    depth, owned, classes = peers // 2, boxes.shape[0], refs.shape[0]
    level, side = mine // 2, lax.rem(mine, 2)
    partner = {"classes": 1 - core}
    across = {"particle": level * 2 + 1 - side}
    others = [{"particle": lax.rem(mine + d, peers)} for d in range(1, peers)]
    near, far = level + 1 - 2 * lax.rem(level, 2), lax.rem(level + 2, depth)
    levels = [lax.rem(near + 2, depth), far, near, level]
    diagonal = [{"particle": there * 2 + side, "classes": 1 - core} for there in (far, near)]
    straight = [{"particle": there * 2 + side} for there in (far, near)]
    barrier = pltpu.get_barrier_semaphore()
    friends = [partner] + others + diagonal
    for device in friends:
        pl.semaphore_signal(barrier, inc=1, device_id=device, device_id_type=MESH)
    box_rows = pl.ds(pl.multiple_of(core * owned, owned), owned)
    ref_rows = pl.ds(pl.multiple_of(core * classes, classes), classes)
    local = []
    for p in range(peers):
        source = pl.ds(pl.multiple_of((2 * p + core) * STEP, 128), STEP)
        target = pl.ds(p * STEP, STEP)
        local.append(
            pltpu.make_async_copy(refs.at[:, source], rs.at[ref_rows, target], ref_local.at[p])
        )
        local.append(
            pltpu.make_async_copy(boxes.at[:, source], xs.at[box_rows, target], box_local.at[p])
        )
    width = 2 * STEP
    own_copy = pltpu.make_async_copy(
        refs.at[:, pl.ds(pl.multiple_of(mine * width, 128), width)], own, own_local.at[0]
    )
    small = [
        pltpu.make_async_copy(source, target, small_local.at[n])
        for n, (source, target) in enumerate(
            [
                (counts, alive), (places_in, places), (turns_in, turns), (weights_in, weights), (strength_in, strength),
            ]
        )
    ]
    for copy in small + local + [own_copy]:
        copy.start()
    for copy in small:
        copy.wait()
    card = jnp.zeros((8, 128), jnp.float32)
    cards[mine] = card
    slot = lax.broadcasted_iota(jnp.int32, (1, owned), 1)
    cards[mine, 0:1, :CYCLES] = weights[...]
    cards[mine, 1:2, :owned] = places[...].astype(jnp.float32)
    cards[mine, 2:3, :owned] = turns[...].astype(jnp.float32)
    cards[mine, 3:4, :owned] = jnp.where(slot < alive[...], 1.0, 0.0)
    cards[mine, 4:5, :classes] = strength[...]
    duo[core] = cards[mine]

    started = []

    def send(src, dst, sends, recvs, device):
        copy = pltpu.make_async_remote_copy(
            src_ref=src, dst_ref=dst, send_sem=sends, recv_sem=recvs, device_id=device,
            device_id_type=MESH,
        )
        copy.start()
        started.append(copy)
        return copy

    pl.semaphore_wait(barrier, len(friends))
    card_copies = [
        send(cards.at[mine, 0:1], cards.at[mine, 0:1], card_send.at[d], card_recv.at[d], device)
        for d, device in enumerate(others)
    ]
    duo_copy = send(duo.at[core], duo.at[core], duo_send.at[0], duo_recv.at[0], partner)
    ref_copies, box_copies = [], []
    for p in range(peers):
        source = pl.ds(pl.multiple_of((2 * p + 1 - core) * STEP, 128), STEP)
        target = pl.ds(p * STEP, STEP)
        ref_copies.append(
            send(refs.at[:, source], rs.at[ref_rows, target], ref_send.at[p], ref_recv.at[p], partner)
        )
    for p in range(peers):
        source = pl.ds(pl.multiple_of((2 * p + 1 - core) * STEP, 128), STEP)
        target = pl.ds(p * STEP, STEP)
        box_copies.append(
            send(boxes.at[:, source], xs.at[box_rows, target], box_send.at[p], box_recv.at[p], partner)
        )
    own_copy.wait()
    for h in range(2):
        for c in range(PARTS):
            base = (h * PARTS + c) * ANGLES
            base_refs[h, c * classes : (c + 1) * classes, :] = own[:, base : base + ANGLES].astype(
                jnp.float32
            )
    for copy in local:
        copy.wait()
    for p in range(peers):
        ref_copies[p].wait_recv()
        refs_fan(rs, ref_fans, energies, p)

    duo_copy.wait_recv()
    facts = duo[0] + flip(duo[1])
    facts = jnp.concatenate([facts] * (SLOTS // 8), axis=0).T
    place, turn, live = facts[:, 1:2], facts[:, 2:3], facts[:, 3:4]
    force = duo[0, 4:5, :] + pltpu.roll(duo[1, 4:5, :], classes, 1)
    force = force + flip(force)
    lane = lax.broadcasted_iota(jnp.int32, (SLOTS, 128), 1).astype(jnp.float32)
    swing = jnp.cos(TWO_PI * (lane - turn) / ROTATIONS)
    for copy in card_copies:
        copy.wait_recv()
    spread = jnp.zeros((SLOTS, 128), jnp.float32)
    for g in range(peers):
        spread = jnp.where(place == float(g), cards[g, 0:1, :], spread)
    wsum = jnp.sum(spread, axis=1, keepdims=True)
    spread = jnp.where(core == 0, spread, pltpu.roll(spread, 128 - PARTS, 1))
    base = jnp.zeros((SLOTS, 128), jnp.float32)
    for c in range(CYCLES // 2):
        place = c // PARTS * 2 * PARTS + c % PARTS
        factor = jnp.broadcast_to(spread[:, place : place + 1], (SLOTS, 128))
        wide[c] = factor
        base = base + factor * energies[c : c + 1, :]
    base = -0.5 * base
    for copy in box_copies:
        copy.wait_recv()

    low = low_lanes(SLOTS)
    score_copies, tops, norms = [], [], []

    def finish(f):
        score_copies[f].wait_recv()
        values = []
        for t in range(2):
            cols = slice(t * 128, (t + 1) * 128)
            r = f + 2 * t * TILES
            prior = jnp.where(low, swing[:, r : r + 1], swing[:, r + TILES : r + TILES + 1]) * force
            values.append(mine_s[f, :, cols] + theirs_s[f, :, cols] + prior)
        top = jnp.max(jnp.maximum(values[0], values[1]), axis=1, keepdims=True)
        values = [jnp.exp(v - top) for v in values]
        for t in range(2):
            terms[f, :, t * 128 : (t + 1) * 128] = values[t]
        tops.append(top)
        norms.append(jnp.sum(values[0] + values[1], axis=1, keepdims=True))

    for g in range(TILES // 2):
        for f, tile in enumerate(score_tiles(xs, ref_fans, wide, g, CYCLES // 2), 2 * g):
            mine_s[f] = tile + jnp.concatenate([base, base], axis=1)
        for f in (2 * g, 2 * g + 1):
            score_copies.append(
                send(mine_s.at[f], theirs_s.at[f], score_send.at[f], score_recv.at[f], partner)
            )
        if g > 0:
            finish(2 * g - 2)
            finish(2 * g - 1)
    for p in range(peers):
        boxes_fan(xs, box_fans, p)
    finish(TILES - 2)
    finish(TILES - 1)
    top = functools.reduce(jnp.maximum, tops)
    factors = [jnp.exp(t - top) for t in tops]
    norm = sum(n * s for n, s in zip(norms, factors))
    for f in range(TILES):
        factor = jnp.where(live > 0.0, factors[f] / norm, 0.0)
        post[f * SLOTS : (f + 1) * SLOTS, :] = (terms[f] * factor).astype(jnp.bfloat16)

    def mass_and_evidence():
        mass = jnp.zeros((8, 256), jnp.float32)
        for f in range(TILES):
            value = post[f * SLOTS : (f + 1) * SLOTS, :].astype(jnp.float32)
            for i in range(SLOTS // 8):
                mass = mass + value[i * 8 : (i + 1) * 8]
        mass = mass[:, :128] + mass[:, 128:]
        mass = mass + flip(mass)
        masses[mine] = jnp.broadcast_to(jnp.sum(mass, axis=0, keepdims=True), (8, 128))
        for d, device in enumerate(others):
            mass_copies.append(
                send(
                    masses.at[mine, 0:1], masses.at[mine, 0:1], mass_send.at[d], mass_recv.at[d],
                    device,
                )
            )
        proof = jnp.where(live > 0.0, (top + jnp.log(norm)) / (ANGLES * wsum), 0.0)
        proof = jnp.broadcast_to(proof, (SLOTS, 128)).T[0:1]
        evidence[...] = jnp.where(core == 0, proof, flip(proof))[:, :owned]

    mass_copies = []
    y_copies, z_copies, near_copies, waited = [], [[], []], [], set()

    def away(i, blocks):
        for h, value in enumerate(blocks):
            encode(value, y_out.at[i, h], y_out_s.at[i, h : h + 1])
        y_copies.append(
            [send(y_out_s.at[i, 0:2], y_in_s.at[i, 0:2], ys_send.at[i], ys_recv.at[i], across)]
            + [
                send(y_out.at[i, h], y_in.at[i, h], y_send.at[i, n], y_recv.at[i, n], across)
                for n, h in enumerate([1 - core, core])
            ]
        )

    def home(i, blocks):
        for h, value in enumerate(blocks):
            keep[i, h] = value

    halves = [1 - core, core]

    def arrived(copies):
        for copy in copies:
            if id(copy) not in waited:
                copy.wait_recv()
                waited.add(id(copy))

    def summed(i, n):
        half = halves[n]
        arrived(y_copies[i][: n + 2])
        row = jnp.where(half == 0, y_in_s[i, 0:1, :], y_in_s[i, 1:2, :])
        codes = y_in[i, half].astype(jnp.int32).astype(jnp.float32)
        return keep[i, half] + codes * row

    def to_near(n):
        half = halves[n]
        encode(summed(0, n), near_out.at[half], near_out_s.at[half])
        near_copies.append(
            [
                send(
                    near_out_s.at[half, 0:1], near_in_s.at[half, 0:1], near_send.at[n, 1],
                    near_recv.at[n, 1], straight[1],
                ),
                send(
                    near_out.at[half], near_in.at[half], near_send.at[n, 0], near_recv.at[n, 0],
                    straight[1],
                ),
            ]
        )

    def to_owner(j, n):
        half = halves[n]
        total = summed(j + 1, n)
        if j == 0:
            arrived(near_copies[n])
            codes = near_in[half].astype(jnp.int32).astype(jnp.float32)
            total = total + codes * near_in_s[half, 0:1, :]
        encode(total, z_out.at[j, half], z_out_s.at[j, half])
        device = diagonal[j] if n == 0 else straight[j]
        z_copies[j].append(
            send(
                z_out_s.at[j, half, 0:1], z_in_s.at[j, core, 0:1], zs_send.at[j, n],
                zs_recv.at[j, n], device,
            )
        )
        z_copies[j].append(
            send(z_out.at[j, half], z_in.at[j, core], z_send.at[j, n], z_recv.at[j, n], device)
        )

    shards = lambda i: (levels[i] * 2 + 1 - side, levels[i] * 2 + side)
    away(0, class_sums(box_fans, post, shards(0)[0]))
    for i in range(1, depth):
        held = class_sums(box_fans, post, shards(i - 1)[1])
        away(i, class_sums(box_fans, post, shards(i)[0]))
        home(i - 1, held)
        if i == 1:
            mass_and_evidence()
        if i < depth - 1:
            to_near(i - 1)
    home(depth - 1, class_sums(box_fans, post, shards(depth - 1)[1]))
    for j in range(2):
        for n in range(2):
            to_owner(j, n)

    for copy in mass_copies:
        copy.wait_recv()
    weight = masses[0, 0:1, :]
    for g in range(1, peers):
        weight = weight + masses[g, 0:1, :]
    weight = jnp.broadcast_to(weight, (8, 128))
    first = low_lanes(8, 32, 64)
    weight = jnp.where(
        core == 0,
        jnp.where(first, weight, pltpu.roll(weight, 32, 1)),
        jnp.where(first, pltpu.roll(weight, 96, 1), weight),
    )
    scale[...] = jnp.concatenate([weight] * 16, axis=0).T + 1.0

    def crossed(j, h):
        arrived(z_copies[j])
        return z_in[j, h].astype(jnp.int32).astype(jnp.float32) * z_in_s[j, h, 0:1, :]

    def store(half, value):
        result = (value.T + base_refs[half]) / scale[:, 0:1]
        for c in range(PARTS):
            out[:, half * PARTS + c, :] = result[c * classes : (c + 1) * classes]

    pair_out[...] = summed(depth - 1, 0)
    pair_copy = send(pair_out, pair_in, pair_send.at[0], pair_recv.at[0], partner)
    held = summed(depth - 1, 1)
    for h in range(2):
        totals[h] = crossed(1, h)
    pair_copy.wait_recv()
    for h in range(2):
        totals[h] = totals[h] + jnp.where(core == h, held, pair_in[...])
    for h in range(2):
        store(h, totals[h] + crossed(0, h))
    for copy in started:
        copy.wait_send()


def whole(boxes, counts, places, turns, refs, weights, strength, peers):
    given = (boxes, counts, places, turns, refs, weights, strength)
    classes, depth = refs.shape[0], peers // 2
    half = CYCLES * ANGLES // 2
    f32, bf16, i16 = jnp.float32, jnp.bfloat16, jnp.int16
    room = lambda dtype, *shape: pltpu.VMEM(shape, dtype)
    sems = lambda *shape: pltpu.SemaphoreType.DMA(shape)
    vmem = pl.BlockSpec(memory_space=pltpu.VMEM)
    hbm = pl.BlockSpec(memory_space=pltpu.HBM)
    return pl.pallas_call(
        functools.partial(whole_kernel, peers),
        in_specs=[hbm] * 7,
        out_specs=[vmem, vmem],
        out_shape=[
            jax.ShapeDtypeStruct((classes, CYCLES // peers, ANGLES), f32),
            jax.ShapeDtypeStruct((1, boxes.shape[0]), f32),
        ],
        scratch_shapes=[
            pltpu.VMEM(counts.shape, counts.dtype), pltpu.VMEM(places.shape, places.dtype),
            pltpu.VMEM(turns.shape, turns.dtype), pltpu.VMEM(weights.shape, f32),
            pltpu.VMEM(strength.shape, f32), room(bf16, SLOTS, half), room(bf16, 2 * classes, half), room(bf16, classes, 2 * STEP),
            room(f32, peers, 8, 128), room(f32, 2, 8, 128),
            room(bf16, 2, half, 128), room(bf16, 2, half, 128), room(f32, CYCLES // 2, 128),
            room(f32, 2, 128, ANGLES), room(f32, CYCLES // 2, SLOTS, 128),
            room(f32, TILES, SLOTS, 256), room(f32, TILES, SLOTS, 256), room(f32, TILES, SLOTS, 256),
            room(bf16, TILES * SLOTS, 256), room(f32, peers, 8, 128),
            room(i16, depth, 2, ANGLES, 128), room(f32, depth, 8, 128),
            room(i16, depth, 2, ANGLES, 128), room(f32, depth, 8, 128),
            room(f32, depth, 2, ANGLES, 128),
            room(i16, 2, ANGLES, 128), room(f32, 2, 8, 128), room(i16, 2, ANGLES, 128), room(f32, 2, 8, 128),
            room(i16, 2, 2, ANGLES, 128), room(f32, 2, 2, 8, 128),
            room(i16, 2, 2, ANGLES, 128), room(f32, 2, 2, 8, 128),
            room(f32, ANGLES, 128), room(f32, ANGLES, 128), room(f32, 128, 128), room(f32, 2, ANGLES, 128),
            sems(5), sems(peers), sems(peers), sems(1), sems(peers), sems(peers), sems(peers), sems(peers),
            sems(peers - 1), sems(peers - 1), sems(1), sems(1), sems(TILES), sems(TILES),
            sems(peers - 1), sems(peers - 1), sems(depth, 2), sems(depth, 2), sems(depth), sems(depth),
            sems(2, 2), sems(2, 2), sems(2, 2), sems(2, 2), sems(2, 2), sems(2, 2),
            sems(1), sems(1),
        ],
        compiler_params=pltpu.CompilerParams(
            collective_id=3, has_side_effects=True, vmem_limit_bytes=48 * 1024 * 1024
        ),
    )(*[pltpu.with_memory_space_constraint(x, pltpu.HBM) for x in given])


def on_device(boxes, counts, destinations, prior_rot, references, cycle_weights, prior_strength):
    peers = lax.axis_size("particle")
    cycle_index = lax.axis_index("particle")
    cycles_dev = CYCLES // peers
    width = cycles_dev * ANGLES
    if width == 2 * STEP:
        new_references, evidence = whole(
            boxes, jnp.broadcast_to(counts[None, :], (1, boxes.shape[0])), destinations[None, :], prior_rot[None, :], references,
            cycle_weights, prior_strength[None, :], peers,
        )
        return new_references, evidence[0]
    owned = boxes.shape[0]
    classes_dev = references.shape[0]
    lane_index = lax.axis_index("classes")
    row = jnp.concatenate([cycle_weights[0], prior_strength])
    row = jnp.pad(row, (0, 128 - row.shape[0]))[None, :]
    refs, rows = gathered(references, row, peers)
    refs = refs.reshape(2 * classes_dev, -1)
    group_wts = rows[:peers, 0, :CYCLES]
    other = rows[peers, 0, CYCLES : CYCLES + classes_dev]
    strength = jnp.where(
        lane_index == 0,
        jnp.concatenate([prior_strength, other]),
        jnp.concatenate([other, prior_strength]),
    ).reshape(1, -1)
    mine = destinations[:, None] == jnp.arange(peers, dtype=jnp.int32)[None, :]
    wts = jnp.sum(jnp.where(mine[:, :, None], group_wts[None], 0.0), axis=1)
    live = (jnp.arange(owned, dtype=jnp.int32) < counts[0]).astype(jnp.float32)
    turn_ids = jnp.arange(ROTATIONS, dtype=jnp.float32)
    gap = TWO_PI * (turn_ids[None, :] - prior_rot[:, None].astype(jnp.float32)) / ROTATIONS
    aux = jnp.concatenate([jnp.cos(gap), live[:, None], jnp.sum(wts, axis=1)[:, None]], axis=1)
    wts = jnp.transpose(wts.reshape(owned, STEPS, STEP_CYCLES), (1, 0, 2))
    post, mass, evidence = scores(
        boxes, refs, wts, aux, jnp.concatenate([strength, strength], axis=1)
    )
    if width % STEP == 0:
        new_references = fused_sums(boxes, post, mass, references, peers)
    else:
        sums = scattered(plain_sums(boxes, post, mass, classes_dev, peers))
        own_refs = lax.dynamic_slice_in_dim(references, cycle_index * width, width, 1)
        new_references = (sums[:, :width] + own_refs.astype(jnp.float32)) / (
            sums[:, width : width + 1] + 1.0
        )
    return new_references.reshape(classes_dev, cycles_dev, ANGLES), evidence[:, 0]


def solution(mesh):
    in_specs = (
        P(("groups", "particle", "classes"), None),
        P(("groups", "particle", "classes")),
        P(("groups", "particle", "classes")),
        P(("groups", "particle", "classes")),
        P(("groups", "classes"), None),
        P(("groups", "particle"), None),
        P(("groups", "classes")),
    )
    out_specs = (P(("groups", "classes"), "particle", None), P(("groups", "particle", "classes")))
    return jax.shard_map(
        on_device, mesh=mesh, in_specs=in_specs, out_specs=out_specs, check_vma=False
    )
```

```python
import functools
import math

import jax
import jax.numpy as jnp
from jax import lax
from jax.experimental import pallas as pl
from jax.experimental.pallas import tpu as pltpu
from jax.sharding import PartitionSpec as P

CYCLES = 64
ANGLES = 192
ROTATIONS = 24
FINE = 4
COARSE = ROTATIONS // FINE
SHIFT = ANGLES // ROTATIONS
STEP_CYCLES = 4
STEP = STEP_CYCLES * ANGLES
STEPS = CYCLES // STEP_CYCLES
TWO_PI = 2.0 * math.pi


def roll_rows(block, shift):
    shift = shift % ANGLES
    if shift == 0:
        return block
    pieces = []
    for c in range(STEP_CYCLES):
        base = c * ANGLES
        pieces.append(block[base + ANGLES - shift : base + ANGLES])
        pieces.append(block[base : base + ANGLES - shift])
    return jnp.concatenate(pieces, axis=0)


def fan_out(rows, sign):
    plain = jnp.concatenate([rows, rows], axis=0).T
    low = lax.broadcasted_iota(jnp.int32, plain.shape, 1) < rows.shape[0]
    tiles = [
        jnp.where(low, roll_rows(plain, sign * SHIFT * f), roll_rows(plain, sign * SHIFT * (f + 1)))
        for f in range(0, FINE, 2)
    ]
    return jnp.concatenate([t.astype(jnp.bfloat16) for t in tiles], axis=1), plain


def score_kernel(boxes_ref, refs_ref, wts_ref, aux_ref, str_ref, post, mass, ev_ref, acc, off):
    step = pl.program_id(0)
    owned = boxes_ref.shape[0]
    half = str_ref.shape[1]

    @pl.when(step == 0)
    def _():
        acc[...] = jnp.zeros_like(acc)
        off[...] = jnp.zeros_like(off)

    @pl.when(step >= 0)
    def _():
        wts = wts_ref[0]
        lane = lax.broadcasted_iota(jnp.int32, (owned, STEP), 1)
        spread = jnp.broadcast_to(wts[:, 0:1], (owned, STEP))
        for c in range(1, STEP_CYCLES):
            spread = jnp.where(lane >= c * ANGLES, wts[:, c : c + 1], spread)
        scaled = boxes_ref[...].astype(jnp.float32) * spread
        high = scaled.astype(jnp.bfloat16)
        rest = (scaled - high.astype(jnp.float32)).astype(jnp.bfloat16)
        lhs = jnp.concatenate([high, rest], axis=0)
        fan, plain = fan_out(refs_ref[...].astype(jnp.float32), 1)
        total = off[...]
        for c in range(STEP_CYCLES):
            piece = plain[c * ANGLES : (c + 1) * ANGLES]
            total = total + wts[:, c : c + 1] * jnp.sum(piece * piece, axis=0, keepdims=True)
        off[...] = total
        for q in range(COARSE):
            acc[q] += jnp.dot(
                lhs, roll_rows(fan, SHIFT * FINE * q), preferred_element_type=jnp.float32
            )

    @pl.when(step == STEPS - 1)
    def _():
        aux = aux_ref[...]
        live = aux[:, ROTATIONS : ROTATIONS + 1]
        wsum = aux[:, ROTATIONS + 1 : ROTATIONS + 2]
        low = lax.broadcasted_iota(jnp.int32, (owned, half), 1) < owned
        base = -0.5 * off[...]
        strength = str_ref[...]
        top = None
        for q in range(COARSE):
            for t in range(FINE // 2):
                r = q * FINE + 2 * t
                cols = slice(t * half, (t + 1) * half)
                turn = jnp.where(low, aux[:, r : r + 1], aux[:, r + 1 : r + 2])
                score = acc[q, :owned, cols] + acc[q, owned:, cols] + base + turn * strength
                acc[q, :owned, cols] = score
                top = score if top is None else jnp.maximum(top, score)
        top = jnp.max(top, axis=1, keepdims=True)
        norm = jnp.zeros((owned, half), jnp.float32)
        for q in range(COARSE):
            for t in range(FINE // 2):
                cols = slice(t * half, (t + 1) * half)
                term = jnp.exp(acc[q, :owned, cols] - top)
                acc[q, :owned, cols] = term
                norm = norm + term
        norm = jnp.sum(norm, axis=1, keepdims=True)
        ev_ref[...] = jnp.where(live > 0.0, (top + jnp.log(norm)) / (ANGLES * wsum), 0.0)
        seen = jnp.zeros((owned, half), jnp.float32)

        def weight(q, t):
            cols = slice(t * half, (t + 1) * half)
            value = jnp.where(live > 0.0, acc[q, :owned, cols] / norm, 0.0)
            return value.astype(jnp.bfloat16).astype(jnp.float32)

        for q in range(0, COARSE, 2):
            for t in range(FINE // 2):
                first, second = weight(q, t), weight(q + 1, t)
                seen = seen + first + second
                even = jnp.where(low, first, pltpu.roll(second, half // 2, 1))
                odd = jnp.where(low, pltpu.roll(first, half // 2, 1), second)
                cols = slice(q // 2 * half, (q // 2 + 1) * half)
                post[2 * t * owned : (2 * t + 1) * owned, cols] = even.astype(jnp.bfloat16)
                post[(2 * t + 1) * owned : (2 * t + 2) * owned, cols] = odd.astype(jnp.bfloat16)
        seen = jnp.sum(seen, axis=0, keepdims=True)
        mass[...] = seen + pltpu.roll(seen, half // 2, 1)


def turned_sums(boxes, post):
    half = 2 * boxes.shape[0]
    fan, _unused = fan_out(boxes.astype(jnp.float32), -1)
    sums = jnp.dot(fan, post, preferred_element_type=jnp.float32)
    both = sums[:, :half]
    for p in range(1, COARSE // 2):
        both = both + roll_rows(sums[:, p * half : (p + 1) * half], -2 * p * SHIFT * FINE)
    whole = both + pltpu.roll(roll_rows(both, -SHIFT * FINE), half // 2, 1)
    return whole.T


def plain_sums_kernel(width, boxes_ref, post_ref, mass_ref, out_ref):
    turned = turned_sums(boxes_ref[...], post_ref[...])
    classes = out_ref.shape[2]
    mass = jnp.broadcast_to(mass_ref[...], (128, 128)).T
    for h in range(2):
        rows = turned[h * classes : (h + 1) * classes]
        tail = mass[h * classes : (h + 1) * classes, : out_ref.shape[3] - width]
        for j in range(STEP // width):
            out_ref[j, h, :, :width] = rows[:, j * width : (j + 1) * width]
            out_ref[j, h, :, width:] = tail


def plain_sums(boxes, post, mass, classes, peers):
    width = CYCLES // peers * ANGLES
    padded = (width + 1 + 127) // 128 * 128
    return pl.pallas_call(
        functools.partial(plain_sums_kernel, width),
        grid=(STEPS,),
        in_specs=[
            pl.BlockSpec((boxes.shape[0], STEP), lambda i: (0, i)),
            pl.BlockSpec(post.shape, lambda i: (0, 0)),
            pl.BlockSpec(mass.shape, lambda i: (0, 0)),
        ],
        out_specs=pl.BlockSpec((STEP // width, 2, classes, padded), lambda i: (i, 0, 0, 0)),
        out_shape=jax.ShapeDtypeStruct((peers, 2, classes, padded), jnp.float32),
    )(boxes, post, mass)


def scores(boxes, refs, wts, aux, strength):
    owned, classes, half = boxes.shape[0], refs.shape[0], strength.shape[1]
    whole = lambda shape: pl.BlockSpec(shape, lambda i: (0, 0))
    post = (FINE * owned, COARSE * classes)
    return pl.pallas_call(
        score_kernel,
        grid=(STEPS,),
        in_specs=[
            pl.BlockSpec((owned, STEP), lambda i: (0, i)),
            pl.BlockSpec((classes, STEP), lambda i: (0, i)),
            pl.BlockSpec((1, owned, STEP_CYCLES), lambda i: (i, 0, 0)),
            whole(aux.shape),
            whole((1, half)),
        ],
        out_specs=[whole(post), whole((1, half)), whole((owned, 1))],
        out_shape=[
            jax.ShapeDtypeStruct(post, jnp.bfloat16),
            jax.ShapeDtypeStruct((1, half), jnp.float32),
            jax.ShapeDtypeStruct((owned, 1), jnp.float32),
        ],
        scratch_shapes=[
            pltpu.VMEM((COARSE, 2 * owned, FINE * classes), jnp.float32),
            pltpu.VMEM((owned, half), jnp.float32),
        ],
        compiler_params=pltpu.CompilerParams(
            dimension_semantics=("arbitrary",), vmem_limit_bytes=40 * 1024 * 1024
        ),
    )(boxes, refs, wts, aux, strength)


MESH = pl.DeviceIdType.MESH
CHUNKS = 4


def greet(devices):
    barrier = pltpu.get_barrier_semaphore()
    for device in devices:
        pl.semaphore_signal(barrier, inc=1, device_id=device, device_id_type=MESH)
    pl.semaphore_wait(barrier, len(devices))


def gather_kernel(peers, refs_ref, row_ref, all_refs, all_rows, local, send, recv):
    mine, core = lax.axis_index("particle"), lax.axis_index("classes")
    partner = {"classes": 1 - core}
    others = [{"particle": lax.rem(mine + d, peers)} for d in range(1, peers)]
    greet([partner] + others)
    copies = [
        pltpu.make_async_remote_copy(
            src_ref=refs_ref, dst_ref=all_refs.at[core], send_sem=send.at[0], recv_sem=recv.at[0],
            device_id=partner, device_id_type=MESH,
        ),
        pltpu.make_async_remote_copy(
            src_ref=row_ref, dst_ref=all_rows.at[peers], send_sem=send.at[1], recv_sem=recv.at[1],
            device_id=partner, device_id_type=MESH,
        ),
    ]
    for d, other in enumerate(others):
        copies.append(
            pltpu.make_async_remote_copy(
                src_ref=row_ref, dst_ref=all_rows.at[mine], send_sem=send.at[2 + d],
                recv_sem=recv.at[2 + d], device_id=other, device_id_type=MESH,
            )
        )
    for copy in copies:
        copy.start()
    own = [
        pltpu.make_async_copy(refs_ref, all_refs.at[core], local.at[0]),
        pltpu.make_async_copy(row_ref, all_rows.at[mine], local.at[1]),
    ]
    for copy in own:
        copy.start()
    for copy in own + copies:
        copy.wait()


def gathered(refs, row, peers):
    return pl.pallas_call(
        functools.partial(gather_kernel, peers),
        in_specs=[pl.BlockSpec(memory_space=pltpu.VMEM)] * 2,
        out_specs=[pl.BlockSpec(memory_space=pltpu.VMEM)] * 2,
        out_shape=[
            jax.ShapeDtypeStruct((2,) + refs.shape, refs.dtype),
            jax.ShapeDtypeStruct((peers + 1,) + row.shape, row.dtype),
        ],
        scratch_shapes=[
            pltpu.SemaphoreType.DMA((2,)),
            pltpu.SemaphoreType.DMA((peers + 1,)),
            pltpu.SemaphoreType.DMA((peers + 1,)),
        ],
        compiler_params=pltpu.CompilerParams(collective_id=0, has_side_effects=True),
    )(refs, row)


def scatter_kernel(depth, parts, out, pair_in, side_out, side_in, line_out, line_in,
                   pair_send, pair_recv, side_send, side_recv, line_send, line_recv):
    mine, core = lax.axis_index("particle"), lax.axis_index("classes")
    level, side = mine // 2, lax.rem(mine, 2)
    partner = {"classes": 1 - core}
    across = {"particle": level * 2 + 1 - side}
    levels = [lax.rem(level + d, depth) for d in range(1, depth)]
    line = [{"particle": other * 2 + side} for other in levels]
    greet([partner, across] + line)
    rows = out.shape[0] // CHUNKS
    pair, cross, lines = [], [], []
    for j in range(CHUNKS):
        copy = pltpu.make_async_remote_copy(
            src_ref=parts.at[:, :, 1 - core, j * rows : (j + 1) * rows], dst_ref=pair_in.at[j],
            send_sem=pair_send.at[j], recv_sem=pair_recv.at[j], device_id=partner,
            device_id_type=MESH,
        )
        copy.start()
        pair.append(copy)
    for j in range(CHUNKS):
        span = slice(j * rows, (j + 1) * rows)
        pair[j].wait_recv()
        side_out[j] = parts[:, 1 - side, core, span] + pair_in[j, :, 1 - side]
        copy = pltpu.make_async_remote_copy(
            src_ref=side_out.at[j], dst_ref=side_in.at[j], send_sem=side_send.at[j],
            recv_sem=side_recv.at[j], device_id=across, device_id_type=MESH,
        )
        copy.start()
        cross.append(copy)
        line_out[j] = parts[:, side, core, span] + pair_in[j, :, side]
    for j in range(CHUNKS):
        cross[j].wait_recv()
        line_out[j] = line_out[j] + side_in[j]
        for d in range(depth - 1):
            copy = pltpu.make_async_remote_copy(
                src_ref=line_out.at[j, levels[d]], dst_ref=line_in.at[j, d],
                send_sem=line_send.at[j, d], recv_sem=line_recv.at[j, d], device_id=line[d],
                device_id_type=MESH,
            )
            copy.start()
            lines.append(copy)
    for j in range(CHUNKS):
        total = line_out[j, level]
        for d in range(depth - 1):
            lines[j * (depth - 1) + d].wait_recv()
            total = total + line_in[j, d]
        out[j * rows : (j + 1) * rows] = total
    for copy in pair + cross + lines:
        copy.wait_send()


def scattered(parts):
    peers, _, classes, width = parts.shape
    depth = peers // 2
    rows = classes // CHUNKS
    sems = pltpu.SemaphoreType.DMA((CHUNKS,))
    line_sems = pltpu.SemaphoreType.DMA((CHUNKS, max(depth - 1, 1)))
    return pl.pallas_call(
        functools.partial(scatter_kernel, depth),
        in_specs=[pl.BlockSpec(memory_space=pltpu.VMEM)],
        out_specs=pl.BlockSpec(memory_space=pltpu.VMEM),
        out_shape=jax.ShapeDtypeStruct((classes, width), jnp.float32),
        scratch_shapes=[
            pltpu.VMEM((CHUNKS, depth, 2, rows, width), jnp.float32),
            pltpu.VMEM((CHUNKS, depth, rows, width), jnp.float32),
            pltpu.VMEM((CHUNKS, depth, rows, width), jnp.float32),
            pltpu.VMEM((CHUNKS, depth, rows, width), jnp.float32),
            pltpu.VMEM((CHUNKS, max(depth - 1, 1), rows, width), jnp.float32),
            sems, sems, sems, sems, line_sems, line_sems,
        ],
        compiler_params=pltpu.CompilerParams(
            collective_id=1, has_side_effects=True, vmem_limit_bytes=48 * 1024 * 1024
        ),
    )(parts.reshape(depth, 2, 2, classes, width))


def sums_kernel(peers, boxes, post, mass, refs, out, pair_out, pair_in, keep, side_out, side_in,
                line_in, mass_in, column, pair_send, pair_recv, side_send, side_recv, line_send,
                line_recv, mass_send, mass_recv):
    mine, core = lax.axis_index("particle"), lax.axis_index("classes")
    depth, width, classes = peers // 2, out.shape[1], out.shape[0]
    level, side = mine // 2, lax.rem(mine, 2)
    place = mine * 2 + core
    partner = {"classes": 1 - core}
    across = {"particle": level * 2 + 1 - side}
    everyone = []
    for e in range(1, 2 * peers):
        there = lax.rem(place + e, 2 * peers)
        everyone.append({"particle": there // 2, "classes": lax.rem(there, 2)})
    greet(everyone)
    started, masses = [], []

    def send(src, dst, sends, recvs, device):
        copy = pltpu.make_async_remote_copy(
            src_ref=src, dst_ref=dst, send_sem=sends, recv_sem=recvs, device_id=device,
            device_id_type=MESH,
        )
        copy.start()
        started.append(copy)
        return copy

    for e, device in enumerate(everyone):
        masses.append(
            send(mass, mass_in.at[e], mass_send.at[e], mass_recv.at[e], device)
        )
    turns = list(range(1, depth)) + [0]
    blocks = [(i, d, True) for i, d in enumerate(turns)] + [(i, d, False) for i, d in enumerate(turns)]
    pair, cross, lines = [], [], []

    def advance(n):
        i, d, away = blocks[n]
        pair[n].wait_recv()
        if away:
            side_out[i] = keep[n] + pair_in[n]
            cross.append(
                send(side_out.at[i], side_in.at[i], side_send.at[i], side_recv.at[i], across)
            )
            return
        cross[i].wait_recv()
        keep[n] = keep[n] + pair_in[n] + side_in[i]
        if d > 0:
            there = {"particle": lax.rem(level + d, depth) * 2 + side}
            lines.append(
                send(keep.at[n], line_in.at[i], line_send.at[i], line_recv.at[i], there)
            )

    for n, (i, d, away) in enumerate(blocks):
        shard = lax.rem(level + d, depth) * 2 + (1 - side if away else side)

        @pl.loop(0, width // STEP)
        def _(part):
            source = pl.multiple_of(shard * width + part * STEP, 128)
            target = pl.multiple_of(part * STEP, 128)
            turned = turned_sums(boxes[:, pl.ds(source, STEP)], post[...])
            low, high = turned[:classes], turned[classes : 2 * classes]
            keep[n, :, pl.ds(target, STEP)] = jnp.where(core == 0, low, high)
            pair_out[n, :, pl.ds(target, STEP)] = jnp.where(core == 0, high, low)

        pair.append(send(pair_out.at[n], pair_in.at[n], pair_send.at[n], pair_recv.at[n], partner))
        if n > 0:
            advance(n - 1)
    advance(len(blocks) - 1)
    weight = mass[...]
    for e, copy in enumerate(masses):
        copy.wait_recv()
        weight = weight + mass_in[e]
    column[...] = jnp.broadcast_to(weight, column.shape).T
    scale = column[pl.ds(pl.multiple_of(core * classes, 8), classes), :]
    total = keep[len(blocks) - 1]
    for i in range(depth - 1):
        lines[i].wait_recv()
        total = total + line_in[i]
    base = refs[:, pl.ds(pl.multiple_of(mine * width, 128), width)].astype(jnp.float32)
    out[...] = (total + base) / (scale[:, 0:1] + 1.0)
    for copy in started:
        copy.wait_send()


def fused_sums(boxes, post, mass, refs, peers):
    classes, width, depth = refs.shape[0], CYCLES // peers * ANGLES, peers // 2
    room = lambda count: pltpu.VMEM((count, classes, width), jnp.float32)
    sems = lambda count: pltpu.SemaphoreType.DMA((count,))
    others = 2 * peers - 1
    return pl.pallas_call(
        functools.partial(sums_kernel, peers),
        in_specs=[pl.BlockSpec(memory_space=pltpu.VMEM)] * 4,
        out_specs=pl.BlockSpec(memory_space=pltpu.VMEM),
        out_shape=jax.ShapeDtypeStruct((classes, width), jnp.float32),
        scratch_shapes=[
            room(peers), room(peers), room(peers), room(depth), room(depth), room(depth - 1),
            pltpu.VMEM((others,) + mass.shape, jnp.float32),
            pltpu.VMEM((mass.shape[1], mass.shape[1]), jnp.float32),
            sems(peers), sems(peers), sems(depth), sems(depth), sems(depth - 1), sems(depth - 1),
            sems(others), sems(others),
        ],
        compiler_params=pltpu.CompilerParams(
            collective_id=2, has_side_effects=True, vmem_limit_bytes=48 * 1024 * 1024
        ),
    )(boxes, post, mass, refs)


PARTS = 4
QUARTERS = 4
TILES = 6
APART = ANGLES // QUARTERS
SLOTS = 128
LEVELS = 32767.0


def turned(block, shift):
    shift = shift % ANGLES
    if shift == 0:
        return block
    return jnp.concatenate([block[ANGLES - shift :], block[: ANGLES - shift]], axis=0)


def flip(block):
    return pltpu.roll(block, 64, 1)


def low_lanes(rows, width=64, period=128):
    lane = lax.broadcasted_iota(jnp.int32, (rows, 128), 1)
    return lax.rem(lane, period) < width


def encode(block, codes, scales):
    largest = jnp.maximum(jnp.max(jnp.abs(block), axis=0, keepdims=True), 1e-30)
    codes[...] = jnp.round(block * (LEVELS / largest)).astype(jnp.int32).astype(jnp.int16)
    scales[0:1, :] = largest * (1.0 / LEVELS)


def refs_fan(refs, fans, energies, p):
    cols = slice(p * STEP, (p + 1) * STEP)
    rows = refs[:, cols].astype(jnp.float32)
    plain = jnp.concatenate([rows, rows], axis=0).T
    low = low_lanes(ANGLES)
    for c in range(PARTS):
        base = p * STEP + c * ANGLES
        piece = plain[c * ANGLES : (c + 1) * ANGLES]
        energies[p * PARTS + c : p * PARTS + c + 1, :] = jnp.sum(piece * piece, axis=0, keepdims=True)
        both = jnp.where(low, piece, turned(piece, APART))
        fans[0, base : base + ANGLES, :] = both.astype(jnp.bfloat16)
        fans[1, base : base + ANGLES, :] = turned(both, SHIFT).astype(jnp.bfloat16)


def boxes_fan(boxes, fans, p):
    cols = slice(p * STEP, (p + 1) * STEP)
    plain = boxes[:, cols].astype(jnp.float32).T
    fans[0, cols, :] = plain.astype(jnp.bfloat16)
    for c in range(PARTS):
        base = p * STEP + c * ANGLES
        piece = plain[c * ANGLES : (c + 1) * ANGLES]
        fans[1, base : base + ANGLES, :] = turned(piece, -SHIFT).astype(jnp.bfloat16)


def score_tiles(boxes, fans, wide, g, cycles):
    totals = [None, None]
    blank = jnp.zeros((256 - ANGLES, 256), jnp.bfloat16)
    for c in range(cycles):
        base, window = c * ANGLES, c // 2 * 2 * ANGLES + c % 2 * 128
        factor = wide[c]
        factor = jnp.concatenate([factor, factor], axis=1)
        for parity in range(2):
            piece = fans[parity, base : base + ANGLES, :]
            shift = 2 * SHIFT * g
            piece = jnp.concatenate(
                [turned(piece, shift), turned(piece, shift + 2 * APART)], axis=1
            )
            piece = jnp.concatenate([piece, blank] if c % 2 == 0 else [blank, piece], axis=0)
            part = factor * jnp.dot(
                boxes[:, window : window + 256], piece, preferred_element_type=jnp.float32
            )
            totals[parity] = part if totals[parity] is None else totals[parity] + part
    return totals


def class_sums(fans, post, shard):
    rows = []
    for c in range(PARTS):
        base = pl.multiple_of(shard * STEP + c * ANGLES, 64)
        even = fans[0, pl.ds(base, ANGLES), :]
        odd = fans[1, pl.ds(base, ANGLES), :]
        rows.append(
            jnp.concatenate(
                [turned(x, -2 * SHIFT * s) for s in range(TILES // 2) for x in (even, odd)], axis=1
            )
        )
    sums = jnp.dot(jnp.concatenate(rows, axis=0), post[...], preferred_element_type=jnp.float32)
    low, first = low_lanes(ANGLES), low_lanes(ANGLES, 32, 64)
    both = []
    for c in range(PARTS):
        piece = sums[c * ANGLES : (c + 1) * ANGLES]
        b = piece[:, :128] + turned(piece[:, 128:], -2 * APART)
        both.append((b, turned(b, -APART)))

    def pair(i, j):
        return jnp.where(low, both[i][0], both[j][1]) + flip(jnp.where(low, both[j][0], both[i][1]))

    a, b = pair(0, 2), pair(1, 3)
    return jnp.where(first, a, pltpu.roll(b, 32, 1)), jnp.where(first, pltpu.roll(a, 96, 1), b)


def whole_kernel(
    peers, boxes, counts, places_in, turns_in, refs, weights_in, strength_in, out, evidence,
    places, turns, weights, strength, xs, rs, own, cards, duo, ref_fans, box_fans, energies, base_refs, wide, mine_s, theirs_s, terms,
    post, masses, y_out, y_out_s, y_in, y_in_s, keep, near_out, near_out_s, near_in, near_in_s, z_out, z_out_s, z_in, z_in_s, pair_out, pair_in, scale, totals,
    small_local, box_local, ref_local, own_local, box_send, box_recv, ref_send, ref_recv, card_send, card_recv,
    duo_send, duo_recv, score_send, score_recv, mass_send, mass_recv, y_send, y_recv, ys_send, ys_recv,
    near_send, near_recv, z_send, z_recv, zs_send, zs_recv, pair_send, pair_recv,
):
    mine, core = lax.axis_index("particle"), lax.axis_index("classes")
    depth, owned, classes = peers // 2, boxes.shape[0], refs.shape[0]
    level, side = mine // 2, lax.rem(mine, 2)
    partner = {"classes": 1 - core}
    across = {"particle": level * 2 + 1 - side}
    others = [{"particle": lax.rem(mine + d, peers)} for d in range(1, peers)]
    near, far = level + 1 - 2 * lax.rem(level, 2), lax.rem(level + 2, depth)
    levels = [lax.rem(near + 2, depth), far, near, level]
    diagonal = [{"particle": there * 2 + side, "classes": 1 - core} for there in (far, near)]
    straight = [{"particle": there * 2 + side} for there in (far, near)]
    barrier = pltpu.get_barrier_semaphore()
    friends = [partner] + others + diagonal
    for device in friends:
        pl.semaphore_signal(barrier, inc=1, device_id=device, device_id_type=MESH)
    box_rows = pl.ds(pl.multiple_of(core * owned, owned), owned)
    ref_rows = pl.ds(pl.multiple_of(core * classes, classes), classes)
    local = []
    for p in range(peers):
        source = pl.ds(pl.multiple_of((2 * p + core) * STEP, 128), STEP)
        target = pl.ds(p * STEP, STEP)
        local.append(
            pltpu.make_async_copy(refs.at[:, source], rs.at[ref_rows, target], ref_local.at[p])
        )
        local.append(
            pltpu.make_async_copy(boxes.at[:, source], xs.at[box_rows, target], box_local.at[p])
        )
    width = 2 * STEP
    own_copy = pltpu.make_async_copy(
        refs.at[:, pl.ds(pl.multiple_of(mine * width, 128), width)], own, own_local.at[0]
    )
    small = [
        pltpu.make_async_copy(source, target, small_local.at[n])
        for n, (source, target) in enumerate(
            [
                (places_in, places), (turns_in, turns), (weights_in, weights), (strength_in, strength),
            ]
        )
    ]
    for copy in small + local + [own_copy]:
        copy.start()
    for copy in small:
        copy.wait()
    card = jnp.zeros((8, 128), jnp.float32)
    cards[mine] = card
    slot = lax.broadcasted_iota(jnp.int32, (1, owned), 1)
    cards[mine, 0:1, :CYCLES] = weights[...]
    cards[mine, 1:2, :owned] = places[...].astype(jnp.float32)
    cards[mine, 2:3, :owned] = turns[...].astype(jnp.float32)
    cards[mine, 3:4, :owned] = jnp.where(slot < counts[0], 1.0, 0.0)
    cards[mine, 4:5, :classes] = strength[...]
    duo[core] = cards[mine]

    started = []

    def send(src, dst, sends, recvs, device):
        copy = pltpu.make_async_remote_copy(
            src_ref=src, dst_ref=dst, send_sem=sends, recv_sem=recvs, device_id=device,
            device_id_type=MESH,
        )
        copy.start()
        started.append(copy)
        return copy

    pl.semaphore_wait(barrier, len(friends))
    card_copies = [
        send(cards.at[mine, 0:1], cards.at[mine, 0:1], card_send.at[d], card_recv.at[d], device)
        for d, device in enumerate(others)
    ]
    duo_copy = send(duo.at[core], duo.at[core], duo_send.at[0], duo_recv.at[0], partner)
    ref_copies, box_copies = [], []
    for p in range(peers):
        source = pl.ds(pl.multiple_of((2 * p + 1 - core) * STEP, 128), STEP)
        target = pl.ds(p * STEP, STEP)
        ref_copies.append(
            send(refs.at[:, source], rs.at[ref_rows, target], ref_send.at[p], ref_recv.at[p], partner)
        )
    for p in range(peers):
        source = pl.ds(pl.multiple_of((2 * p + 1 - core) * STEP, 128), STEP)
        target = pl.ds(p * STEP, STEP)
        box_copies.append(
            send(boxes.at[:, source], xs.at[box_rows, target], box_send.at[p], box_recv.at[p], partner)
        )
    own_copy.wait()
    for h in range(2):
        for c in range(PARTS):
            base = (h * PARTS + c) * ANGLES
            base_refs[h, c * classes : (c + 1) * classes, :] = own[:, base : base + ANGLES].astype(
                jnp.float32
            )
    for copy in local:
        copy.wait()
    for p in range(peers):
        ref_copies[p].wait_recv()
        refs_fan(rs, ref_fans, energies, p)

    duo_copy.wait_recv()
    facts = duo[0] + flip(duo[1])
    facts = jnp.concatenate([facts] * (SLOTS // 8), axis=0).T
    place, turn, live = facts[:, 1:2], facts[:, 2:3], facts[:, 3:4]
    force = duo[0, 4:5, :] + pltpu.roll(duo[1, 4:5, :], classes, 1)
    force = force + flip(force)
    lane = lax.broadcasted_iota(jnp.int32, (SLOTS, 128), 1).astype(jnp.float32)
    swing = jnp.cos(TWO_PI * (lane - turn) / ROTATIONS)
    for copy in card_copies:
        copy.wait_recv()
    spread = jnp.zeros((SLOTS, 128), jnp.float32)
    for g in range(peers):
        spread = jnp.where(place == float(g), cards[g, 0:1, :], spread)
    wsum = jnp.sum(spread, axis=1, keepdims=True)
    spread = jnp.where(core == 0, spread, pltpu.roll(spread, 128 - PARTS, 1))
    base = jnp.zeros((SLOTS, 128), jnp.float32)
    for c in range(CYCLES // 2):
        place = c // PARTS * 2 * PARTS + c % PARTS
        factor = jnp.broadcast_to(spread[:, place : place + 1], (SLOTS, 128))
        wide[c] = factor
        base = base + factor * energies[c : c + 1, :]
    base = -0.5 * base
    for copy in box_copies:
        copy.wait_recv()

    low = low_lanes(SLOTS)
    score_copies, tops, norms = [], [], []

    def finish(f):
        score_copies[f].wait_recv()
        values = []
        for t in range(2):
            cols = slice(t * 128, (t + 1) * 128)
            r = f + 2 * t * TILES
            prior = jnp.where(low, swing[:, r : r + 1], swing[:, r + TILES : r + TILES + 1]) * force
            values.append(mine_s[f, :, cols] + theirs_s[f, :, cols] + prior)
        top = jnp.max(jnp.maximum(values[0], values[1]), axis=1, keepdims=True)
        values = [jnp.exp(v - top) for v in values]
        for t in range(2):
            terms[f, :, t * 128 : (t + 1) * 128] = values[t]
        tops.append(top)
        norms.append(jnp.sum(values[0] + values[1], axis=1, keepdims=True))

    for g in range(TILES // 2):
        for f, tile in enumerate(score_tiles(xs, ref_fans, wide, g, CYCLES // 2), 2 * g):
            mine_s[f] = tile + jnp.concatenate([base, base], axis=1)
        for f in (2 * g, 2 * g + 1):
            score_copies.append(
                send(mine_s.at[f], theirs_s.at[f], score_send.at[f], score_recv.at[f], partner)
            )
        if g > 0:
            finish(2 * g - 2)
            finish(2 * g - 1)
    for p in range(peers):
        boxes_fan(xs, box_fans, p)
    finish(TILES - 2)
    finish(TILES - 1)
    top = functools.reduce(jnp.maximum, tops)
    factors = [jnp.exp(t - top) for t in tops]
    norm = sum(n * s for n, s in zip(norms, factors))
    for f in range(TILES):
        factor = jnp.where(live > 0.0, factors[f] / norm, 0.0)
        post[f * SLOTS : (f + 1) * SLOTS, :] = (terms[f] * factor).astype(jnp.bfloat16)

    def mass_and_evidence():
        mass = jnp.zeros((8, 256), jnp.float32)
        for f in range(TILES):
            value = post[f * SLOTS : (f + 1) * SLOTS, :].astype(jnp.float32)
            for i in range(SLOTS // 8):
                mass = mass + value[i * 8 : (i + 1) * 8]
        mass = mass[:, :128] + mass[:, 128:]
        mass = mass + flip(mass)
        masses[mine] = jnp.broadcast_to(jnp.sum(mass, axis=0, keepdims=True), (8, 128))
        for d, device in enumerate(others):
            mass_copies.append(
                send(
                    masses.at[mine, 0:1], masses.at[mine, 0:1], mass_send.at[d], mass_recv.at[d],
                    device,
                )
            )
        proof = jnp.where(live > 0.0, (top + jnp.log(norm)) / (ANGLES * wsum), 0.0)
        proof = jnp.broadcast_to(proof, (SLOTS, 128)).T[0:1]
        evidence[...] = jnp.where(core == 0, proof, flip(proof))[:, :owned]

    mass_copies = []
    y_copies, z_copies, near_copies, waited = [], [[], []], [], set()

    def away(i, blocks):
        for h, value in enumerate(blocks):
            encode(value, y_out.at[i, h], y_out_s.at[i, h : h + 1])
        y_copies.append(
            [send(y_out_s.at[i, 0:2], y_in_s.at[i, 0:2], ys_send.at[i], ys_recv.at[i], across)]
            + [
                send(y_out.at[i, h], y_in.at[i, h], y_send.at[i, n], y_recv.at[i, n], across)
                for n, h in enumerate([1 - core, core])
            ]
        )

    def home(i, blocks):
        for h, value in enumerate(blocks):
            keep[i, h] = value

    halves = [1 - core, core]

    def arrived(copies):
        for copy in copies:
            if id(copy) not in waited:
                copy.wait_recv()
                waited.add(id(copy))

    def summed(i, n):
        half = halves[n]
        arrived(y_copies[i][: n + 2])
        row = jnp.where(half == 0, y_in_s[i, 0:1, :], y_in_s[i, 1:2, :])
        codes = y_in[i, half].astype(jnp.int32).astype(jnp.float32)
        return keep[i, half] + codes * row

    def to_near(n):
        half = halves[n]
        encode(summed(0, n), near_out.at[half], near_out_s.at[half])
        near_copies.append(
            [
                send(
                    near_out_s.at[half, 0:1], near_in_s.at[half, 0:1], near_send.at[n, 1],
                    near_recv.at[n, 1], straight[1],
                ),
                send(
                    near_out.at[half], near_in.at[half], near_send.at[n, 0], near_recv.at[n, 0],
                    straight[1],
                ),
            ]
        )

    def to_owner(j, n):
        half = halves[n]
        total = summed(j + 1, n)
        if j == 0:
            arrived(near_copies[n])
            codes = near_in[half].astype(jnp.int32).astype(jnp.float32)
            total = total + codes * near_in_s[half, 0:1, :]
        encode(total, z_out.at[j, half], z_out_s.at[j, half])
        device = diagonal[j] if n == 0 else straight[j]
        z_copies[j].append(
            send(
                z_out_s.at[j, half, 0:1], z_in_s.at[j, core, 0:1], zs_send.at[j, n],
                zs_recv.at[j, n], device,
            )
        )
        z_copies[j].append(
            send(z_out.at[j, half], z_in.at[j, core], z_send.at[j, n], z_recv.at[j, n], device)
        )

    shards = lambda i: (levels[i] * 2 + 1 - side, levels[i] * 2 + side)
    away(0, class_sums(box_fans, post, shards(0)[0]))
    for i in range(1, depth):
        held = class_sums(box_fans, post, shards(i - 1)[1])
        away(i, class_sums(box_fans, post, shards(i)[0]))
        home(i - 1, held)
        if i == 1:
            mass_and_evidence()
        if i < depth - 1:
            to_near(i - 1)
    home(depth - 1, class_sums(box_fans, post, shards(depth - 1)[1]))
    for j in range(2):
        for n in range(2):
            to_owner(j, n)

    for copy in mass_copies:
        copy.wait_recv()
    weight = masses[0, 0:1, :]
    for g in range(1, peers):
        weight = weight + masses[g, 0:1, :]
    weight = jnp.broadcast_to(weight, (8, 128))
    first = low_lanes(8, 32, 64)
    weight = jnp.where(
        core == 0,
        jnp.where(first, weight, pltpu.roll(weight, 32, 1)),
        jnp.where(first, pltpu.roll(weight, 96, 1), weight),
    )
    scale[...] = jnp.concatenate([weight] * 16, axis=0).T + 1.0

    def crossed(j, h):
        arrived(z_copies[j])
        return z_in[j, h].astype(jnp.int32).astype(jnp.float32) * z_in_s[j, h, 0:1, :]

    def store(half, value):
        result = (value.T + base_refs[half]) / scale[:, 0:1]
        for c in range(PARTS):
            out[:, half * PARTS + c, :] = result[c * classes : (c + 1) * classes]

    pair_out[...] = summed(depth - 1, 0)
    pair_copy = send(pair_out, pair_in, pair_send.at[0], pair_recv.at[0], partner)
    held = summed(depth - 1, 1)
    for h in range(2):
        totals[h] = crossed(1, h)
    pair_copy.wait_recv()
    for h in range(2):
        totals[h] = totals[h] + jnp.where(core == h, held, pair_in[...])
    for h in range(2):
        store(h, totals[h] + crossed(0, h))
    for copy in started:
        copy.wait_send()


def whole(boxes, counts, places, turns, refs, weights, strength, peers):
    given = (boxes, places, turns, refs, weights, strength)
    pinned = [pltpu.with_memory_space_constraint(x, pltpu.HBM) for x in given]
    classes, depth = refs.shape[0], peers // 2
    half = CYCLES * ANGLES // 2
    f32, bf16, i16 = jnp.float32, jnp.bfloat16, jnp.int16
    room = lambda dtype, *shape: pltpu.VMEM(shape, dtype)
    sems = lambda *shape: pltpu.SemaphoreType.DMA(shape)
    vmem = pl.BlockSpec(memory_space=pltpu.VMEM)
    hbm = pl.BlockSpec(memory_space=pltpu.HBM)
    return pl.pallas_call(
        functools.partial(whole_kernel, peers),
        in_specs=[hbm, pl.BlockSpec(memory_space=pltpu.SMEM)] + [hbm] * 5,
        out_specs=[vmem, vmem],
        out_shape=[
            jax.ShapeDtypeStruct((classes, CYCLES // peers, ANGLES), f32),
            jax.ShapeDtypeStruct((1, boxes.shape[0]), f32),
        ],
        scratch_shapes=[
            pltpu.VMEM(places.shape, places.dtype),
            pltpu.VMEM(turns.shape, turns.dtype), pltpu.VMEM(weights.shape, f32),
            pltpu.VMEM(strength.shape, f32), room(bf16, SLOTS, half), room(bf16, 2 * classes, half), room(bf16, classes, 2 * STEP),
            room(f32, peers, 8, 128), room(f32, 2, 8, 128),
            room(bf16, 2, half, 128), room(bf16, 2, half, 128), room(f32, CYCLES // 2, 128),
            room(f32, 2, 128, ANGLES), room(f32, CYCLES // 2, SLOTS, 128),
            room(f32, TILES, SLOTS, 256), room(f32, TILES, SLOTS, 256), room(f32, TILES, SLOTS, 256),
            room(bf16, TILES * SLOTS, 256), room(f32, peers, 8, 128),
            room(i16, depth, 2, ANGLES, 128), room(f32, depth, 8, 128),
            room(i16, depth, 2, ANGLES, 128), room(f32, depth, 8, 128),
            room(f32, depth, 2, ANGLES, 128),
            room(i16, 2, ANGLES, 128), room(f32, 2, 8, 128), room(i16, 2, ANGLES, 128), room(f32, 2, 8, 128),
            room(i16, 2, 2, ANGLES, 128), room(f32, 2, 2, 8, 128),
            room(i16, 2, 2, ANGLES, 128), room(f32, 2, 2, 8, 128),
            room(f32, ANGLES, 128), room(f32, ANGLES, 128), room(f32, 128, 128), room(f32, 2, ANGLES, 128),
            sems(4), sems(peers), sems(peers), sems(1), sems(peers), sems(peers), sems(peers), sems(peers),
            sems(peers - 1), sems(peers - 1), sems(1), sems(1), sems(TILES), sems(TILES),
            sems(peers - 1), sems(peers - 1), sems(depth, 2), sems(depth, 2), sems(depth), sems(depth),
            sems(2, 2), sems(2, 2), sems(2, 2), sems(2, 2), sems(2, 2), sems(2, 2),
            sems(1), sems(1),
        ],
        compiler_params=pltpu.CompilerParams(
            collective_id=3, has_side_effects=True, vmem_limit_bytes=48 * 1024 * 1024
        ),
    )(pinned[0], counts, *pinned[1:])


def on_device(boxes, counts, destinations, prior_rot, references, cycle_weights, prior_strength):
    peers = lax.axis_size("particle")
    cycle_index = lax.axis_index("particle")
    cycles_dev = CYCLES // peers
    width = cycles_dev * ANGLES
    if width == 2 * STEP:
        new_references, evidence = whole(
            boxes, counts, destinations[None, :], prior_rot[None, :], references,
            cycle_weights, prior_strength[None, :], peers,
        )
        return new_references, evidence[0]
    owned = boxes.shape[0]
    classes_dev = references.shape[0]
    lane_index = lax.axis_index("classes")
    row = jnp.concatenate([cycle_weights[0], prior_strength])
    row = jnp.pad(row, (0, 128 - row.shape[0]))[None, :]
    refs, rows = gathered(references, row, peers)
    refs = refs.reshape(2 * classes_dev, -1)
    group_wts = rows[:peers, 0, :CYCLES]
    other = rows[peers, 0, CYCLES : CYCLES + classes_dev]
    strength = jnp.where(
        lane_index == 0,
        jnp.concatenate([prior_strength, other]),
        jnp.concatenate([other, prior_strength]),
    ).reshape(1, -1)
    mine = destinations[:, None] == jnp.arange(peers, dtype=jnp.int32)[None, :]
    wts = jnp.sum(jnp.where(mine[:, :, None], group_wts[None], 0.0), axis=1)
    live = (jnp.arange(owned, dtype=jnp.int32) < counts[0]).astype(jnp.float32)
    turn_ids = jnp.arange(ROTATIONS, dtype=jnp.float32)
    gap = TWO_PI * (turn_ids[None, :] - prior_rot[:, None].astype(jnp.float32)) / ROTATIONS
    aux = jnp.concatenate([jnp.cos(gap), live[:, None], jnp.sum(wts, axis=1)[:, None]], axis=1)
    wts = jnp.transpose(wts.reshape(owned, STEPS, STEP_CYCLES), (1, 0, 2))
    post, mass, evidence = scores(
        boxes, refs, wts, aux, jnp.concatenate([strength, strength], axis=1)
    )
    if width % STEP == 0:
        new_references = fused_sums(boxes, post, mass, references, peers)
    else:
        sums = scattered(plain_sums(boxes, post, mass, classes_dev, peers))
        own_refs = lax.dynamic_slice_in_dim(references, cycle_index * width, width, 1)
        new_references = (sums[:, :width] + own_refs.astype(jnp.float32)) / (
            sums[:, width : width + 1] + 1.0
        )
    return new_references.reshape(classes_dev, cycles_dev, ANGLES), evidence[:, 0]


def solution(mesh):
    in_specs = (
        P(("groups", "particle", "classes"), None),
        P(("groups", "particle", "classes")),
        P(("groups", "particle", "classes")),
        P(("groups", "particle", "classes")),
        P(("groups", "classes"), None),
        P(("groups", "particle"), None),
        P(("groups", "classes")),
    )
    out_specs = (P(("groups", "classes"), "particle", None), P(("groups", "particle", "classes")))
    return jax.shard_map(
        on_device, mesh=mesh, in_specs=in_specs, out_specs=out_specs, check_vma=False
    )
```

```python
import functools
import math

import jax
import jax.numpy as jnp
from jax import lax
from jax.experimental import pallas as pl
from jax.experimental.pallas import tpu as pltpu
from jax.sharding import PartitionSpec as P

CYCLES = 64
ANGLES = 192
ROTATIONS = 24
FINE = 4
COARSE = ROTATIONS // FINE
SHIFT = ANGLES // ROTATIONS
STEP_CYCLES = 4
STEP = STEP_CYCLES * ANGLES
STEPS = CYCLES // STEP_CYCLES
TWO_PI = 2.0 * math.pi


def roll_rows(block, shift):
    shift = shift % ANGLES
    if shift == 0:
        return block
    pieces = []
    for c in range(STEP_CYCLES):
        base = c * ANGLES
        pieces.append(block[base + ANGLES - shift : base + ANGLES])
        pieces.append(block[base : base + ANGLES - shift])
    return jnp.concatenate(pieces, axis=0)


def fan_out(rows, sign):
    plain = jnp.concatenate([rows, rows], axis=0).T
    low = lax.broadcasted_iota(jnp.int32, plain.shape, 1) < rows.shape[0]
    tiles = [
        jnp.where(low, roll_rows(plain, sign * SHIFT * f), roll_rows(plain, sign * SHIFT * (f + 1)))
        for f in range(0, FINE, 2)
    ]
    return jnp.concatenate([t.astype(jnp.bfloat16) for t in tiles], axis=1), plain


def score_kernel(boxes_ref, refs_ref, wts_ref, aux_ref, str_ref, post, mass, ev_ref, acc, off):
    step = pl.program_id(0)
    owned = boxes_ref.shape[0]
    half = str_ref.shape[1]

    @pl.when(step == 0)
    def _():
        acc[...] = jnp.zeros_like(acc)
        off[...] = jnp.zeros_like(off)

    @pl.when(step >= 0)
    def _():
        wts = wts_ref[0]
        lane = lax.broadcasted_iota(jnp.int32, (owned, STEP), 1)
        spread = jnp.broadcast_to(wts[:, 0:1], (owned, STEP))
        for c in range(1, STEP_CYCLES):
            spread = jnp.where(lane >= c * ANGLES, wts[:, c : c + 1], spread)
        scaled = boxes_ref[...].astype(jnp.float32) * spread
        high = scaled.astype(jnp.bfloat16)
        rest = (scaled - high.astype(jnp.float32)).astype(jnp.bfloat16)
        lhs = jnp.concatenate([high, rest], axis=0)
        fan, plain = fan_out(refs_ref[...].astype(jnp.float32), 1)
        total = off[...]
        for c in range(STEP_CYCLES):
            piece = plain[c * ANGLES : (c + 1) * ANGLES]
            total = total + wts[:, c : c + 1] * jnp.sum(piece * piece, axis=0, keepdims=True)
        off[...] = total
        for q in range(COARSE):
            acc[q] += jnp.dot(
                lhs, roll_rows(fan, SHIFT * FINE * q), preferred_element_type=jnp.float32
            )

    @pl.when(step == STEPS - 1)
    def _():
        aux = aux_ref[...]
        live = aux[:, ROTATIONS : ROTATIONS + 1]
        wsum = aux[:, ROTATIONS + 1 : ROTATIONS + 2]
        low = lax.broadcasted_iota(jnp.int32, (owned, half), 1) < owned
        base = -0.5 * off[...]
        strength = str_ref[...]
        top = None
        for q in range(COARSE):
            for t in range(FINE // 2):
                r = q * FINE + 2 * t
                cols = slice(t * half, (t + 1) * half)
                turn = jnp.where(low, aux[:, r : r + 1], aux[:, r + 1 : r + 2])
                score = acc[q, :owned, cols] + acc[q, owned:, cols] + base + turn * strength
                acc[q, :owned, cols] = score
                top = score if top is None else jnp.maximum(top, score)
        top = jnp.max(top, axis=1, keepdims=True)
        norm = jnp.zeros((owned, half), jnp.float32)
        for q in range(COARSE):
            for t in range(FINE // 2):
                cols = slice(t * half, (t + 1) * half)
                term = jnp.exp(acc[q, :owned, cols] - top)
                acc[q, :owned, cols] = term
                norm = norm + term
        norm = jnp.sum(norm, axis=1, keepdims=True)
        ev_ref[...] = jnp.where(live > 0.0, (top + jnp.log(norm)) / (ANGLES * wsum), 0.0)
        seen = jnp.zeros((owned, half), jnp.float32)

        def weight(q, t):
            cols = slice(t * half, (t + 1) * half)
            value = jnp.where(live > 0.0, acc[q, :owned, cols] / norm, 0.0)
            return value.astype(jnp.bfloat16).astype(jnp.float32)

        for q in range(0, COARSE, 2):
            for t in range(FINE // 2):
                first, second = weight(q, t), weight(q + 1, t)
                seen = seen + first + second
                even = jnp.where(low, first, pltpu.roll(second, half // 2, 1))
                odd = jnp.where(low, pltpu.roll(first, half // 2, 1), second)
                cols = slice(q // 2 * half, (q // 2 + 1) * half)
                post[2 * t * owned : (2 * t + 1) * owned, cols] = even.astype(jnp.bfloat16)
                post[(2 * t + 1) * owned : (2 * t + 2) * owned, cols] = odd.astype(jnp.bfloat16)
        seen = jnp.sum(seen, axis=0, keepdims=True)
        mass[...] = seen + pltpu.roll(seen, half // 2, 1)


def turned_sums(boxes, post):
    half = 2 * boxes.shape[0]
    fan, _unused = fan_out(boxes.astype(jnp.float32), -1)
    sums = jnp.dot(fan, post, preferred_element_type=jnp.float32)
    both = sums[:, :half]
    for p in range(1, COARSE // 2):
        both = both + roll_rows(sums[:, p * half : (p + 1) * half], -2 * p * SHIFT * FINE)
    whole = both + pltpu.roll(roll_rows(both, -SHIFT * FINE), half // 2, 1)
    return whole.T


def plain_sums_kernel(width, boxes_ref, post_ref, mass_ref, out_ref):
    turned = turned_sums(boxes_ref[...], post_ref[...])
    classes = out_ref.shape[2]
    mass = jnp.broadcast_to(mass_ref[...], (128, 128)).T
    for h in range(2):
        rows = turned[h * classes : (h + 1) * classes]
        tail = mass[h * classes : (h + 1) * classes, : out_ref.shape[3] - width]
        for j in range(STEP // width):
            out_ref[j, h, :, :width] = rows[:, j * width : (j + 1) * width]
            out_ref[j, h, :, width:] = tail


def plain_sums(boxes, post, mass, classes, peers):
    width = CYCLES // peers * ANGLES
    padded = (width + 1 + 127) // 128 * 128
    return pl.pallas_call(
        functools.partial(plain_sums_kernel, width),
        grid=(STEPS,),
        in_specs=[
            pl.BlockSpec((boxes.shape[0], STEP), lambda i: (0, i)),
            pl.BlockSpec(post.shape, lambda i: (0, 0)),
            pl.BlockSpec(mass.shape, lambda i: (0, 0)),
        ],
        out_specs=pl.BlockSpec((STEP // width, 2, classes, padded), lambda i: (i, 0, 0, 0)),
        out_shape=jax.ShapeDtypeStruct((peers, 2, classes, padded), jnp.float32),
    )(boxes, post, mass)


def scores(boxes, refs, wts, aux, strength):
    owned, classes, half = boxes.shape[0], refs.shape[0], strength.shape[1]
    whole = lambda shape: pl.BlockSpec(shape, lambda i: (0, 0))
    post = (FINE * owned, COARSE * classes)
    return pl.pallas_call(
        score_kernel,
        grid=(STEPS,),
        in_specs=[
            pl.BlockSpec((owned, STEP), lambda i: (0, i)),
            pl.BlockSpec((classes, STEP), lambda i: (0, i)),
            pl.BlockSpec((1, owned, STEP_CYCLES), lambda i: (i, 0, 0)),
            whole(aux.shape),
            whole((1, half)),
        ],
        out_specs=[whole(post), whole((1, half)), whole((owned, 1))],
        out_shape=[
            jax.ShapeDtypeStruct(post, jnp.bfloat16),
            jax.ShapeDtypeStruct((1, half), jnp.float32),
            jax.ShapeDtypeStruct((owned, 1), jnp.float32),
        ],
        scratch_shapes=[
            pltpu.VMEM((COARSE, 2 * owned, FINE * classes), jnp.float32),
            pltpu.VMEM((owned, half), jnp.float32),
        ],
        compiler_params=pltpu.CompilerParams(
            dimension_semantics=("arbitrary",), vmem_limit_bytes=40 * 1024 * 1024
        ),
    )(boxes, refs, wts, aux, strength)


MESH = pl.DeviceIdType.MESH
CHUNKS = 4


def greet(devices):
    barrier = pltpu.get_barrier_semaphore()
    for device in devices:
        pl.semaphore_signal(barrier, inc=1, device_id=device, device_id_type=MESH)
    pl.semaphore_wait(barrier, len(devices))


def gather_kernel(peers, refs_ref, row_ref, all_refs, all_rows, local, send, recv):
    mine, core = lax.axis_index("particle"), lax.axis_index("classes")
    partner = {"classes": 1 - core}
    others = [{"particle": lax.rem(mine + d, peers)} for d in range(1, peers)]
    greet([partner] + others)
    copies = [
        pltpu.make_async_remote_copy(
            src_ref=refs_ref, dst_ref=all_refs.at[core], send_sem=send.at[0], recv_sem=recv.at[0],
            device_id=partner, device_id_type=MESH,
        ),
        pltpu.make_async_remote_copy(
            src_ref=row_ref, dst_ref=all_rows.at[peers], send_sem=send.at[1], recv_sem=recv.at[1],
            device_id=partner, device_id_type=MESH,
        ),
    ]
    for d, other in enumerate(others):
        copies.append(
            pltpu.make_async_remote_copy(
                src_ref=row_ref, dst_ref=all_rows.at[mine], send_sem=send.at[2 + d],
                recv_sem=recv.at[2 + d], device_id=other, device_id_type=MESH,
            )
        )
    for copy in copies:
        copy.start()
    own = [
        pltpu.make_async_copy(refs_ref, all_refs.at[core], local.at[0]),
        pltpu.make_async_copy(row_ref, all_rows.at[mine], local.at[1]),
    ]
    for copy in own:
        copy.start()
    for copy in own + copies:
        copy.wait()


def gathered(refs, row, peers):
    return pl.pallas_call(
        functools.partial(gather_kernel, peers),
        in_specs=[pl.BlockSpec(memory_space=pltpu.VMEM)] * 2,
        out_specs=[pl.BlockSpec(memory_space=pltpu.VMEM)] * 2,
        out_shape=[
            jax.ShapeDtypeStruct((2,) + refs.shape, refs.dtype),
            jax.ShapeDtypeStruct((peers + 1,) + row.shape, row.dtype),
        ],
        scratch_shapes=[
            pltpu.SemaphoreType.DMA((2,)),
            pltpu.SemaphoreType.DMA((peers + 1,)),
            pltpu.SemaphoreType.DMA((peers + 1,)),
        ],
        compiler_params=pltpu.CompilerParams(collective_id=0, has_side_effects=True),
    )(refs, row)


def scatter_kernel(depth, parts, out, pair_in, side_out, side_in, line_out, line_in,
                   pair_send, pair_recv, side_send, side_recv, line_send, line_recv):
    mine, core = lax.axis_index("particle"), lax.axis_index("classes")
    level, side = mine // 2, lax.rem(mine, 2)
    partner = {"classes": 1 - core}
    across = {"particle": level * 2 + 1 - side}
    levels = [lax.rem(level + d, depth) for d in range(1, depth)]
    line = [{"particle": other * 2 + side} for other in levels]
    greet([partner, across] + line)
    rows = out.shape[0] // CHUNKS
    pair, cross, lines = [], [], []
    for j in range(CHUNKS):
        copy = pltpu.make_async_remote_copy(
            src_ref=parts.at[:, :, 1 - core, j * rows : (j + 1) * rows], dst_ref=pair_in.at[j],
            send_sem=pair_send.at[j], recv_sem=pair_recv.at[j], device_id=partner,
            device_id_type=MESH,
        )
        copy.start()
        pair.append(copy)
    for j in range(CHUNKS):
        span = slice(j * rows, (j + 1) * rows)
        pair[j].wait_recv()
        side_out[j] = parts[:, 1 - side, core, span] + pair_in[j, :, 1 - side]
        copy = pltpu.make_async_remote_copy(
            src_ref=side_out.at[j], dst_ref=side_in.at[j], send_sem=side_send.at[j],
            recv_sem=side_recv.at[j], device_id=across, device_id_type=MESH,
        )
        copy.start()
        cross.append(copy)
        line_out[j] = parts[:, side, core, span] + pair_in[j, :, side]
    for j in range(CHUNKS):
        cross[j].wait_recv()
        line_out[j] = line_out[j] + side_in[j]
        for d in range(depth - 1):
            copy = pltpu.make_async_remote_copy(
                src_ref=line_out.at[j, levels[d]], dst_ref=line_in.at[j, d],
                send_sem=line_send.at[j, d], recv_sem=line_recv.at[j, d], device_id=line[d],
                device_id_type=MESH,
            )
            copy.start()
            lines.append(copy)
    for j in range(CHUNKS):
        total = line_out[j, level]
        for d in range(depth - 1):
            lines[j * (depth - 1) + d].wait_recv()
            total = total + line_in[j, d]
        out[j * rows : (j + 1) * rows] = total
    for copy in pair + cross + lines:
        copy.wait_send()


def scattered(parts):
    peers, _, classes, width = parts.shape
    depth = peers // 2
    rows = classes // CHUNKS
    sems = pltpu.SemaphoreType.DMA((CHUNKS,))
    line_sems = pltpu.SemaphoreType.DMA((CHUNKS, max(depth - 1, 1)))
    return pl.pallas_call(
        functools.partial(scatter_kernel, depth),
        in_specs=[pl.BlockSpec(memory_space=pltpu.VMEM)],
        out_specs=pl.BlockSpec(memory_space=pltpu.VMEM),
        out_shape=jax.ShapeDtypeStruct((classes, width), jnp.float32),
        scratch_shapes=[
            pltpu.VMEM((CHUNKS, depth, 2, rows, width), jnp.float32),
            pltpu.VMEM((CHUNKS, depth, rows, width), jnp.float32),
            pltpu.VMEM((CHUNKS, depth, rows, width), jnp.float32),
            pltpu.VMEM((CHUNKS, depth, rows, width), jnp.float32),
            pltpu.VMEM((CHUNKS, max(depth - 1, 1), rows, width), jnp.float32),
            sems, sems, sems, sems, line_sems, line_sems,
        ],
        compiler_params=pltpu.CompilerParams(
            collective_id=1, has_side_effects=True, vmem_limit_bytes=48 * 1024 * 1024
        ),
    )(parts.reshape(depth, 2, 2, classes, width))


def sums_kernel(peers, boxes, post, mass, refs, out, pair_out, pair_in, keep, side_out, side_in,
                line_in, mass_in, column, pair_send, pair_recv, side_send, side_recv, line_send,
                line_recv, mass_send, mass_recv):
    mine, core = lax.axis_index("particle"), lax.axis_index("classes")
    depth, width, classes = peers // 2, out.shape[1], out.shape[0]
    level, side = mine // 2, lax.rem(mine, 2)
    place = mine * 2 + core
    partner = {"classes": 1 - core}
    across = {"particle": level * 2 + 1 - side}
    everyone = []
    for e in range(1, 2 * peers):
        there = lax.rem(place + e, 2 * peers)
        everyone.append({"particle": there // 2, "classes": lax.rem(there, 2)})
    greet(everyone)
    started, masses = [], []

    def send(src, dst, sends, recvs, device):
        copy = pltpu.make_async_remote_copy(
            src_ref=src, dst_ref=dst, send_sem=sends, recv_sem=recvs, device_id=device,
            device_id_type=MESH,
        )
        copy.start()
        started.append(copy)
        return copy

    for e, device in enumerate(everyone):
        masses.append(
            send(mass, mass_in.at[e], mass_send.at[e], mass_recv.at[e], device)
        )
    turns = list(range(1, depth)) + [0]
    blocks = [(i, d, True) for i, d in enumerate(turns)] + [(i, d, False) for i, d in enumerate(turns)]
    pair, cross, lines = [], [], []

    def advance(n):
        i, d, away = blocks[n]
        pair[n].wait_recv()
        if away:
            side_out[i] = keep[n] + pair_in[n]
            cross.append(
                send(side_out.at[i], side_in.at[i], side_send.at[i], side_recv.at[i], across)
            )
            return
        cross[i].wait_recv()
        keep[n] = keep[n] + pair_in[n] + side_in[i]
        if d > 0:
            there = {"particle": lax.rem(level + d, depth) * 2 + side}
            lines.append(
                send(keep.at[n], line_in.at[i], line_send.at[i], line_recv.at[i], there)
            )

    for n, (i, d, away) in enumerate(blocks):
        shard = lax.rem(level + d, depth) * 2 + (1 - side if away else side)

        @pl.loop(0, width // STEP)
        def _(part):
            source = pl.multiple_of(shard * width + part * STEP, 128)
            target = pl.multiple_of(part * STEP, 128)
            turned = turned_sums(boxes[:, pl.ds(source, STEP)], post[...])
            low, high = turned[:classes], turned[classes : 2 * classes]
            keep[n, :, pl.ds(target, STEP)] = jnp.where(core == 0, low, high)
            pair_out[n, :, pl.ds(target, STEP)] = jnp.where(core == 0, high, low)

        pair.append(send(pair_out.at[n], pair_in.at[n], pair_send.at[n], pair_recv.at[n], partner))
        if n > 0:
            advance(n - 1)
    advance(len(blocks) - 1)
    weight = mass[...]
    for e, copy in enumerate(masses):
        copy.wait_recv()
        weight = weight + mass_in[e]
    column[...] = jnp.broadcast_to(weight, column.shape).T
    scale = column[pl.ds(pl.multiple_of(core * classes, 8), classes), :]
    total = keep[len(blocks) - 1]
    for i in range(depth - 1):
        lines[i].wait_recv()
        total = total + line_in[i]
    base = refs[:, pl.ds(pl.multiple_of(mine * width, 128), width)].astype(jnp.float32)
    out[...] = (total + base) / (scale[:, 0:1] + 1.0)
    for copy in started:
        copy.wait_send()


def fused_sums(boxes, post, mass, refs, peers):
    classes, width, depth = refs.shape[0], CYCLES // peers * ANGLES, peers // 2
    room = lambda count: pltpu.VMEM((count, classes, width), jnp.float32)
    sems = lambda count: pltpu.SemaphoreType.DMA((count,))
    others = 2 * peers - 1
    return pl.pallas_call(
        functools.partial(sums_kernel, peers),
        in_specs=[pl.BlockSpec(memory_space=pltpu.VMEM)] * 4,
        out_specs=pl.BlockSpec(memory_space=pltpu.VMEM),
        out_shape=jax.ShapeDtypeStruct((classes, width), jnp.float32),
        scratch_shapes=[
            room(peers), room(peers), room(peers), room(depth), room(depth), room(depth - 1),
            pltpu.VMEM((others,) + mass.shape, jnp.float32),
            pltpu.VMEM((mass.shape[1], mass.shape[1]), jnp.float32),
            sems(peers), sems(peers), sems(depth), sems(depth), sems(depth - 1), sems(depth - 1),
            sems(others), sems(others),
        ],
        compiler_params=pltpu.CompilerParams(
            collective_id=2, has_side_effects=True, vmem_limit_bytes=48 * 1024 * 1024
        ),
    )(boxes, post, mass, refs)


PARTS = 4
QUARTERS = 4
TILES = 6
GROUPS = ((0, 1, 2, 3), (4, 5))
APART = ANGLES // QUARTERS
SLOTS = 128
LEVELS = 32767.0


def turned(block, shift):
    shift = shift % ANGLES
    if shift == 0:
        return block
    return jnp.concatenate([block[ANGLES - shift :], block[: ANGLES - shift]], axis=0)


def flip(block):
    return pltpu.roll(block, 64, 1)


def low_lanes(rows, width=64, period=128):
    lane = lax.broadcasted_iota(jnp.int32, (rows, 128), 1)
    return lax.rem(lane, period) < width


def encode(block, codes, scales):
    largest = jnp.maximum(jnp.max(jnp.abs(block), axis=0, keepdims=True), 1e-30)
    codes[...] = jnp.round(block * (LEVELS / largest)).astype(jnp.int32).astype(jnp.int16)
    scales[0:1, :] = largest * (1.0 / LEVELS)


def refs_fan(refs, fans, energies, p):
    cols = slice(p * STEP, (p + 1) * STEP)
    rows = refs[:, cols].astype(jnp.float32)
    plain = jnp.concatenate([rows, rows], axis=0).T
    low = low_lanes(ANGLES)
    for c in range(PARTS):
        base = p * STEP + c * ANGLES
        piece = plain[c * ANGLES : (c + 1) * ANGLES]
        energies[p * PARTS + c : p * PARTS + c + 1, :] = jnp.sum(piece * piece, axis=0, keepdims=True)
        both = jnp.where(low, piece, turned(piece, APART))
        fans[0, base : base + ANGLES, :] = both.astype(jnp.bfloat16)
        fans[1, base : base + ANGLES, :] = turned(both, SHIFT).astype(jnp.bfloat16)


def boxes_fan(boxes, fans, p):
    cols = slice(p * STEP, (p + 1) * STEP)
    plain = boxes[:, cols].astype(jnp.float32).T
    fans[0, cols, :] = plain.astype(jnp.bfloat16)
    for c in range(PARTS):
        base = p * STEP + c * ANGLES
        piece = plain[c * ANGLES : (c + 1) * ANGLES]
        fans[1, base : base + ANGLES, :] = turned(piece, -SHIFT).astype(jnp.bfloat16)


def score_tiles(boxes, fans, wide, tiles, cycles):
    totals = [None] * len(tiles)
    blank = jnp.zeros((256 - ANGLES, 256), jnp.bfloat16)
    for c in range(cycles):
        base, window = c * ANGLES, c // 2 * 2 * ANGLES + c % 2 * 128
        factor = wide[c]
        factor = jnp.concatenate([factor, factor], axis=1)
        for n, f in enumerate(tiles):
            piece = fans[f % 2, base : base + ANGLES, :]
            shift = SHIFT * (f - f % 2)
            piece = jnp.concatenate(
                [turned(piece, shift), turned(piece, shift + 2 * APART)], axis=1
            )
            piece = jnp.concatenate([piece, blank] if c % 2 == 0 else [blank, piece], axis=0)
            part = factor * jnp.dot(
                boxes[:, window : window + 256], piece, preferred_element_type=jnp.float32
            )
            totals[n] = part if totals[n] is None else totals[n] + part
    return totals


def class_sums(fans, post, shard):
    rows = []
    for c in range(PARTS):
        base = pl.multiple_of(shard * STEP + c * ANGLES, 64)
        even = fans[0, pl.ds(base, ANGLES), :]
        odd = fans[1, pl.ds(base, ANGLES), :]
        rows.append(
            jnp.concatenate(
                [turned(x, -2 * SHIFT * s) for s in range(TILES // 2) for x in (even, odd)], axis=1
            )
        )
    sums = jnp.dot(jnp.concatenate(rows, axis=0), post[...], preferred_element_type=jnp.float32)
    low, first = low_lanes(ANGLES), low_lanes(ANGLES, 32, 64)
    both = []
    for c in range(PARTS):
        piece = sums[c * ANGLES : (c + 1) * ANGLES]
        b = piece[:, :128] + turned(piece[:, 128:], -2 * APART)
        both.append((b, turned(b, -APART)))

    def pair(i, j):
        return jnp.where(low, both[i][0], both[j][1]) + flip(jnp.where(low, both[j][0], both[i][1]))

    a, b = pair(0, 2), pair(1, 3)
    return jnp.where(first, a, pltpu.roll(b, 32, 1)), jnp.where(first, pltpu.roll(a, 96, 1), b)


def whole_kernel(
    peers, boxes, counts, places_in, turns_in, refs, weights_in, strength_in, out, evidence,
    places, turns, weights, strength, xs, rs, own, cards, duo, ref_fans, box_fans, energies, base_refs, wide, mine_s, theirs_s, terms,
    post, masses, y_out, y_out_s, y_in, y_in_s, keep, near_out, near_out_s, near_in, near_in_s, z_out, z_out_s, z_in, z_in_s, pair_out, pair_in, scale, totals,
    small_local, box_local, ref_local, own_local, box_send, box_recv, ref_send, ref_recv, card_send, card_recv,
    duo_send, duo_recv, score_send, score_recv, mass_send, mass_recv, y_send, y_recv, ys_send, ys_recv,
    near_send, near_recv, z_send, z_recv, zs_send, zs_recv, pair_send, pair_recv,
):
    mine, core = lax.axis_index("particle"), lax.axis_index("classes")
    depth, owned, classes = peers // 2, boxes.shape[0], refs.shape[0]
    level, side = mine // 2, lax.rem(mine, 2)
    partner = {"classes": 1 - core}
    across = {"particle": level * 2 + 1 - side}
    others = [{"particle": lax.rem(mine + d, peers)} for d in range(1, peers)]
    near, far = level + 1 - 2 * lax.rem(level, 2), lax.rem(level + 2, depth)
    levels = [lax.rem(near + 2, depth), far, near, level]
    diagonal = [{"particle": there * 2 + side, "classes": 1 - core} for there in (far, near)]
    straight = [{"particle": there * 2 + side} for there in (far, near)]
    barrier = pltpu.get_barrier_semaphore()
    friends = [partner] + others + diagonal
    for device in friends:
        pl.semaphore_signal(barrier, inc=1, device_id=device, device_id_type=MESH)
    box_rows = pl.ds(pl.multiple_of(core * owned, owned), owned)
    ref_rows = pl.ds(pl.multiple_of(core * classes, classes), classes)
    local = []
    for p in range(peers):
        source = pl.ds(pl.multiple_of((2 * p + core) * STEP, 128), STEP)
        target = pl.ds(p * STEP, STEP)
        local.append(
            pltpu.make_async_copy(refs.at[:, source], rs.at[ref_rows, target], ref_local.at[p])
        )
        local.append(
            pltpu.make_async_copy(boxes.at[:, source], xs.at[box_rows, target], box_local.at[p])
        )
    width = 2 * STEP
    own_copy = pltpu.make_async_copy(
        refs.at[:, pl.ds(pl.multiple_of(mine * width, 128), width)], own, own_local.at[0]
    )
    small = [
        pltpu.make_async_copy(source, target, small_local.at[n])
        for n, (source, target) in enumerate(
            [
                (places_in, places), (turns_in, turns), (weights_in, weights), (strength_in, strength),
            ]
        )
    ]
    for copy in small + local + [own_copy]:
        copy.start()
    for copy in small:
        copy.wait()
    card = jnp.zeros((8, 128), jnp.float32)
    cards[mine] = card
    slot = lax.broadcasted_iota(jnp.int32, (1, owned), 1)
    cards[mine, 0:1, :CYCLES] = weights[...]
    cards[mine, 1:2, :owned] = places[...].astype(jnp.float32)
    cards[mine, 2:3, :owned] = turns[...].astype(jnp.float32)
    cards[mine, 3:4, :owned] = jnp.where(slot < counts[0], 1.0, 0.0)
    cards[mine, 4:5, :classes] = strength[...]
    duo[core] = cards[mine]

    started = []

    def send(src, dst, sends, recvs, device):
        copy = pltpu.make_async_remote_copy(
            src_ref=src, dst_ref=dst, send_sem=sends, recv_sem=recvs, device_id=device,
            device_id_type=MESH,
        )
        copy.start()
        started.append(copy)
        return copy

    pl.semaphore_wait(barrier, len(friends))
    card_copies = [
        send(cards.at[mine, 0:1], cards.at[mine, 0:1], card_send.at[d], card_recv.at[d], device)
        for d, device in enumerate(others)
    ]
    duo_copy = send(duo.at[core], duo.at[core], duo_send.at[0], duo_recv.at[0], partner)
    ref_copies, box_copies = [], []
    for p in range(peers):
        source = pl.ds(pl.multiple_of((2 * p + 1 - core) * STEP, 128), STEP)
        target = pl.ds(p * STEP, STEP)
        ref_copies.append(
            send(refs.at[:, source], rs.at[ref_rows, target], ref_send.at[p], ref_recv.at[p], partner)
        )
    for p in range(peers):
        source = pl.ds(pl.multiple_of((2 * p + 1 - core) * STEP, 128), STEP)
        target = pl.ds(p * STEP, STEP)
        box_copies.append(
            send(boxes.at[:, source], xs.at[box_rows, target], box_send.at[p], box_recv.at[p], partner)
        )
    own_copy.wait()
    for h in range(2):
        for c in range(PARTS):
            base = (h * PARTS + c) * ANGLES
            base_refs[h, c * classes : (c + 1) * classes, :] = own[:, base : base + ANGLES].astype(
                jnp.float32
            )
    for copy in local:
        copy.wait()
    for p in range(peers):
        ref_copies[p].wait_recv()
        refs_fan(rs, ref_fans, energies, p)

    duo_copy.wait_recv()
    facts = duo[0] + flip(duo[1])
    facts = jnp.concatenate([facts] * (SLOTS // 8), axis=0).T
    place, turn, live = facts[:, 1:2], facts[:, 2:3], facts[:, 3:4]
    force = duo[0, 4:5, :] + pltpu.roll(duo[1, 4:5, :], classes, 1)
    force = force + flip(force)
    lane = lax.broadcasted_iota(jnp.int32, (SLOTS, 128), 1).astype(jnp.float32)
    swing = jnp.cos(TWO_PI * (lane - turn) / ROTATIONS)
    for copy in card_copies:
        copy.wait_recv()
    spread = jnp.zeros((SLOTS, 128), jnp.float32)
    for g in range(peers):
        spread = jnp.where(place == float(g), cards[g, 0:1, :], spread)
    wsum = jnp.sum(spread, axis=1, keepdims=True)
    spread = jnp.where(core == 0, spread, pltpu.roll(spread, 128 - PARTS, 1))
    base = jnp.zeros((SLOTS, 128), jnp.float32)
    for c in range(CYCLES // 2):
        place = c // PARTS * 2 * PARTS + c % PARTS
        factor = jnp.broadcast_to(spread[:, place : place + 1], (SLOTS, 128))
        wide[c] = factor
        base = base + factor * energies[c : c + 1, :]
    base = -0.5 * base
    for copy in box_copies:
        copy.wait_recv()

    low = low_lanes(SLOTS)
    score_copies, tops, norms = [], [], []

    def finish(f):
        score_copies[f].wait_recv()
        values = []
        for t in range(2):
            cols = slice(t * 128, (t + 1) * 128)
            r = f + 2 * t * TILES
            prior = jnp.where(low, swing[:, r : r + 1], swing[:, r + TILES : r + TILES + 1]) * force
            values.append(mine_s[f, :, cols] + theirs_s[f, :, cols] + prior)
        top = jnp.max(jnp.maximum(values[0], values[1]), axis=1, keepdims=True)
        values = [jnp.exp(v - top) for v in values]
        for t in range(2):
            terms[f, :, t * 128 : (t + 1) * 128] = values[t]
        tops.append(top)
        norms.append(jnp.sum(values[0] + values[1], axis=1, keepdims=True))

    for g, tiles in enumerate(GROUPS):
        for f, tile in zip(tiles, score_tiles(xs, ref_fans, wide, tiles, CYCLES // 2)):
            mine_s[f] = tile + jnp.concatenate([base, base], axis=1)
        for f in tiles:
            score_copies.append(
                send(mine_s.at[f], theirs_s.at[f], score_send.at[f], score_recv.at[f], partner)
            )
        if g > 0:
            for f in GROUPS[g - 1]:
                finish(f)
    for p in range(peers):
        boxes_fan(xs, box_fans, p)
    for f in GROUPS[-1]:
        finish(f)
    top = functools.reduce(jnp.maximum, tops)
    factors = [jnp.exp(t - top) for t in tops]
    norm = sum(n * s for n, s in zip(norms, factors))
    for f in range(TILES):
        factor = jnp.where(live > 0.0, factors[f] / norm, 0.0)
        post[f * SLOTS : (f + 1) * SLOTS, :] = (terms[f] * factor).astype(jnp.bfloat16)

    def mass_and_evidence():
        mass = jnp.zeros((8, 256), jnp.float32)
        for f in range(TILES):
            value = post[f * SLOTS : (f + 1) * SLOTS, :].astype(jnp.float32)
            for i in range(SLOTS // 8):
                mass = mass + value[i * 8 : (i + 1) * 8]
        mass = mass[:, :128] + mass[:, 128:]
        mass = mass + flip(mass)
        masses[mine] = jnp.broadcast_to(jnp.sum(mass, axis=0, keepdims=True), (8, 128))
        for d, device in enumerate(others):
            mass_copies.append(
                send(
                    masses.at[mine, 0:1], masses.at[mine, 0:1], mass_send.at[d], mass_recv.at[d],
                    device,
                )
            )
        proof = jnp.where(live > 0.0, (top + jnp.log(norm)) / (ANGLES * wsum), 0.0)
        proof = jnp.broadcast_to(proof, (SLOTS, 128)).T[0:1]
        evidence[...] = jnp.where(core == 0, proof, flip(proof))[:, :owned]

    mass_copies = []
    y_copies, z_copies, near_copies, waited = [], [[], []], [], set()

    def away(i, blocks):
        for h, value in enumerate(blocks):
            encode(value, y_out.at[i, h], y_out_s.at[i, h : h + 1])
        y_copies.append(
            [send(y_out_s.at[i, 0:2], y_in_s.at[i, 0:2], ys_send.at[i], ys_recv.at[i], across)]
            + [
                send(y_out.at[i, h], y_in.at[i, h], y_send.at[i, n], y_recv.at[i, n], across)
                for n, h in enumerate([1 - core, core])
            ]
        )

    def home(i, blocks):
        for h, value in enumerate(blocks):
            keep[i, h] = value

    halves = [1 - core, core]

    def arrived(copies):
        for copy in copies:
            if id(copy) not in waited:
                copy.wait_recv()
                waited.add(id(copy))

    def summed(i, n):
        half = halves[n]
        arrived(y_copies[i][: n + 2])
        row = jnp.where(half == 0, y_in_s[i, 0:1, :], y_in_s[i, 1:2, :])
        codes = y_in[i, half].astype(jnp.int32).astype(jnp.float32)
        return keep[i, half] + codes * row

    def to_near(n):
        half = halves[n]
        encode(summed(0, n), near_out.at[half], near_out_s.at[half])
        near_copies.append(
            [
                send(
                    near_out_s.at[half, 0:1], near_in_s.at[half, 0:1], near_send.at[n, 1],
                    near_recv.at[n, 1], straight[1],
                ),
                send(
                    near_out.at[half], near_in.at[half], near_send.at[n, 0], near_recv.at[n, 0],
                    straight[1],
                ),
            ]
        )

    def to_owner(j, n):
        half = halves[n]
        total = summed(j + 1, n)
        if j == 0:
            arrived(near_copies[n])
            codes = near_in[half].astype(jnp.int32).astype(jnp.float32)
            total = total + codes * near_in_s[half, 0:1, :]
        encode(total, z_out.at[j, half], z_out_s.at[j, half])
        device = diagonal[j] if n == 0 else straight[j]
        z_copies[j].append(
            send(
                z_out_s.at[j, half, 0:1], z_in_s.at[j, core, 0:1], zs_send.at[j, n],
                zs_recv.at[j, n], device,
            )
        )
        z_copies[j].append(
            send(z_out.at[j, half], z_in.at[j, core], z_send.at[j, n], z_recv.at[j, n], device)
        )

    shards = lambda i: (levels[i] * 2 + 1 - side, levels[i] * 2 + side)
    away(0, class_sums(box_fans, post, shards(0)[0]))
    for i in range(1, depth):
        held = class_sums(box_fans, post, shards(i - 1)[1])
        away(i, class_sums(box_fans, post, shards(i)[0]))
        home(i - 1, held)
        if i == 1:
            mass_and_evidence()
        if i < depth - 1:
            to_near(i - 1)
    home(depth - 1, class_sums(box_fans, post, shards(depth - 1)[1]))
    for j in range(2):
        for n in range(2):
            to_owner(j, n)

    for copy in mass_copies:
        copy.wait_recv()
    weight = masses[0, 0:1, :]
    for g in range(1, peers):
        weight = weight + masses[g, 0:1, :]
    weight = jnp.broadcast_to(weight, (8, 128))
    first = low_lanes(8, 32, 64)
    weight = jnp.where(
        core == 0,
        jnp.where(first, weight, pltpu.roll(weight, 32, 1)),
        jnp.where(first, pltpu.roll(weight, 96, 1), weight),
    )
    scale[...] = jnp.concatenate([weight] * 16, axis=0).T + 1.0

    def crossed(j, n):
        half = halves[n]
        arrived(z_copies[j][2 * n : 2 * n + 2])
        return z_in[j, half].astype(jnp.int32).astype(jnp.float32) * z_in_s[j, half, 0:1, :]

    def store(half, value):
        result = (value.T + base_refs[half]) / scale[:, 0:1]
        for c in range(PARTS):
            out[:, half * PARTS + c, :] = result[c * classes : (c + 1) * classes]

    pair_out[...] = summed(depth - 1, 0)
    pair_copy = send(pair_out, pair_in, pair_send.at[0], pair_recv.at[0], partner)
    held = summed(depth - 1, 1)
    for n in range(2):
        totals[n] = crossed(1, n)
    totals[1] = totals[1] + held
    pair_copy.wait_recv()
    totals[0] = totals[0] + pair_in[...]
    for n in range(2):
        store(halves[n], totals[n] + crossed(0, n))
    for copy in started:
        copy.wait_send()


def whole(boxes, counts, places, turns, refs, weights, strength, peers):
    given = (boxes, places, turns, refs, weights, strength)
    pinned = [pltpu.with_memory_space_constraint(x, pltpu.HBM) for x in given]
    classes, depth = refs.shape[0], peers // 2
    half = CYCLES * ANGLES // 2
    f32, bf16, i16 = jnp.float32, jnp.bfloat16, jnp.int16
    room = lambda dtype, *shape: pltpu.VMEM(shape, dtype)
    sems = lambda *shape: pltpu.SemaphoreType.DMA(shape)
    vmem = pl.BlockSpec(memory_space=pltpu.VMEM)
    hbm = pl.BlockSpec(memory_space=pltpu.HBM)
    return pl.pallas_call(
        functools.partial(whole_kernel, peers),
        in_specs=[hbm, pl.BlockSpec(memory_space=pltpu.SMEM)] + [hbm] * 5,
        out_specs=[vmem, vmem],
        out_shape=[
            jax.ShapeDtypeStruct((classes, CYCLES // peers, ANGLES), f32),
            jax.ShapeDtypeStruct((1, boxes.shape[0]), f32),
        ],
        scratch_shapes=[
            pltpu.VMEM(places.shape, places.dtype),
            pltpu.VMEM(turns.shape, turns.dtype), pltpu.VMEM(weights.shape, f32),
            pltpu.VMEM(strength.shape, f32), room(bf16, SLOTS, half), room(bf16, 2 * classes, half), room(bf16, classes, 2 * STEP),
            room(f32, peers, 8, 128), room(f32, 2, 8, 128),
            room(bf16, 2, half, 128), room(bf16, 2, half, 128), room(f32, CYCLES // 2, 128),
            room(f32, 2, 128, ANGLES), room(f32, CYCLES // 2, SLOTS, 128),
            room(f32, TILES, SLOTS, 256), room(f32, TILES, SLOTS, 256), room(f32, TILES, SLOTS, 256),
            room(bf16, TILES * SLOTS, 256), room(f32, peers, 8, 128),
            room(i16, depth, 2, ANGLES, 128), room(f32, depth, 8, 128),
            room(i16, depth, 2, ANGLES, 128), room(f32, depth, 8, 128),
            room(f32, depth, 2, ANGLES, 128),
            room(i16, 2, ANGLES, 128), room(f32, 2, 8, 128), room(i16, 2, ANGLES, 128), room(f32, 2, 8, 128),
            room(i16, 2, 2, ANGLES, 128), room(f32, 2, 2, 8, 128),
            room(i16, 2, 2, ANGLES, 128), room(f32, 2, 2, 8, 128),
            room(f32, ANGLES, 128), room(f32, ANGLES, 128), room(f32, 128, 128), room(f32, 2, ANGLES, 128),
            sems(4), sems(peers), sems(peers), sems(1), sems(peers), sems(peers), sems(peers), sems(peers),
            sems(peers - 1), sems(peers - 1), sems(1), sems(1), sems(TILES), sems(TILES),
            sems(peers - 1), sems(peers - 1), sems(depth, 2), sems(depth, 2), sems(depth), sems(depth),
            sems(2, 2), sems(2, 2), sems(2, 2), sems(2, 2), sems(2, 2), sems(2, 2),
            sems(1), sems(1),
        ],
        compiler_params=pltpu.CompilerParams(
            collective_id=3, has_side_effects=True, vmem_limit_bytes=48 * 1024 * 1024
        ),
    )(pinned[0], counts, *pinned[1:])


def on_device(boxes, counts, destinations, prior_rot, references, cycle_weights, prior_strength):
    peers = lax.axis_size("particle")
    cycle_index = lax.axis_index("particle")
    cycles_dev = CYCLES // peers
    width = cycles_dev * ANGLES
    if width == 2 * STEP:
        new_references, evidence = whole(
            boxes, counts, destinations[None, :], prior_rot[None, :], references,
            cycle_weights, prior_strength[None, :], peers,
        )
        return new_references, evidence[0]
    owned = boxes.shape[0]
    classes_dev = references.shape[0]
    lane_index = lax.axis_index("classes")
    row = jnp.concatenate([cycle_weights[0], prior_strength])
    row = jnp.pad(row, (0, 128 - row.shape[0]))[None, :]
    refs, rows = gathered(references, row, peers)
    refs = refs.reshape(2 * classes_dev, -1)
    group_wts = rows[:peers, 0, :CYCLES]
    other = rows[peers, 0, CYCLES : CYCLES + classes_dev]
    strength = jnp.where(
        lane_index == 0,
        jnp.concatenate([prior_strength, other]),
        jnp.concatenate([other, prior_strength]),
    ).reshape(1, -1)
    mine = destinations[:, None] == jnp.arange(peers, dtype=jnp.int32)[None, :]
    wts = jnp.sum(jnp.where(mine[:, :, None], group_wts[None], 0.0), axis=1)
    live = (jnp.arange(owned, dtype=jnp.int32) < counts[0]).astype(jnp.float32)
    turn_ids = jnp.arange(ROTATIONS, dtype=jnp.float32)
    gap = TWO_PI * (turn_ids[None, :] - prior_rot[:, None].astype(jnp.float32)) / ROTATIONS
    aux = jnp.concatenate([jnp.cos(gap), live[:, None], jnp.sum(wts, axis=1)[:, None]], axis=1)
    wts = jnp.transpose(wts.reshape(owned, STEPS, STEP_CYCLES), (1, 0, 2))
    post, mass, evidence = scores(
        boxes, refs, wts, aux, jnp.concatenate([strength, strength], axis=1)
    )
    if width % STEP == 0:
        new_references = fused_sums(boxes, post, mass, references, peers)
    else:
        sums = scattered(plain_sums(boxes, post, mass, classes_dev, peers))
        own_refs = lax.dynamic_slice_in_dim(references, cycle_index * width, width, 1)
        new_references = (sums[:, :width] + own_refs.astype(jnp.float32)) / (
            sums[:, width : width + 1] + 1.0
        )
    return new_references.reshape(classes_dev, cycles_dev, ANGLES), evidence[:, 0]


def solution(mesh):
    in_specs = (
        P(("groups", "particle", "classes"), None),
        P(("groups", "particle", "classes")),
        P(("groups", "particle", "classes")),
        P(("groups", "particle", "classes")),
        P(("groups", "classes"), None),
        P(("groups", "particle"), None),
        P(("groups", "classes")),
    )
    out_specs = (P(("groups", "classes"), "particle", None), P(("groups", "particle", "classes")))
    return jax.shard_map(
        on_device, mesh=mesh, in_specs=in_specs, out_specs=out_specs, check_vma=False
    )
```

```python
import functools
import math

import jax
import jax.numpy as jnp
from jax import lax
from jax.experimental import pallas as pl
from jax.experimental.pallas import tpu as pltpu
from jax.sharding import PartitionSpec as P

CYCLES = 64
ANGLES = 192
ROTATIONS = 24
FINE = 4
COARSE = ROTATIONS // FINE
SHIFT = ANGLES // ROTATIONS
STEP_CYCLES = 4
STEP = STEP_CYCLES * ANGLES
STEPS = CYCLES // STEP_CYCLES
TWO_PI = 2.0 * math.pi


def roll_rows(block, shift):
    shift = shift % ANGLES
    if shift == 0:
        return block
    pieces = []
    for c in range(STEP_CYCLES):
        base = c * ANGLES
        pieces.append(block[base + ANGLES - shift : base + ANGLES])
        pieces.append(block[base : base + ANGLES - shift])
    return jnp.concatenate(pieces, axis=0)


def fan_out(rows, sign):
    plain = jnp.concatenate([rows, rows], axis=0).T
    low = lax.broadcasted_iota(jnp.int32, plain.shape, 1) < rows.shape[0]
    tiles = [
        jnp.where(low, roll_rows(plain, sign * SHIFT * f), roll_rows(plain, sign * SHIFT * (f + 1)))
        for f in range(0, FINE, 2)
    ]
    return jnp.concatenate([t.astype(jnp.bfloat16) for t in tiles], axis=1), plain


def score_kernel(boxes_ref, refs_ref, wts_ref, aux_ref, str_ref, post, mass, ev_ref, acc, off):
    step = pl.program_id(0)
    owned = boxes_ref.shape[0]
    half = str_ref.shape[1]

    @pl.when(step == 0)
    def _():
        acc[...] = jnp.zeros_like(acc)
        off[...] = jnp.zeros_like(off)

    @pl.when(step >= 0)
    def _():
        wts = wts_ref[0]
        lane = lax.broadcasted_iota(jnp.int32, (owned, STEP), 1)
        spread = jnp.broadcast_to(wts[:, 0:1], (owned, STEP))
        for c in range(1, STEP_CYCLES):
            spread = jnp.where(lane >= c * ANGLES, wts[:, c : c + 1], spread)
        scaled = boxes_ref[...].astype(jnp.float32) * spread
        high = scaled.astype(jnp.bfloat16)
        rest = (scaled - high.astype(jnp.float32)).astype(jnp.bfloat16)
        lhs = jnp.concatenate([high, rest], axis=0)
        fan, plain = fan_out(refs_ref[...].astype(jnp.float32), 1)
        total = off[...]
        for c in range(STEP_CYCLES):
            piece = plain[c * ANGLES : (c + 1) * ANGLES]
            total = total + wts[:, c : c + 1] * jnp.sum(piece * piece, axis=0, keepdims=True)
        off[...] = total
        for q in range(COARSE):
            acc[q] += jnp.dot(
                lhs, roll_rows(fan, SHIFT * FINE * q), preferred_element_type=jnp.float32
            )

    @pl.when(step == STEPS - 1)
    def _():
        aux = aux_ref[...]
        live = aux[:, ROTATIONS : ROTATIONS + 1]
        wsum = aux[:, ROTATIONS + 1 : ROTATIONS + 2]
        low = lax.broadcasted_iota(jnp.int32, (owned, half), 1) < owned
        base = -0.5 * off[...]
        strength = str_ref[...]
        top = None
        for q in range(COARSE):
            for t in range(FINE // 2):
                r = q * FINE + 2 * t
                cols = slice(t * half, (t + 1) * half)
                turn = jnp.where(low, aux[:, r : r + 1], aux[:, r + 1 : r + 2])
                score = acc[q, :owned, cols] + acc[q, owned:, cols] + base + turn * strength
                acc[q, :owned, cols] = score
                top = score if top is None else jnp.maximum(top, score)
        top = jnp.max(top, axis=1, keepdims=True)
        norm = jnp.zeros((owned, half), jnp.float32)
        for q in range(COARSE):
            for t in range(FINE // 2):
                cols = slice(t * half, (t + 1) * half)
                term = jnp.exp(acc[q, :owned, cols] - top)
                acc[q, :owned, cols] = term
                norm = norm + term
        norm = jnp.sum(norm, axis=1, keepdims=True)
        ev_ref[...] = jnp.where(live > 0.0, (top + jnp.log(norm)) / (ANGLES * wsum), 0.0)
        seen = jnp.zeros((owned, half), jnp.float32)

        def weight(q, t):
            cols = slice(t * half, (t + 1) * half)
            value = jnp.where(live > 0.0, acc[q, :owned, cols] / norm, 0.0)
            return value.astype(jnp.bfloat16).astype(jnp.float32)

        for q in range(0, COARSE, 2):
            for t in range(FINE // 2):
                first, second = weight(q, t), weight(q + 1, t)
                seen = seen + first + second
                even = jnp.where(low, first, pltpu.roll(second, half // 2, 1))
                odd = jnp.where(low, pltpu.roll(first, half // 2, 1), second)
                cols = slice(q // 2 * half, (q // 2 + 1) * half)
                post[2 * t * owned : (2 * t + 1) * owned, cols] = even.astype(jnp.bfloat16)
                post[(2 * t + 1) * owned : (2 * t + 2) * owned, cols] = odd.astype(jnp.bfloat16)
        seen = jnp.sum(seen, axis=0, keepdims=True)
        mass[...] = seen + pltpu.roll(seen, half // 2, 1)


def turned_sums(boxes, post):
    half = 2 * boxes.shape[0]
    fan, _unused = fan_out(boxes.astype(jnp.float32), -1)
    sums = jnp.dot(fan, post, preferred_element_type=jnp.float32)
    both = sums[:, :half]
    for p in range(1, COARSE // 2):
        both = both + roll_rows(sums[:, p * half : (p + 1) * half], -2 * p * SHIFT * FINE)
    whole = both + pltpu.roll(roll_rows(both, -SHIFT * FINE), half // 2, 1)
    return whole.T


def plain_sums_kernel(width, boxes_ref, post_ref, mass_ref, out_ref):
    turned = turned_sums(boxes_ref[...], post_ref[...])
    classes = out_ref.shape[2]
    mass = jnp.broadcast_to(mass_ref[...], (128, 128)).T
    for h in range(2):
        rows = turned[h * classes : (h + 1) * classes]
        tail = mass[h * classes : (h + 1) * classes, : out_ref.shape[3] - width]
        for j in range(STEP // width):
            out_ref[j, h, :, :width] = rows[:, j * width : (j + 1) * width]
            out_ref[j, h, :, width:] = tail


def plain_sums(boxes, post, mass, classes, peers):
    width = CYCLES // peers * ANGLES
    padded = (width + 1 + 127) // 128 * 128
    return pl.pallas_call(
        functools.partial(plain_sums_kernel, width),
        grid=(STEPS,),
        in_specs=[
            pl.BlockSpec((boxes.shape[0], STEP), lambda i: (0, i)),
            pl.BlockSpec(post.shape, lambda i: (0, 0)),
            pl.BlockSpec(mass.shape, lambda i: (0, 0)),
        ],
        out_specs=pl.BlockSpec((STEP // width, 2, classes, padded), lambda i: (i, 0, 0, 0)),
        out_shape=jax.ShapeDtypeStruct((peers, 2, classes, padded), jnp.float32),
    )(boxes, post, mass)


def scores(boxes, refs, wts, aux, strength):
    owned, classes, half = boxes.shape[0], refs.shape[0], strength.shape[1]
    whole = lambda shape: pl.BlockSpec(shape, lambda i: (0, 0))
    post = (FINE * owned, COARSE * classes)
    return pl.pallas_call(
        score_kernel,
        grid=(STEPS,),
        in_specs=[
            pl.BlockSpec((owned, STEP), lambda i: (0, i)),
            pl.BlockSpec((classes, STEP), lambda i: (0, i)),
            pl.BlockSpec((1, owned, STEP_CYCLES), lambda i: (i, 0, 0)),
            whole(aux.shape),
            whole((1, half)),
        ],
        out_specs=[whole(post), whole((1, half)), whole((owned, 1))],
        out_shape=[
            jax.ShapeDtypeStruct(post, jnp.bfloat16),
            jax.ShapeDtypeStruct((1, half), jnp.float32),
            jax.ShapeDtypeStruct((owned, 1), jnp.float32),
        ],
        scratch_shapes=[
            pltpu.VMEM((COARSE, 2 * owned, FINE * classes), jnp.float32),
            pltpu.VMEM((owned, half), jnp.float32),
        ],
        compiler_params=pltpu.CompilerParams(
            dimension_semantics=("arbitrary",), vmem_limit_bytes=40 * 1024 * 1024
        ),
    )(boxes, refs, wts, aux, strength)


MESH = pl.DeviceIdType.MESH
CHUNKS = 4


def greet(devices):
    barrier = pltpu.get_barrier_semaphore()
    for device in devices:
        pl.semaphore_signal(barrier, inc=1, device_id=device, device_id_type=MESH)
    pl.semaphore_wait(barrier, len(devices))


def gather_kernel(peers, refs_ref, row_ref, all_refs, all_rows, local, send, recv):
    mine, core = lax.axis_index("particle"), lax.axis_index("classes")
    partner = {"classes": 1 - core}
    others = [{"particle": lax.rem(mine + d, peers)} for d in range(1, peers)]
    greet([partner] + others)
    copies = [
        pltpu.make_async_remote_copy(
            src_ref=refs_ref, dst_ref=all_refs.at[core], send_sem=send.at[0], recv_sem=recv.at[0],
            device_id=partner, device_id_type=MESH,
        ),
        pltpu.make_async_remote_copy(
            src_ref=row_ref, dst_ref=all_rows.at[peers], send_sem=send.at[1], recv_sem=recv.at[1],
            device_id=partner, device_id_type=MESH,
        ),
    ]
    for d, other in enumerate(others):
        copies.append(
            pltpu.make_async_remote_copy(
                src_ref=row_ref, dst_ref=all_rows.at[mine], send_sem=send.at[2 + d],
                recv_sem=recv.at[2 + d], device_id=other, device_id_type=MESH,
            )
        )
    for copy in copies:
        copy.start()
    own = [
        pltpu.make_async_copy(refs_ref, all_refs.at[core], local.at[0]),
        pltpu.make_async_copy(row_ref, all_rows.at[mine], local.at[1]),
    ]
    for copy in own:
        copy.start()
    for copy in own + copies:
        copy.wait()


def gathered(refs, row, peers):
    return pl.pallas_call(
        functools.partial(gather_kernel, peers),
        in_specs=[pl.BlockSpec(memory_space=pltpu.VMEM)] * 2,
        out_specs=[pl.BlockSpec(memory_space=pltpu.VMEM)] * 2,
        out_shape=[
            jax.ShapeDtypeStruct((2,) + refs.shape, refs.dtype),
            jax.ShapeDtypeStruct((peers + 1,) + row.shape, row.dtype),
        ],
        scratch_shapes=[
            pltpu.SemaphoreType.DMA((2,)),
            pltpu.SemaphoreType.DMA((peers + 1,)),
            pltpu.SemaphoreType.DMA((peers + 1,)),
        ],
        compiler_params=pltpu.CompilerParams(collective_id=0, has_side_effects=True),
    )(refs, row)


def scatter_kernel(depth, parts, out, pair_in, side_out, side_in, line_out, line_in,
                   pair_send, pair_recv, side_send, side_recv, line_send, line_recv):
    mine, core = lax.axis_index("particle"), lax.axis_index("classes")
    level, side = mine // 2, lax.rem(mine, 2)
    partner = {"classes": 1 - core}
    across = {"particle": level * 2 + 1 - side}
    levels = [lax.rem(level + d, depth) for d in range(1, depth)]
    line = [{"particle": other * 2 + side} for other in levels]
    greet([partner, across] + line)
    rows = out.shape[0] // CHUNKS
    pair, cross, lines = [], [], []
    for j in range(CHUNKS):
        copy = pltpu.make_async_remote_copy(
            src_ref=parts.at[:, :, 1 - core, j * rows : (j + 1) * rows], dst_ref=pair_in.at[j],
            send_sem=pair_send.at[j], recv_sem=pair_recv.at[j], device_id=partner,
            device_id_type=MESH,
        )
        copy.start()
        pair.append(copy)
    for j in range(CHUNKS):
        span = slice(j * rows, (j + 1) * rows)
        pair[j].wait_recv()
        side_out[j] = parts[:, 1 - side, core, span] + pair_in[j, :, 1 - side]
        copy = pltpu.make_async_remote_copy(
            src_ref=side_out.at[j], dst_ref=side_in.at[j], send_sem=side_send.at[j],
            recv_sem=side_recv.at[j], device_id=across, device_id_type=MESH,
        )
        copy.start()
        cross.append(copy)
        line_out[j] = parts[:, side, core, span] + pair_in[j, :, side]
    for j in range(CHUNKS):
        cross[j].wait_recv()
        line_out[j] = line_out[j] + side_in[j]
        for d in range(depth - 1):
            copy = pltpu.make_async_remote_copy(
                src_ref=line_out.at[j, levels[d]], dst_ref=line_in.at[j, d],
                send_sem=line_send.at[j, d], recv_sem=line_recv.at[j, d], device_id=line[d],
                device_id_type=MESH,
            )
            copy.start()
            lines.append(copy)
    for j in range(CHUNKS):
        total = line_out[j, level]
        for d in range(depth - 1):
            lines[j * (depth - 1) + d].wait_recv()
            total = total + line_in[j, d]
        out[j * rows : (j + 1) * rows] = total
    for copy in pair + cross + lines:
        copy.wait_send()


def scattered(parts):
    peers, _, classes, width = parts.shape
    depth = peers // 2
    rows = classes // CHUNKS
    sems = pltpu.SemaphoreType.DMA((CHUNKS,))
    line_sems = pltpu.SemaphoreType.DMA((CHUNKS, max(depth - 1, 1)))
    return pl.pallas_call(
        functools.partial(scatter_kernel, depth),
        in_specs=[pl.BlockSpec(memory_space=pltpu.VMEM)],
        out_specs=pl.BlockSpec(memory_space=pltpu.VMEM),
        out_shape=jax.ShapeDtypeStruct((classes, width), jnp.float32),
        scratch_shapes=[
            pltpu.VMEM((CHUNKS, depth, 2, rows, width), jnp.float32),
            pltpu.VMEM((CHUNKS, depth, rows, width), jnp.float32),
            pltpu.VMEM((CHUNKS, depth, rows, width), jnp.float32),
            pltpu.VMEM((CHUNKS, depth, rows, width), jnp.float32),
            pltpu.VMEM((CHUNKS, max(depth - 1, 1), rows, width), jnp.float32),
            sems, sems, sems, sems, line_sems, line_sems,
        ],
        compiler_params=pltpu.CompilerParams(
            collective_id=1, has_side_effects=True, vmem_limit_bytes=48 * 1024 * 1024
        ),
    )(parts.reshape(depth, 2, 2, classes, width))


def sums_kernel(peers, boxes, post, mass, refs, out, pair_out, pair_in, keep, side_out, side_in,
                line_in, mass_in, column, pair_send, pair_recv, side_send, side_recv, line_send,
                line_recv, mass_send, mass_recv):
    mine, core = lax.axis_index("particle"), lax.axis_index("classes")
    depth, width, classes = peers // 2, out.shape[1], out.shape[0]
    level, side = mine // 2, lax.rem(mine, 2)
    place = mine * 2 + core
    partner = {"classes": 1 - core}
    across = {"particle": level * 2 + 1 - side}
    everyone = []
    for e in range(1, 2 * peers):
        there = lax.rem(place + e, 2 * peers)
        everyone.append({"particle": there // 2, "classes": lax.rem(there, 2)})
    greet(everyone)
    started, masses = [], []

    def send(src, dst, sends, recvs, device):
        copy = pltpu.make_async_remote_copy(
            src_ref=src, dst_ref=dst, send_sem=sends, recv_sem=recvs, device_id=device,
            device_id_type=MESH,
        )
        copy.start()
        started.append(copy)
        return copy

    for e, device in enumerate(everyone):
        masses.append(
            send(mass, mass_in.at[e], mass_send.at[e], mass_recv.at[e], device)
        )
    turns = list(range(1, depth)) + [0]
    blocks = [(i, d, True) for i, d in enumerate(turns)] + [(i, d, False) for i, d in enumerate(turns)]
    pair, cross, lines = [], [], []

    def advance(n):
        i, d, away = blocks[n]
        pair[n].wait_recv()
        if away:
            side_out[i] = keep[n] + pair_in[n]
            cross.append(
                send(side_out.at[i], side_in.at[i], side_send.at[i], side_recv.at[i], across)
            )
            return
        cross[i].wait_recv()
        keep[n] = keep[n] + pair_in[n] + side_in[i]
        if d > 0:
            there = {"particle": lax.rem(level + d, depth) * 2 + side}
            lines.append(
                send(keep.at[n], line_in.at[i], line_send.at[i], line_recv.at[i], there)
            )

    for n, (i, d, away) in enumerate(blocks):
        shard = lax.rem(level + d, depth) * 2 + (1 - side if away else side)

        @pl.loop(0, width // STEP)
        def _(part):
            source = pl.multiple_of(shard * width + part * STEP, 128)
            target = pl.multiple_of(part * STEP, 128)
            turned = turned_sums(boxes[:, pl.ds(source, STEP)], post[...])
            low, high = turned[:classes], turned[classes : 2 * classes]
            keep[n, :, pl.ds(target, STEP)] = jnp.where(core == 0, low, high)
            pair_out[n, :, pl.ds(target, STEP)] = jnp.where(core == 0, high, low)

        pair.append(send(pair_out.at[n], pair_in.at[n], pair_send.at[n], pair_recv.at[n], partner))
        if n > 0:
            advance(n - 1)
    advance(len(blocks) - 1)
    weight = mass[...]
    for e, copy in enumerate(masses):
        copy.wait_recv()
        weight = weight + mass_in[e]
    column[...] = jnp.broadcast_to(weight, column.shape).T
    scale = column[pl.ds(pl.multiple_of(core * classes, 8), classes), :]
    total = keep[len(blocks) - 1]
    for i in range(depth - 1):
        lines[i].wait_recv()
        total = total + line_in[i]
    base = refs[:, pl.ds(pl.multiple_of(mine * width, 128), width)].astype(jnp.float32)
    out[...] = (total + base) / (scale[:, 0:1] + 1.0)
    for copy in started:
        copy.wait_send()


def fused_sums(boxes, post, mass, refs, peers):
    classes, width, depth = refs.shape[0], CYCLES // peers * ANGLES, peers // 2
    room = lambda count: pltpu.VMEM((count, classes, width), jnp.float32)
    sems = lambda count: pltpu.SemaphoreType.DMA((count,))
    others = 2 * peers - 1
    return pl.pallas_call(
        functools.partial(sums_kernel, peers),
        in_specs=[pl.BlockSpec(memory_space=pltpu.VMEM)] * 4,
        out_specs=pl.BlockSpec(memory_space=pltpu.VMEM),
        out_shape=jax.ShapeDtypeStruct((classes, width), jnp.float32),
        scratch_shapes=[
            room(peers), room(peers), room(peers), room(depth), room(depth), room(depth - 1),
            pltpu.VMEM((others,) + mass.shape, jnp.float32),
            pltpu.VMEM((mass.shape[1], mass.shape[1]), jnp.float32),
            sems(peers), sems(peers), sems(depth), sems(depth), sems(depth - 1), sems(depth - 1),
            sems(others), sems(others),
        ],
        compiler_params=pltpu.CompilerParams(
            collective_id=2, has_side_effects=True, vmem_limit_bytes=48 * 1024 * 1024
        ),
    )(boxes, post, mass, refs)


PARTS = 4
QUARTERS = 4
TILES = 6
GROUPS = ((0, 1, 2, 3), (4, 5))
APART = ANGLES // QUARTERS
SLOTS = 128
LEVELS = 32767.0


def turned(block, shift):
    shift = shift % ANGLES
    if shift == 0:
        return block
    return jnp.concatenate([block[ANGLES - shift :], block[: ANGLES - shift]], axis=0)


def flip(block):
    return pltpu.roll(block, 64, 1)


def low_lanes(rows, width=64, period=128):
    lane = lax.broadcasted_iota(jnp.int32, (rows, 128), 1)
    return lax.rem(lane, period) < width


def encode(block, codes, scales):
    largest = jnp.maximum(jnp.max(jnp.abs(block), axis=0, keepdims=True), 1e-30)
    codes[...] = jnp.round(block * (LEVELS / largest)).astype(jnp.int32).astype(jnp.int16)
    scales[0:1, :] = largest * (1.0 / LEVELS)


def refs_fan(refs, fans, energies, p):
    cols = slice(p * STEP, (p + 1) * STEP)
    rows = refs[:, cols].astype(jnp.float32)
    plain = jnp.concatenate([rows, rows], axis=0).T
    low = low_lanes(ANGLES)
    for c in range(PARTS):
        base = p * STEP + c * ANGLES
        piece = plain[c * ANGLES : (c + 1) * ANGLES]
        energies[p * PARTS + c : p * PARTS + c + 1, :] = jnp.sum(piece * piece, axis=0, keepdims=True)
        both = jnp.where(low, piece, turned(piece, APART))
        fans[0, base : base + ANGLES, :] = both.astype(jnp.bfloat16)
        fans[1, base : base + ANGLES, :] = turned(both, SHIFT).astype(jnp.bfloat16)


def boxes_fan(boxes, fans, p):
    cols = slice(p * STEP, (p + 1) * STEP)
    plain = boxes[:, cols].astype(jnp.float32).T
    fans[0, cols, :] = plain.astype(jnp.bfloat16)
    for c in range(PARTS):
        base = p * STEP + c * ANGLES
        piece = plain[c * ANGLES : (c + 1) * ANGLES]
        fans[1, base : base + ANGLES, :] = turned(piece, -SHIFT).astype(jnp.bfloat16)


def score_tiles(boxes, fans, wide, tiles, cycles):
    totals = [None] * len(tiles)
    blank = jnp.zeros((256 - ANGLES, 256), jnp.bfloat16)
    for c in range(cycles):
        base, window = c * ANGLES, c // 2 * 2 * ANGLES + c % 2 * 128
        factor = wide[c]
        factor = jnp.concatenate([factor, factor], axis=1)
        for n, f in enumerate(tiles):
            piece = fans[f % 2, base : base + ANGLES, :]
            shift = SHIFT * (f - f % 2)
            piece = jnp.concatenate(
                [turned(piece, shift), turned(piece, shift + 2 * APART)], axis=1
            )
            piece = jnp.concatenate([piece, blank] if c % 2 == 0 else [blank, piece], axis=0)
            part = factor * jnp.dot(
                boxes[:, window : window + 256], piece, preferred_element_type=jnp.float32
            )
            totals[n] = part if totals[n] is None else totals[n] + part
    return totals


def class_sums(fans, post, shard):
    rows = []
    for c in range(PARTS):
        base = pl.multiple_of(shard * STEP + c * ANGLES, 64)
        even = fans[0, pl.ds(base, ANGLES), :]
        odd = fans[1, pl.ds(base, ANGLES), :]
        rows.append(
            jnp.concatenate(
                [turned(x, -2 * SHIFT * s) for s in range(TILES // 2) for x in (even, odd)], axis=1
            )
        )
    sums = jnp.dot(jnp.concatenate(rows, axis=0), post[...], preferred_element_type=jnp.float32)
    low, first = low_lanes(ANGLES), low_lanes(ANGLES, 32, 64)
    both = []
    for c in range(PARTS):
        piece = sums[c * ANGLES : (c + 1) * ANGLES]
        b = piece[:, :128] + turned(piece[:, 128:], -2 * APART)
        both.append((b, turned(b, -APART)))

    def pair(i, j):
        return jnp.where(low, both[i][0], both[j][1]) + flip(jnp.where(low, both[j][0], both[i][1]))

    a, b = pair(0, 2), pair(1, 3)
    return jnp.where(first, a, pltpu.roll(b, 32, 1)), jnp.where(first, pltpu.roll(a, 96, 1), b)


def whole_kernel(
    peers, boxes, counts, places_in, turns_in, refs, weights_in, strength_in, out, evidence,
    places, turns, weights, strength, xs, rs, own, cards, duo, ref_fans, box_fans, energies, base_refs, wide, mine_s, theirs_s, terms,
    post, masses, y_out, y_out_s, y_in, y_in_s, keep, near_out, near_out_s, near_in, near_in_s, z_out, z_out_s, z_in, z_in_s, pair_out, pair_in, scale, totals,
    small_local, box_local, ref_local, own_local, box_send, box_recv, ref_send, ref_recv, card_send, card_recv,
    duo_send, duo_recv, score_send, score_recv, mass_send, mass_recv, y_send, y_recv, ys_send, ys_recv,
    near_send, near_recv, z_send, z_recv, zs_send, zs_recv, pair_send, pair_recv,
):
    mine, core = lax.axis_index("particle"), lax.axis_index("classes")
    depth, owned, classes = peers // 2, boxes.shape[0], refs.shape[0]
    level, side = mine // 2, lax.rem(mine, 2)
    partner = {"classes": 1 - core}
    across = {"particle": level * 2 + 1 - side}
    others = [{"particle": lax.rem(mine + d, peers)} for d in range(1, peers)]
    near, far = level + 1 - 2 * lax.rem(level, 2), lax.rem(level + 2, depth)
    levels = [lax.rem(near + 2, depth), far, near, level]
    diagonal = [{"particle": there * 2 + side, "classes": 1 - core} for there in (far, near)]
    straight = [{"particle": there * 2 + side} for there in (far, near)]
    barrier = pltpu.get_barrier_semaphore()
    friends = [partner] + others + diagonal
    for device in friends:
        pl.semaphore_signal(barrier, inc=1, device_id=device, device_id_type=MESH)
    box_rows = pl.ds(pl.multiple_of(core * owned, owned), owned)
    ref_rows = pl.ds(pl.multiple_of(core * classes, classes), classes)
    local = []
    for p in range(peers):
        source = pl.ds(pl.multiple_of((2 * p + core) * STEP, 128), STEP)
        target = pl.ds(p * STEP, STEP)
        local.append(
            pltpu.make_async_copy(refs.at[:, source], rs.at[ref_rows, target], ref_local.at[p])
        )
        local.append(
            pltpu.make_async_copy(boxes.at[:, source], xs.at[box_rows, target], box_local.at[p])
        )
    width = 2 * STEP
    own_copy = pltpu.make_async_copy(
        refs.at[:, pl.ds(pl.multiple_of(mine * width, 128), width)], own, own_local.at[0]
    )
    small = [
        pltpu.make_async_copy(source, target, small_local.at[n])
        for n, (source, target) in enumerate(
            [
                (places_in, places), (turns_in, turns), (weights_in, weights), (strength_in, strength),
            ]
        )
    ]
    for copy in small + local + [own_copy]:
        copy.start()
    for copy in small:
        copy.wait()
    card = jnp.zeros((8, 128), jnp.float32)
    cards[mine] = card
    slot = lax.broadcasted_iota(jnp.int32, (1, owned), 1)
    cards[mine, 0:1, :CYCLES] = weights[...]
    cards[mine, 1:2, :owned] = places[...].astype(jnp.float32)
    cards[mine, 2:3, :owned] = turns[...].astype(jnp.float32)
    cards[mine, 3:4, :owned] = jnp.where(slot < counts[0], 1.0, 0.0)
    cards[mine, 4:5, :classes] = strength[...]
    duo[core] = cards[mine]

    started = []

    def send(src, dst, sends, recvs, device):
        copy = pltpu.make_async_remote_copy(
            src_ref=src, dst_ref=dst, send_sem=sends, recv_sem=recvs, device_id=device,
            device_id_type=MESH,
        )
        copy.start()
        started.append(copy)
        return copy

    pl.semaphore_wait(barrier, len(friends))
    card_copies = [
        send(cards.at[mine, 0:1], cards.at[mine, 0:1], card_send.at[d], card_recv.at[d], device)
        for d, device in enumerate(others)
    ]
    duo_copy = send(duo.at[core], duo.at[core], duo_send.at[0], duo_recv.at[0], partner)
    ref_copies, box_copies = [], []
    for p in range(peers):
        source = pl.ds(pl.multiple_of((2 * p + 1 - core) * STEP, 128), STEP)
        target = pl.ds(p * STEP, STEP)
        ref_copies.append(
            send(refs.at[:, source], rs.at[ref_rows, target], ref_send.at[p], ref_recv.at[p], partner)
        )
    for p in range(peers):
        source = pl.ds(pl.multiple_of((2 * p + 1 - core) * STEP, 128), STEP)
        target = pl.ds(p * STEP, STEP)
        box_copies.append(
            send(boxes.at[:, source], xs.at[box_rows, target], box_send.at[p], box_recv.at[p], partner)
        )
    own_copy.wait()
    for h in range(2):
        for c in range(PARTS):
            base = (h * PARTS + c) * ANGLES
            base_refs[h, c * classes : (c + 1) * classes, :] = own[:, base : base + ANGLES].astype(
                jnp.float32
            )
    for copy in local:
        copy.wait()
    for p in range(peers):
        ref_copies[p].wait_recv()
        refs_fan(rs, ref_fans, energies, p)

    duo_copy.wait_recv()
    facts = duo[0] + flip(duo[1])
    facts = jnp.concatenate([facts] * (SLOTS // 8), axis=0).T
    place, turn, live = facts[:, 1:2], facts[:, 2:3], facts[:, 3:4]
    force = duo[0, 4:5, :] + pltpu.roll(duo[1, 4:5, :], classes, 1)
    force = force + flip(force)
    lane = lax.broadcasted_iota(jnp.int32, (SLOTS, 128), 1).astype(jnp.float32)
    swing = jnp.cos(TWO_PI * (lane - turn) / ROTATIONS)
    for copy in card_copies:
        copy.wait_recv()
    spread = jnp.zeros((SLOTS, 128), jnp.float32)
    for g in range(peers):
        spread = jnp.where(place == float(g), cards[g, 0:1, :], spread)
    wsum = jnp.sum(spread, axis=1, keepdims=True)
    spread = jnp.where(core == 0, spread, pltpu.roll(spread, 128 - PARTS, 1))
    base = jnp.zeros((SLOTS, 128), jnp.float32)
    for c in range(CYCLES // 2):
        place = c // PARTS * 2 * PARTS + c % PARTS
        factor = jnp.broadcast_to(spread[:, place : place + 1], (SLOTS, 128))
        wide[c] = factor
        base = base + factor * energies[c : c + 1, :]
    base = -0.5 * base
    for copy in box_copies:
        copy.wait_recv()

    low = low_lanes(SLOTS)
    score_copies, tops, norms = [], [], []

    def finish(f):
        score_copies[f].wait_recv()
        values = []
        for t in range(2):
            cols = slice(t * 128, (t + 1) * 128)
            r = f + 2 * t * TILES
            prior = jnp.where(low, swing[:, r : r + 1], swing[:, r + TILES : r + TILES + 1]) * force
            values.append(mine_s[f, :, cols] + theirs_s[f, :, cols] + prior)
        top = jnp.max(jnp.maximum(values[0], values[1]), axis=1, keepdims=True)
        values = [jnp.exp(v - top) for v in values]
        for t in range(2):
            terms[f, :, t * 128 : (t + 1) * 128] = values[t]
        tops.append(top)
        norms.append(jnp.sum(values[0] + values[1], axis=1, keepdims=True))

    for g, tiles in enumerate(GROUPS):
        for f, tile in zip(tiles, score_tiles(xs, ref_fans, wide, tiles, CYCLES // 2)):
            mine_s[f] = tile + jnp.concatenate([base, base], axis=1)
        for f in tiles:
            score_copies.append(
                send(mine_s.at[f], theirs_s.at[f], score_send.at[f], score_recv.at[f], partner)
            )
        if g > 0:
            for f in GROUPS[g - 1]:
                finish(f)
    for p in range(peers):
        boxes_fan(xs, box_fans, p)
    for f in GROUPS[-1]:
        finish(f)
    top = functools.reduce(jnp.maximum, tops)
    factors = [jnp.exp(t - top) for t in tops]
    norm = sum(n * s for n, s in zip(norms, factors))
    for f in range(TILES):
        factor = jnp.where(live > 0.0, factors[f] / norm, 0.0)
        post[f * SLOTS : (f + 1) * SLOTS, :] = (terms[f] * factor).astype(jnp.bfloat16)

    def mass_and_evidence():
        mass = jnp.zeros((8, 256), jnp.float32)
        for f in range(TILES):
            value = post[f * SLOTS : (f + 1) * SLOTS, :].astype(jnp.float32)
            for i in range(SLOTS // 8):
                mass = mass + value[i * 8 : (i + 1) * 8]
        mass = mass[:, :128] + mass[:, 128:]
        mass = mass + flip(mass)
        masses[mine] = jnp.broadcast_to(jnp.sum(mass, axis=0, keepdims=True), (8, 128))
        for d, device in enumerate(others):
            mass_copies.append(
                send(
                    masses.at[mine, 0:1], masses.at[mine, 0:1], mass_send.at[d], mass_recv.at[d],
                    device,
                )
            )
        proof = jnp.where(live > 0.0, (top + jnp.log(norm)) / (ANGLES * wsum), 0.0)
        proof = jnp.broadcast_to(proof, (SLOTS, 128)).T[0:1]
        evidence[...] = jnp.where(core == 0, proof, flip(proof))[:, :owned]

    mass_copies = []
    y_copies, z_copies, near_copies, waited = [], [[], []], [], set()

    def away(i, blocks):
        for h, value in enumerate(blocks):
            encode(value, y_out.at[i, h], y_out_s.at[i, h : h + 1])
        y_copies.append(
            [send(y_out_s.at[i, 0:2], y_in_s.at[i, 0:2], ys_send.at[i], ys_recv.at[i], across)]
            + (
                [send(y_out.at[i], y_in.at[i], y_send.at[i, 0], y_recv.at[i, 0], across)]
                if i == depth - 1
                else [
                    send(y_out.at[i, h], y_in.at[i, h], y_send.at[i, n], y_recv.at[i, n], across)
                    for n, h in enumerate([1 - core, core])
                ]
            )
        )

    def home(i, blocks):
        for h, value in enumerate(blocks):
            keep[i, h] = value

    halves = [1 - core, core]

    def arrived(copies):
        for copy in copies:
            if id(copy) not in waited:
                copy.wait_recv()
                waited.add(id(copy))

    def summed(i, n):
        half = halves[n]
        arrived(y_copies[i][: n + 2])
        row = jnp.where(half == 0, y_in_s[i, 0:1, :], y_in_s[i, 1:2, :])
        codes = y_in[i, half].astype(jnp.int32).astype(jnp.float32)
        return keep[i, half] + codes * row

    def to_near(n):
        half = halves[n]
        encode(summed(0, n), near_out.at[half], near_out_s.at[half])
        near_copies.append(
            [
                send(
                    near_out_s.at[half, 0:1], near_in_s.at[half, 0:1], near_send.at[n, 1],
                    near_recv.at[n, 1], straight[1],
                ),
                send(
                    near_out.at[half], near_in.at[half], near_send.at[n, 0], near_recv.at[n, 0],
                    straight[1],
                ),
            ]
        )

    def to_owner(j, n):
        half = halves[n]
        total = summed(j + 1, n)
        if j == 0:
            arrived(near_copies[n])
            codes = near_in[half].astype(jnp.int32).astype(jnp.float32)
            total = total + codes * near_in_s[half, 0:1, :]
        encode(total, z_out.at[j, half], z_out_s.at[j, half])
        device = diagonal[j] if n == 0 else straight[j]
        z_copies[j].append(
            send(
                z_out_s.at[j, half, 0:1], z_in_s.at[j, core, 0:1], zs_send.at[j, n],
                zs_recv.at[j, n], device,
            )
        )
        z_copies[j].append(
            send(z_out.at[j, half], z_in.at[j, core], z_send.at[j, n], z_recv.at[j, n], device)
        )

    shards = lambda i: (levels[i] * 2 + 1 - side, levels[i] * 2 + side)
    away(0, class_sums(box_fans, post, shards(0)[0]))
    for i in range(1, depth):
        held = class_sums(box_fans, post, shards(i - 1)[1])
        away(i, class_sums(box_fans, post, shards(i)[0]))
        home(i - 1, held)
        if i == 3:
            mass_and_evidence()
        if i < depth - 1:
            to_near(i - 1)
    home(depth - 1, class_sums(box_fans, post, shards(depth - 1)[1]))
    for j in range(2):
        for n in range(2):
            to_owner(j, n)

    for copy in mass_copies:
        copy.wait_recv()
    weight = masses[0, 0:1, :]
    for g in range(1, peers):
        weight = weight + masses[g, 0:1, :]
    weight = jnp.broadcast_to(weight, (8, 128))
    first = low_lanes(8, 32, 64)
    weight = jnp.where(
        core == 0,
        jnp.where(first, weight, pltpu.roll(weight, 32, 1)),
        jnp.where(first, pltpu.roll(weight, 96, 1), weight),
    )
    scale[...] = jnp.concatenate([weight] * 16, axis=0).T + 1.0

    def crossed(j, n):
        half = halves[n]
        arrived(z_copies[j][2 * n : 2 * n + 2])
        return z_in[j, half].astype(jnp.int32).astype(jnp.float32) * z_in_s[j, half, 0:1, :]

    def store(half, value):
        result = (value.T + base_refs[half]) / scale[:, 0:1]
        for c in range(PARTS):
            out[:, half * PARTS + c, :] = result[c * classes : (c + 1) * classes]

    pair_out[...] = summed(depth - 1, 0)
    pair_copy = send(pair_out, pair_in, pair_send.at[0], pair_recv.at[0], partner)
    held = summed(depth - 1, 1)
    for n in range(2):
        totals[n] = crossed(1, n)
    totals[1] = totals[1] + held
    pair_copy.wait_recv()
    totals[0] = totals[0] + pair_in[...]
    for n in range(2):
        store(halves[n], totals[n] + crossed(0, n))
    for copy in started:
        copy.wait_send()


def whole(boxes, counts, places, turns, refs, weights, strength, peers):
    given = (boxes, places, turns, refs, weights, strength)
    pinned = [pltpu.with_memory_space_constraint(x, pltpu.HBM) for x in given]
    classes, depth = refs.shape[0], peers // 2
    half = CYCLES * ANGLES // 2
    f32, bf16, i16 = jnp.float32, jnp.bfloat16, jnp.int16
    room = lambda dtype, *shape: pltpu.VMEM(shape, dtype)
    sems = lambda *shape: pltpu.SemaphoreType.DMA(shape)
    vmem = pl.BlockSpec(memory_space=pltpu.VMEM)
    hbm = pl.BlockSpec(memory_space=pltpu.HBM)
    return pl.pallas_call(
        functools.partial(whole_kernel, peers),
        in_specs=[hbm, pl.BlockSpec(memory_space=pltpu.SMEM)] + [hbm] * 5,
        out_specs=[vmem, vmem],
        out_shape=[
            jax.ShapeDtypeStruct((classes, CYCLES // peers, ANGLES), f32),
            jax.ShapeDtypeStruct((1, boxes.shape[0]), f32),
        ],
        scratch_shapes=[
            pltpu.VMEM(places.shape, places.dtype),
            pltpu.VMEM(turns.shape, turns.dtype), pltpu.VMEM(weights.shape, f32),
            pltpu.VMEM(strength.shape, f32), room(bf16, SLOTS, half), room(bf16, 2 * classes, half), room(bf16, classes, 2 * STEP),
            room(f32, peers, 8, 128), room(f32, 2, 8, 128),
            room(bf16, 2, half, 128), room(bf16, 2, half, 128), room(f32, CYCLES // 2, 128),
            room(f32, 2, 128, ANGLES), room(f32, CYCLES // 2, SLOTS, 128),
            room(f32, TILES, SLOTS, 256), room(f32, TILES, SLOTS, 256), room(f32, TILES, SLOTS, 256),
            room(bf16, TILES * SLOTS, 256), room(f32, peers, 8, 128),
            room(i16, depth, 2, ANGLES, 128), room(f32, depth, 8, 128),
            room(i16, depth, 2, ANGLES, 128), room(f32, depth, 8, 128),
            room(f32, depth, 2, ANGLES, 128),
            room(i16, 2, ANGLES, 128), room(f32, 2, 8, 128), room(i16, 2, ANGLES, 128), room(f32, 2, 8, 128),
            room(i16, 2, 2, ANGLES, 128), room(f32, 2, 2, 8, 128),
            room(i16, 2, 2, ANGLES, 128), room(f32, 2, 2, 8, 128),
            room(f32, ANGLES, 128), room(f32, ANGLES, 128), room(f32, 128, 128), room(f32, 2, ANGLES, 128),
            sems(4), sems(peers), sems(peers), sems(1), sems(peers), sems(peers), sems(peers), sems(peers),
            sems(peers - 1), sems(peers - 1), sems(1), sems(1), sems(TILES), sems(TILES),
            sems(peers - 1), sems(peers - 1), sems(depth, 2), sems(depth, 2), sems(depth), sems(depth),
            sems(2, 2), sems(2, 2), sems(2, 2), sems(2, 2), sems(2, 2), sems(2, 2),
            sems(1), sems(1),
        ],
        compiler_params=pltpu.CompilerParams(
            collective_id=3, has_side_effects=True, vmem_limit_bytes=48 * 1024 * 1024
        ),
    )(pinned[0], counts, *pinned[1:])


def on_device(boxes, counts, destinations, prior_rot, references, cycle_weights, prior_strength):
    peers = lax.axis_size("particle")
    cycle_index = lax.axis_index("particle")
    cycles_dev = CYCLES // peers
    width = cycles_dev * ANGLES
    if width == 2 * STEP:
        new_references, evidence = whole(
            boxes, counts, destinations[None, :], prior_rot[None, :], references,
            cycle_weights, prior_strength[None, :], peers,
        )
        return new_references, evidence[0]
    owned = boxes.shape[0]
    classes_dev = references.shape[0]
    lane_index = lax.axis_index("classes")
    row = jnp.concatenate([cycle_weights[0], prior_strength])
    row = jnp.pad(row, (0, 128 - row.shape[0]))[None, :]
    refs, rows = gathered(references, row, peers)
    refs = refs.reshape(2 * classes_dev, -1)
    group_wts = rows[:peers, 0, :CYCLES]
    other = rows[peers, 0, CYCLES : CYCLES + classes_dev]
    strength = jnp.where(
        lane_index == 0,
        jnp.concatenate([prior_strength, other]),
        jnp.concatenate([other, prior_strength]),
    ).reshape(1, -1)
    mine = destinations[:, None] == jnp.arange(peers, dtype=jnp.int32)[None, :]
    wts = jnp.sum(jnp.where(mine[:, :, None], group_wts[None], 0.0), axis=1)
    live = (jnp.arange(owned, dtype=jnp.int32) < counts[0]).astype(jnp.float32)
    turn_ids = jnp.arange(ROTATIONS, dtype=jnp.float32)
    gap = TWO_PI * (turn_ids[None, :] - prior_rot[:, None].astype(jnp.float32)) / ROTATIONS
    aux = jnp.concatenate([jnp.cos(gap), live[:, None], jnp.sum(wts, axis=1)[:, None]], axis=1)
    wts = jnp.transpose(wts.reshape(owned, STEPS, STEP_CYCLES), (1, 0, 2))
    post, mass, evidence = scores(
        boxes, refs, wts, aux, jnp.concatenate([strength, strength], axis=1)
    )
    if width % STEP == 0:
        new_references = fused_sums(boxes, post, mass, references, peers)
    else:
        sums = scattered(plain_sums(boxes, post, mass, classes_dev, peers))
        own_refs = lax.dynamic_slice_in_dim(references, cycle_index * width, width, 1)
        new_references = (sums[:, :width] + own_refs.astype(jnp.float32)) / (
            sums[:, width : width + 1] + 1.0
        )
    return new_references.reshape(classes_dev, cycles_dev, ANGLES), evidence[:, 0]


def solution(mesh):
    in_specs = (
        P(("groups", "particle", "classes"), None),
        P(("groups", "particle", "classes")),
        P(("groups", "particle", "classes")),
        P(("groups", "particle", "classes")),
        P(("groups", "classes"), None),
        P(("groups", "particle"), None),
        P(("groups", "classes")),
    )
    out_specs = (P(("groups", "classes"), "particle", None), P(("groups", "particle", "classes")))
    return jax.shard_map(
        on_device, mesh=mesh, in_specs=in_specs, out_specs=out_specs, check_vma=False
    )
```
